128 devices in a mesh: dev: 16 (over z_hi, y, core), ha: 8 (over z_lo, x).
Axes of the slice: x: 4, y: 4, z: 4 (z_hi: 2, z_lo: 2; z = z_hi * 2 + z_lo), core: 2. Of those that a mesh axis runs over, the one named last changes fastest.
Arguments:
- volume: bfloat16 [4, 128, 128, 512], P(None, 'dev', 'ha'), may hold values from -6 to 6
- w_first: bfloat16 [3, 3, 3, 4, 32], replicated, may hold values from -0.625 to 0.625
- w_second: bfloat16 [3, 3, 3, 32, 64], replicated, may hold values from -0.21875 to 0.21875
- w_third: bfloat16 [3, 3, 3, 64, 128], P(None, None, None, None, 'ha'), may hold values from -0.15625 to 0.15625
- cotangent: bfloat16 [128, 16, 16, 64], P('ha', 'dev'), may hold values from -6 to 6
Outputs:
- out_third: bfloat16 [128, 16, 16, 64], P('ha', 'dev')
- grad_first: float32 [3, 3, 3, 4, 32], replicated
- grad_second: float32 [3, 3, 3, 32, 64], replicated
- grad_third: float32 [3, 3, 3, 64, 128], P(None, None, None, None, 'ha')
The draws below stay inside these ranges and needn't reach their ends.
All inputs are finite; a program needn't handle non-finite values.
Results may differ from the reference program's by a relative error of at most 0.0063.
Values may be sent and summed in bfloat16 or wider, within the bound.
A program may use at most 192 MiB of HBM per device.

```python
import jax
import jax.numpy as jnp
from jax import lax

CIN = 4
C1 = 32
C2 = 64
C3 = 128
W = 512
DEPTH = 128
HEIGHT = 128


def block_scale(stream_key, shape, pieces, least, high):
    def one(dim, blocks):
        steps = jax.random.uniform(jax.random.fold_in(jax.random.fold_in(stream_key, 6), dim), (blocks,), jnp.float32, least / len(pieces), high / len(pieces))
        return jnp.repeat(jnp.exp(steps), shape[dim] // blocks).reshape((-1,) + (1,) * (len(shape) - dim - 1))

    level = one(*pieces[0])
    for cut in pieces[1:]:
        level = level * one(*cut)
    return level


def noise(own_key, shape, deviation, bound, pieces=(), held_as=jnp.bfloat16):
    result = jax.random.normal(own_key, shape, jnp.float32) * deviation
    if len(pieces) > 0:
        result = block_scale(own_key, shape, pieces, -0.22, 0.18) * result
    return jnp.clip(result, min=-bound, max=bound).astype(held_as)


def setup_inputs(seed: int = 0) -> dict:
    key_of = jax.random.split(jax.random.key(seed), 6)
    volume = noise(key_of[0], (CIN, DEPTH, HEIGHT, W), 1.0, 6.0, ((1, 16), (2, 8)))
    w_first = noise(key_of[1], (3, 3, 3, CIN, C1), (27 * CIN) ** -0.5, 0.625)
    w_second = noise(key_of[2], (3, 3, 3, C1, C2), (27 * C1) ** -0.5, 0.21875)
    w_third = noise(key_of[3], (3, 3, 3, C2, C3), (27 * C2) ** -0.5, 0.15625, ((4, 8),))
    cotangent = noise(key_of[4], (C3, DEPTH // 8, HEIGHT // 8, W // 8), 1.0, 6.0, ((0, 8), (1, 16)))
    return {"volume": volume, "w_first": w_first, "w_second": w_second, "w_third": w_third, "cotangent": cotangent}


def convolve(inputs, kernel):
    return lax.conv_general_dilated(inputs[None], kernel, (2, 2, 2), [(1, 0)] * 3, dimension_numbers=('NCDHW', 'DHWIO', 'NCDHW'), preferred_element_type=jnp.float32)[0]

def exact_conv(inputs, kernel):
    return lax.conv_general_dilated(inputs[None], kernel, (2, 2, 2), [(1, 0)] * 3, dimension_numbers=('NCDHW', 'DHWIO', 'NCDHW'), precision=lax.Precision.HIGHEST)[0]

def leaky_relu(values):
    return 0.3 * values + 0.175 * jax.nn.softplus(4.0 * values)

def leaky_slope(values):
    return 0.3 + 0.7 * jax.nn.sigmoid(4.0 * values)

def kernel_grad(inputs, kernel, delta):
    inputs_full = inputs.astype(jnp.float32)

    def apply_kernel(weights):
        return exact_conv(inputs_full, weights)
    unused, pull = jax.vjp(apply_kernel, kernel.astype(jnp.float32))
    return pull(delta.astype(jnp.float32))[0]

def data_grad(inputs, kernel, delta):
    kernel_full = kernel.astype(jnp.float32)

    def apply_data(values):
        return exact_conv(values, kernel_full)
    unused, pull = jax.vjp(apply_data, inputs.astype(jnp.float32))
    return pull(delta.astype(jnp.float32))[0]

def cell_scale(array):
    return 1.0 / jnp.sqrt(jnp.float32(array.shape[1] * array.shape[2] * array.shape[3]))

def reference(volume, w_first, w_second, w_third, cotangent):
    pre_first = convolve(volume, w_first)
    act_first = leaky_relu(pre_first).astype(jnp.bfloat16)
    pre_second = convolve(act_first, w_second)
    act_second = leaky_relu(pre_second).astype(jnp.bfloat16)
    pre_third = convolve(act_second, w_third)
    out_third = leaky_relu(pre_third).astype(jnp.bfloat16)
    delta_third = (cotangent.astype(jnp.float32) * leaky_slope(pre_third)).astype(jnp.bfloat16)
    grad_third = kernel_grad(act_second, w_third, delta_third) * cell_scale(pre_third)
    back_second = data_grad(act_second, w_third, delta_third)
    delta_second = (back_second * leaky_slope(pre_second)).astype(jnp.bfloat16)
    grad_second = kernel_grad(act_first, w_second, delta_second) * cell_scale(pre_second)
    back_first = data_grad(act_first, w_second, delta_second)
    delta_first = (back_first * leaky_slope(pre_first)).astype(jnp.bfloat16)
    grad_first = kernel_grad(volume, w_first, delta_first) * cell_scale(pre_first)
    return (out_third, grad_first, grad_second, grad_third)
```

```python
import functools
import math

import jax
import jax.numpy as jnp
import numpy as np
from jax import lax
from jax.experimental import pallas as pl
from jax.experimental.pallas import tpu as pltpu
from jax.sharding import PartitionSpec as P

MESH = pl.DeviceIdType.MESH
BF = jnp.bfloat16
F32 = jnp.float32


def dot(a, b):
    return lax.dot_general(a, b, (((1,), (0,)), ((), ())), preferred_element_type=F32)


def dot_nt(a, b):
    return lax.dot_general(a, b, (((1,), (1,)), ((), ())), preferred_element_type=F32)


def dot_tn(a, b):
    return lax.dot_general(a, b, (((0,), (0,)), ((), ())), preferred_element_type=F32)


def split_rows(x):
    high = x.astype(BF)
    low = (x - high.astype(F32)).astype(BF)
    return jnp.concatenate([high, low], 0)


def leaky_and_slope(z):
    u = 4.0 * z
    t = jnp.exp(-jnp.abs(u))
    one = 1.0 + t
    soft = jnp.maximum(u, 0.0) + jnp.log(one)
    r = 1.0 / one
    sig = jnp.where(u >= 0.0, r, t * r)
    return 0.3 * z + 0.175 * soft, 0.3 + 0.7 * sig


ORDER2 = np.concatenate([np.arange(0, 128, 2), np.arange(1, 128, 2)])
ORDER1 = np.concatenate([2 * ORDER2, 2 * ORDER2 + 1])


def constants():
    expand = np.zeros((128, 1152), np.float32)
    for a in range(3):
        for e in range(3):
            for c in range(4):
                for h in range(16):
                    col = a * 192 + e * 64 + c * 16 + h
                    row = lambda b: ((a * 3 + b) * 3 + e) * 4 + c
                    expand[row(1 + h % 2), col] = 1
                    if h % 2:
                        expand[row(0), 576 + col] = 1
    halo = np.zeros((128, 1024), np.float32)
    for i in range(4):
        for a in range(3):
            d = 2 * i - 1 + a
            s, plane = (0, d) if d >= 0 else (1, 7)
            for e in range(3):
                for c in range(4):
                    row = (a * 9 + e) * 4 + c
                    halo[row, i * 256 + e * 64 + s * 32 + plane * 4 + c] = 1
    columns = np.zeros((512, 768), np.float32)
    for e in range(3):
        for p in range(256):
            w = 2 * ORDER1[p] - 1 + e
            if w >= 0:
                columns[w, e * 256 + p] = 1
    where2 = {int(l): q for q, l in enumerate(ORDER2)}
    shift2 = np.zeros((128, 128), np.float32)
    for p in range(128):
        if ORDER2[p] >= 1:
            shift2[where2[int(ORDER2[p]) - 1], p] = 1
    taps3 = np.zeros((256, 384), np.float32)
    for jj in range(2):
        for e in range(3):
            for l in range(64):
                w = 2 * l - 1 + e
                if w >= 0:
                    taps3[jj * 128 + where2[w], e * 128 + jj * 64 + l] = 1
    last = np.zeros((32, 512), np.float32)
    for d in range(8):
        for c in range(4):
            last[d * 4 + c, c * 128 + d * 16 + 15] = 1
    return [jnp.asarray(x, BF) for x in (expand, halo, columns, shift2, taps3, last, np.eye(64))]


class Plan:
    def __init__(self, nd, nh):
        self.nd, self.nh = nd, nh
        self.pb = 128 // nh
        self.mb = 64 // nh
        self.w3 = max(128, 2048 // nd)
        self.w2 = max(128, 1024 // nd)
        self.nv3 = -(-1728 // self.w3)
        self.nv2 = -(-864 // self.w2)
        names = ["vd", "vh", "vc", "ad", "ah", "ac", "bd", "bh", "bc", "2d", "2h", "2c", "1d", "1h", "1c"]
        self.sem = {}
        count = 0
        for name in names:
            self.sem[name] = count
            count += 1
        for name in ["w3", "cot", "out", "g3h", "g2h", "g2z", "g1h"]:
            self.sem[name] = count
            count += nh - 1
        for name in ["g3d", "g3a", "g2d", "g2a", "g1d"]:
            self.sem[name] = count
            count += nd - 1
        self.count = count

    def scratch(self):
        nd, nh, pb, mb = self.nd, self.nh, self.pb, self.mb
        v = pltpu.VMEM
        return dict(
            V0=v((4, 16, 512), BF),
            HS=v((32, 512), BF),
            HR=v((2, 32, 512), BF),
            T1=v((9, 192, 256), BF),
            TH=v((192, 256), BF),
            WT=v((256, 576), BF),
            WH=v((4, 32, 192), BF),
            PH=v((4, 32, 256), F32),
            A1=v((5, 288, 256), BF),
            S1=v((4, 256, 256), F32),
            T2=v((5, 864, 128), BF),
            W2T=v((3, 64, 288), BF),
            A2=v((3, 320, 128), BF),
            S2=v((2, 256, 128), F32),
            T3=v((3, 576, 128), BF),
            W3=v((nh, pb, 1728), BF),
            COT=v((nh, pb, 128), BF),
            OS=v((nh, pb, 128), BF),
            OR=v((nh, pb, 128), BF),
            D3=v((1728, 128), F32),
            SD2=v((256, 128), BF),
            SH2=v((2, 64, 128), BF),
            SC2=v((64, 128), BF),
            RD2=v((256, 128), BF),
            RH2=v((2, 64, 128), BF),
            RC2=v((64, 128), BF),
            B2=v((2, 256, 128), F32),
            DL2=v((2, 256, 128), BF),
            SD1=v((256, 256), BF),
            SH1=v((4, 32, 256), BF),
            SC1=v((32, 256), BF),
            RD1=v((256, 256), BF),
            RH1=v((4, 32, 256), BF),
            RC1=v((32, 256), BF),
            Y=v((4, 288, 128), F32),
            B1=v((4, 256, 256), F32),
            DL1=v((4, 256, 256), BF),
            G3F=v((nh, pb, 1728), F32),
            G3S=v((nh, pb, 1728), BF),
            R3H=v((nh, pb, 1728), BF),
            P3S=v((nd, pb, self.w3), F32),
            R3D=v((nd, pb, self.w3), F32),
            F3=v((nd, pb, self.w3), F32),
            Q3=v((pb, self.w3), F32),
            G2S=v((nh, mb, 864), F32),
            R2H=v((nh, mb, 864), F32),
            P2S=v((nd, mb, self.w2), F32),
            R2D=v((nd, mb, self.w2), F32),
            F2=v((nd, mb, self.w2), F32),
            Q2=v((mb, self.w2), F32),
            F2H=v((nh, nd, mb, self.w2), F32),
            G1A=v((256, 576), F32),
            G1S=v((32, 128), F32),
            R1H=v((nh, 32, 128), F32),
            G1D=v((32, 128), F32),
            R1D=v((nd, 32, 128), F32),
            ss=pltpu.SemaphoreType.DMA((self.count,)),
            rs=pltpu.SemaphoreType.DMA((self.count,)),
        )


def kernel(plan, names, scales, *refs):
    nd, nh, pb, mb = plan.nd, plan.nh, plan.pb, plan.mb
    vol, w1n, w2, w3t, cot, expand, halo, columns, shift2, taps3, last, eye = refs[:12]
    o3, g1o, g2o, g3o = refs[12:16]
    s = dict(zip(names, refs[16:]))
    ss, rs = s["ss"], s["rs"]
    dev, ha = lax.axis_index("dev"), lax.axis_index("ha")
    up_d, up_h = dev < nd - 1, ha < nh - 1
    lo_d, lo_h = dev > 0, ha > 0
    up_c, lo_c = up_d & up_h, lo_d & lo_h

    def dev_peer(k):
        return lax.rem(dev + k, nd)

    def ha_peer(k):
        return lax.rem(ha + k, nh)

    if nd * nh > 1:
        barrier = pltpu.get_barrier_semaphore()
        for k in range(1, nh):
            pl.semaphore_signal(barrier, inc=1, device_id=(dev, ha_peer(k)), device_id_type=MESH)
        for k in range(1, nd):
            pl.semaphore_signal(barrier, inc=1, device_id=(dev_peer(k), ha), device_id_type=MESH)

        @pl.when(up_c)
        def _():
            pl.semaphore_signal(barrier, inc=1, device_id=(dev + 1, ha + 1), device_id_type=MESH)

        @pl.when(lo_c)
        def _():
            pl.semaphore_signal(barrier, inc=1, device_id=(dev - 1, ha - 1), device_id_type=MESH)

    def copy(src, dst, k, target):
        return pltpu.make_async_remote_copy(
            src_ref=src, dst_ref=dst, send_sem=ss.at[k], recv_sem=rs.at[k], device_id=target, device_id_type=MESH
        )

    routes = {
        "d": (up_d, lo_d, nd > 1, (jnp.minimum(dev + 1, nd - 1), ha)),
        "h": (up_h, lo_h, nh > 1, (dev, jnp.minimum(ha + 1, nh - 1))),
        "c": (up_c, lo_c, nd > 1 and nh > 1, (jnp.minimum(dev + 1, nd - 1), jnp.minimum(ha + 1, nh - 1))),
    }
    back = {
        "d": (lo_d, up_d, nd > 1, (jnp.maximum(dev - 1, 0), ha)),
        "h": (lo_h, up_h, nh > 1, (dev, jnp.maximum(ha - 1, 0))),
        "c": (lo_c, up_c, nd > 1 and nh > 1, (jnp.maximum(dev - 1, 0), jnp.maximum(ha - 1, 0))),
    }
    pending = []

    def send(group, kind, src, dst, table=routes):
        can_send, can_receive, exists, target = table[kind]
        if not exists:
            return
        c = copy(src, dst, plan.sem[group + kind], target)
        pl.when(can_send)(c.start)
        pending.append((can_send, c))

    def receive(group, kind, src, dst, table=routes):
        can_send, can_receive, exists, target = table[kind]
        if not exists:
            return
        c = copy(src, dst, plan.sem[group + kind], target)
        pl.when(can_receive)(c.wait_recv)

    def blank(kind, ref, table=routes):
        can_send, can_receive, exists, target = table[kind]

        @pl.when(jnp.logical_not(can_receive))
        def _():
            ref[...] = jnp.zeros(ref.shape, ref.dtype)

    v2 = vol[...].reshape(512, 512)
    s["HS"][...] = dot(last[...], v2).astype(BF)

    blank("d", s["V0"])
    blank("h", s["HR"].at[0])
    blank("c", s["HR"].at[1])
    blank("h", s["A1"].at[1:5, 0:32])
    blank("d", s["A1"].at[0, 32:288])
    blank("c", s["A1"].at[0, 0:32])
    blank("h", s["A2"].at[1:3, 0:64])
    blank("d", s["A2"].at[0, 64:320])
    blank("c", s["A2"].at[0, 0:64])
    for n in ("1", "2"):
        blank("d", s["RD" + n], back)
        blank("h", s["RH" + n], back)
        blank("c", s["RC" + n], back)

    if nd * nh > 1:
        count = nh - 1 + nd - 1 + up_c.astype(jnp.int32) + lo_c.astype(jnp.int32)
        pl.semaphore_wait(barrier, count)

    halos_v = [
        ("d", vol.at[:, 7], s["V0"]),
        ("h", s["HS"], s["HR"].at[0]),
        ("c", s["HS"], s["HR"].at[1]),
    ]
    for kind, src, dst in halos_v:
        send("v", kind, src, dst)

    def spread(group, src_of, dst, size, peer_of, valid_send=None, valid_receive=None):
        made = []
        for k in range(1, size):
            peer = peer_of(k)
            target = (dev, peer) if peer_of is ha_peer else (peer, ha)
            c = copy(src_of(peer), dst(k), plan.sem[group] + k - 1, target)
            if valid_send is None:
                c.start()
                pending.append((None, c))
            else:
                ok = valid_send(peer)
                pl.when(ok)(c.start)
                pending.append((ok, c))
            made.append((k, c))
        return made

    def gather(made, valid_receive=None, size=None, me=None):
        for k, c in made:
            if valid_receive is None:
                c.wait_recv()
            else:
                pl.when(valid_receive(lax.rem(me + size - k, size)))(c.wait_recv)

    made_w3 = spread("w3", lambda p: w3t, lambda k: s["W3"].at[ha], nh, ha_peer)
    made_cot = spread("cot", lambda p: cot.at[p], lambda k: s["COT"].at[ha], nh, ha_peer)
    s["W3"][ha] = w3t[...]
    s["COT"][ha] = cot[ha]

    def store_taps(block, plane, channel):
        taps = dot(block, columns[...]).astype(BF)
        for d in range(block.shape[0] // 16):
            for e in range(3):
                s["T1"][plane + d, pl.ds(e * 64 + channel * 16, 16), :] = taps[d * 16 : d * 16 + 16, e * 256 : e * 256 + 256]

    for c in range(4):
        store_taps(vol[c].reshape(128, 512), 1, c)

    base = dot(w1n[...], expand[...])
    base_a, base_b = base[:, 0:576], base[:, 576:1152]
    row_h = lax.broadcasted_iota(jnp.int32, (32, 576), 1) & 15

    def tap_masks(j):
        return (row_h >> 1) == j, ((row_h & 1) == 1) & (((row_h + 1) >> 1) == j)

    for j in range(8):
        mask_a, mask_b = tap_masks(j)
        s["WT"][pl.ds(j * 32, 32), :] = (jnp.where(mask_a, base_a, 0.0) + jnp.where(mask_b, base_b, 0.0)).astype(BF)
    edge = dot(w1n[...], halo[...]).astype(BF)
    for i in range(4):
        s["WH"][i] = edge[:, i * 256 : i * 256 + 192]
    for a in range(3):
        s["W2T"][a] = dot_nt(eye[...], w2[a * 288 : a * 288 + 288, :]).astype(BF)

    for kind, src, dst in halos_v:
        receive("v", kind, src, dst)
    for c in range(4):
        store_taps(s["V0"][c], 0, c)
    rows = dot(s["HR"][...].reshape(64, 512), columns[...]).astype(BF)
    for e in range(3):
        s["TH"][pl.ds(e * 64, 64), :] = rows[:, e * 256 : e * 256 + 256]
    s["PH"][...] = dot(s["WH"][...].reshape(128, 192), s["TH"][...]).reshape(4, 32, 256)

    def first(i):
        z = dot(s["WT"][...], s["T1"][pl.ds(2 * i, 3)].reshape(576, 256))
        z = jnp.concatenate([z[0:32] + s["PH"][i], z[32:256]], 0)
        act, slope = leaky_and_slope(z)
        s["A1"][i + 1, 32:288, :] = act.astype(BF)
        s["S1"][i] = slope

    def second_taps(plane, lo, hi):
        x = s["A1"][plane, lo * 32 : hi * 32, :]
        moved = dot(x[:, 128:256], shift2[...]).astype(BF)
        for j in range(lo, hi):
            r = (j - lo) * 32
            s["T2"][plane, pl.ds(j * 96, 32), :] = moved[r : r + 32]
            s["T2"][plane, pl.ds(j * 96 + 32, 32), :] = x[r : r + 32, 0:128]
            s["T2"][plane, pl.ds(j * 96 + 64, 32), :] = x[r : r + 32, 128:256]

    first(3)
    halos_a = [
        ("d", s["A1"].at[4, 32:288], s["A1"].at[0, 32:288]),
        ("c", s["A1"].at[4, 256:288], s["A1"].at[0, 0:32]),
        ("h", s["A1"].at[1:5, 256:288], s["A1"].at[1:5, 0:32]),
    ]
    send("a", *halos_a[0])
    send("a", *halos_a[1])

    def loop_first(i, carry):
        first(i)
        return carry

    lax.fori_loop(0, 3, loop_first, 0)
    send("a", *halos_a[2])

    def loop_taps(i, carry):
        second_taps(i, 1, 9)
        return carry

    lax.fori_loop(1, 5, loop_taps, 0)
    for halo_a in halos_a:
        receive("a", *halo_a)
    second_taps(0, 0, 9)
    for plane in range(1, 5):
        second_taps(plane, 0, 1)

    for i in (1, 0):
        for j in range(4):
            z = None
            for a in range(3):
                term = dot(s["W2T"][a], s["T2"][2 * i + a, j * 192 : j * 192 + 288, :])
                z = term if z is None else z + term
            act, slope = leaky_and_slope(z)
            s["A2"][i + 1, 64 + 64 * j : 128 + 64 * j, :] = act.astype(BF)
            s["S2"][i, 64 * j : 64 * j + 64, :] = slope
    halos_b = [
        ("d", s["A2"].at[2, 64:320], s["A2"].at[0, 64:320]),
        ("c", s["A2"].at[2, 256:320], s["A2"].at[0, 0:64]),
        ("h", s["A2"].at[1:3, 256:320], s["A2"].at[1:3, 0:64]),
    ]
    for halo_b in halos_b:
        send("b", *halo_b)

    def third_taps(plane, b):
        x = jnp.concatenate(
            [s["A2"][plane, b * 64 : b * 64 + 64, :], s["A2"][plane, b * 64 + 128 : b * 64 + 192, :]], 1
        )
        y = dot(x, taps3[...]).astype(BF)
        for e in range(3):
            s["T3"][plane, b * 192 + e * 64 : b * 192 + e * 64 + 64, :] = y[:, e * 128 : e * 128 + 128]

    for plane in (1, 2):
        for b in (1, 2):
            third_taps(plane, b)
    for halo_b in halos_b:
        receive("b", *halo_b)
    for plane, b in ((0, 0), (0, 1), (0, 2), (1, 0), (2, 0)):
        third_taps(plane, b)
    gather(made_w3)
    gather(made_cot)
    w3 = s["W3"][...].reshape(128, 1728)
    t3 = s["T3"][...].reshape(1728, 128)
    act, slope = leaky_and_slope(dot(w3, t3))
    s["OS"][...] = act.astype(BF).reshape(nh, pb, 128)
    delta3 = (s["COT"][...].reshape(128, 128).astype(F32) * slope).astype(BF)

    s["D3"][...] = dot_tn(w3, delta3)

    def third_back(a):
        parts = []
        for b in range(3):
            r = a * 576 + b * 192
            x = jnp.concatenate([s["D3"][r + 64 * e : r + 64 * e + 64, :] for e in range(3)], 1)
            y = dot_nt(split_rows(x), taps3[...])
            parts.append(y[0:64] + y[64:128])
        left = [y[:, 0:128] for y in parts]
        right = [y[:, 128:256] for y in parts]
        return [left[0], left[1], left[2] + right[0], right[1], right[2]]

    k = third_back(0)
    s["SC2"][...] = k[0].astype(BF)
    for j in range(4):
        s["SD2"][64 * j : 64 * j + 64, :] = k[j + 1].astype(BF)
    for i in range(2):
        k = third_back(i + 1)
        s["SH2"][i] = k[0].astype(BF)
        for j in range(4):
            s["B2"][i, 64 * j : 64 * j + 64, :] = k[j + 1]
    halos_2 = [("d", s["SD2"], s["RD2"]), ("c", s["SC2"], s["RC2"]), ("h", s["SH2"], s["RH2"])]
    for kind, src, dst in halos_2:
        send("2", kind, src, dst, back)
    made_out = spread("out", lambda p: s["OS"].at[p], lambda k: s["OR"].at[ha], nh, ha_peer)
    s["OR"][ha] = s["OS"][ha]
    g3 = dot_nt(delta3, t3)
    s["G3F"][...] = g3.reshape(nh, pb, 1728)
    s["G3S"][...] = g3.astype(BF).reshape(nh, pb, 1728)
    made_g3h = spread("g3h", lambda p: s["G3S"].at[p], lambda k: s["R3H"].at[k], nh, ha_peer)

    for kind, src, dst in halos_2:
        receive("2", kind, src, dst, back)
    s["B2"][1] += s["RD2"][...].astype(F32)
    s["B2"][1, 192:256, :] += s["RC2"][...].astype(F32)
    for i in range(2):
        s["B2"][i, 192:256, :] += s["RH2"][i].astype(F32)
    s["DL2"][...] = (s["B2"][...] * s["S2"][...]).astype(BF)

    lane = lax.broadcasted_iota(jnp.int32, (32, 128), 1)

    def second_back(pairs, store):
        for j in range(4):
            y = None
            for a, i in pairs:
                term = dot(w2[a * 288 : a * 288 + 288, :], s["DL2"][i, j * 64 : j * 64 + 64, :])
                y = term if y is None else y + term
            s["Y"][j] = y
        for k in range(9):
            if k % 2:
                d = s["Y"][k // 2, 96:192, :]
            else:
                d = None
                if k < 8:
                    d = s["Y"][k // 2, 0:96, :]
                if k > 0:
                    more = s["Y"][k // 2 - 1, 192:288, :]
                    d = more if d is None else d + more
            moved = jnp.where(lane < 64, pltpu.roll(d[0:32], 64, 1), pltpu.roll(d[0:32], 63, 1))
            moved = jnp.where(lane == 127, 0.0, moved)
            store(k, d[32:64], d[64:96] + moved)

    def store_plane0(k, even, odd):
        ref = s["SC1"] if k == 0 else s["SD1"].at[32 * k - 32 : 32 * k]
        ref[:, 0:128] = even.astype(BF)
        ref[:, 128:256] = odd.astype(BF)

    def store_plane(plane):
        def store(k, even, odd):
            if k == 0:
                s["SH1"][plane - 1, :, 0:128] = even.astype(BF)
                s["SH1"][plane - 1, :, 128:256] = odd.astype(BF)
            else:
                s["B1"][plane - 1, 32 * k - 32 : 32 * k, 0:128] = even
                s["B1"][plane - 1, 32 * k - 32 : 32 * k, 128:256] = odd

        return store

    halos_1 = [("d", s["SD1"], s["RD1"]), ("c", s["SC1"], s["RC1"]), ("h", s["SH1"], s["RH1"])]
    second_back([(0, 0)], store_plane0)
    send("1", *halos_1[0], back)
    send("1", *halos_1[1], back)
    second_back([(1, 0)], store_plane(1))
    second_back([(2, 0), (0, 1)], store_plane(2))
    second_back([(1, 1)], store_plane(3))
    second_back([(2, 1)], store_plane(4))
    send("1", *halos_1[2], back)

    g2 = None
    for i in range(2):
        for j in (0, 2):
            x = jnp.concatenate([s["DL2"][i, 64 * (j + t) : 64 * (j + t) + 64, :] for t in (0, 1)], 1)
            t2 = jnp.concatenate(
                [s["T2"][2 * i : 2 * i + 3, 192 * (j + t) : 192 * (j + t) + 288, :].reshape(864, 128) for t in (0, 1)], 1
            )
            term = dot_nt(x, t2)
            g2 = term if g2 is None else g2 + term
    s["G2S"][...] = g2.reshape(nh, mb, 864)
    made_g2h = spread("g2h", lambda p: s["G2S"].at[p], lambda k: s["R2H"].at[k], nh, ha_peer)

    def pieces(total, dst, width, size, valid):
        for r in range(valid):
            end = min(size, (r + 1) * width)
            if end < (r + 1) * width:
                dst[r] = jnp.zeros(dst.shape[1:], F32)
            dst[r, :, 0 : end - r * width] = total[:, r * width : end]

    gather(made_g3h)
    total = s["G3F"][ha]
    for k in range(1, nh):
        total = total + s["R3H"][k].astype(F32)
    pieces(total, s["P3S"], plan.w3, 1728, plan.nv3)
    made_g3d = spread(
        "g3d", lambda p: s["P3S"].at[p], lambda k: s["R3D"].at[k], nd, dev_peer, lambda p: p < plan.nv3
    )

    for kind, src, dst in halos_1:
        receive("1", kind, src, dst, back)
    s["B1"][3] += s["RD1"][...].astype(F32)
    s["B1"][3, 224:256, :] += s["RC1"][...].astype(F32)
    for i in range(4):
        s["B1"][i, 224:256, :] += s["RH1"][i].astype(F32)
    s["G1A"][...] = jnp.zeros((256, 576), F32)

    def loop_back(i, carry):
        d = (s["B1"][i] * s["S1"][i]).astype(BF)
        s["DL1"][i] = d
        s["G1A"][...] += dot_nt(d, s["T1"][pl.ds(2 * i, 3)].reshape(576, 256))
        return carry

    lax.fori_loop(0, 4, loop_back, 0)
    gh = dot_nt(s["DL1"][:, 0:32, :].reshape(128, 256), s["TH"][...])
    sum_a = jnp.zeros((32, 576), F32)
    sum_b = jnp.zeros((32, 576), F32)
    for j in range(8):
        mask_a, mask_b = tap_masks(j)
        g = s["G1A"][32 * j : 32 * j + 32, :]
        sum_a = sum_a + jnp.where(mask_a, g, 0.0)
        sum_b = sum_b + jnp.where(mask_b, g, 0.0)
    g1 = dot_nt(split_rows(sum_a), expand[:, 0:576])
    g1 = g1 + dot_nt(split_rows(sum_b), expand[:, 576:1152])
    for i in range(4):
        g1 = g1 + dot_nt(split_rows(gh[32 * i : 32 * i + 32]), halo[:, i * 256 : i * 256 + 192])
    s["G1S"][...] = g1[0:32] + g1[32:64]
    made_g1h = spread("g1h", lambda p: s["G1S"], lambda k: s["R1H"].at[k], nh, ha_peer)

    gather(made_g2h)
    total = s["G2S"][ha]
    for k in range(1, nh):
        total = total + s["R2H"][k]
    pieces(total, s["P2S"], plan.w2, 864, plan.nv2)
    made_g2d = spread(
        "g2d", lambda p: s["P2S"].at[p], lambda k: s["R2D"].at[k], nd, dev_peer, lambda p: p < plan.nv2
    )

    def sum_pieces(made, own, received, dst, flat, group, valid):
        mine = dev < valid

        @pl.when(mine)
        def _():
            total = own[dev]
            for k, c in made:
                c.wait_recv()
                total = total + received[k]
            flat[...] = total
            dst[dev] = total

        return spread(group, lambda p: flat, lambda k: dst.at[dev], nd, dev_peer, lambda p: mine)

    made_g3a = sum_pieces(made_g3d, s["P3S"], s["R3D"], s["F3"], s["Q3"], "g3a", plan.nv3)

    gather(made_g1h)
    total = s["G1S"][...]
    for k in range(1, nh):
        total = total + s["R1H"][k]
    s["G1D"][...] = total
    made_g1d = spread("g1d", lambda p: s["G1D"], lambda k: s["R1D"].at[k], nd, dev_peer)

    made_g2a = sum_pieces(made_g2d, s["P2S"], s["R2D"], s["F2"], s["Q2"], "g2a", plan.nv2)

    gather(made_g2a, lambda src: src < plan.nv2, nd, dev)
    made_g2z = spread(
        "g2z", lambda p: s["F2"].at[0 : plan.nv2], lambda k: s["F2H"].at[ha, 0 : plan.nv2], nh, ha_peer
    )
    s["F2H"][ha, 0 : plan.nv2] = s["F2"][0 : plan.nv2]

    gather(made_g1d)
    total = s["G1D"][...]
    for k in range(1, nd):
        total = total + s["R1D"][k]
    g1o[...] = total * scales[0]
    gather(made_g3a, lambda src: src < plan.nv3, nd, dev)
    g3o[...] = s["F3"][0 : plan.nv3] * scales[2]
    gather(made_out)
    o3[...] = s["OR"][...]
    gather(made_g2z)
    g2o[...] = s["F2H"][:, 0 : plan.nv2] * scales[1]

    for ok, c in pending:
        if ok is None:
            c.wait_send()
        else:
            pl.when(ok)(c.wait_send)


def local(nd, nh, volume, w_first, w_second, w_third, cotangent):
    plan = Plan(nd, nh)
    pb, mb = plan.pb, plan.mb
    cells = volume.shape[1] * nd * volume.shape[2] * nh * volume.shape[3]
    scales = tuple(1.0 / math.sqrt(cells // 8 ** n) for n in (1, 2, 3))
    w1n = jnp.pad(w_first.reshape(108, 32).T, ((0, 0), (0, 20)))
    w2 = w_second.reshape(864, 64)
    w3t = w_third.reshape(1728, pb).T
    cot = jnp.transpose(cotangent.reshape(pb, nh, 128), (1, 0, 2))
    scratch = plan.scratch()
    names = list(scratch)
    vmem = pl.BlockSpec(memory_space=pltpu.VMEM)
    out3, g1, g2, g3 = pl.pallas_call(
        functools.partial(kernel, plan, names, scales),
        out_shape=(
            jax.ShapeDtypeStruct((nh, pb, 128), BF),
            jax.ShapeDtypeStruct((32, 128), F32),
            jax.ShapeDtypeStruct((nh, plan.nv2, mb, plan.w2), F32),
            jax.ShapeDtypeStruct((plan.nv3, pb, plan.w3), F32),
        ),
        in_specs=[vmem] * 12,
        out_specs=(vmem,) * 4,
        scratch_shapes=[scratch[n] for n in names],
        compiler_params=pltpu.CompilerParams(
            collective_id=0 if nd * nh > 1 else None, has_side_effects=True, vmem_limit_bytes=60 * 2**20
        ),
        name="step",
    )(volume, w1n, w2, w3t, cot, *constants())
    out3 = jnp.transpose(out3.reshape(nh, pb, 2, 64), (1, 0, 2, 3)).reshape(pb, 1, 2 * nh, 64)
    g1 = g1[:, 0:108].T.reshape(3, 3, 3, 4, 32)
    g2 = jnp.transpose(g2, (1, 3, 0, 2)).reshape(plan.nv2 * plan.w2, 64)[0:864].reshape(3, 3, 3, 32, 64)
    g3 = jnp.transpose(g3, (0, 2, 1)).reshape(plan.nv3 * plan.w3, pb)[0:1728].reshape(3, 3, 3, 64, pb)
    return out3, g1, g2, g3


def solution(mesh):
    placed = (
        P(None, "dev", "ha", None),
        P(),
        P(),
        P(None, None, None, None, "ha"),
        P("ha", "dev", None, None),
    )
    return jax.shard_map(
        functools.partial(local, mesh.shape["dev"], mesh.shape["ha"]),
        mesh=mesh,
        in_specs=placed,
        out_specs=(P("ha", "dev", None, None), P(), P(), P(None, None, None, None, "ha")),
        check_vma=False,
    )
```

```python
import functools
import math
import types

import jax
import jax.numpy as jnp
import numpy as np
from jax import lax
from jax.experimental import pallas as pl
from jax.experimental.pallas import tpu as pltpu
from jax.sharding import PartitionSpec as P

MESH = pl.DeviceIdType.MESH
BF = jnp.bfloat16
F32 = jnp.float32


def dot(a, b):
    return lax.dot_general(a, b, (((1,), (0,)), ((), ())), preferred_element_type=F32)


def dot_nt(a, b):
    return lax.dot_general(a, b, (((1,), (1,)), ((), ())), preferred_element_type=F32)


def dot_tn(a, b):
    return lax.dot_general(a, b, (((0,), (0,)), ((), ())), preferred_element_type=F32)


def split_rows(x):
    high = x.astype(BF)
    low = (x - high.astype(F32)).astype(BF)
    return jnp.concatenate([high, low], 0)


def leaky_and_slope(z):
    soft = jnp.log(1.0 + jnp.exp(-4.0 * jnp.abs(z)))
    act = jnp.maximum(z, 0.3 * z) + 0.175 * soft
    return act, 0.65 + 0.35 * jnp.tanh(2.0 * z)


ORDER2 = np.concatenate([np.arange(0, 128, 2), np.arange(1, 128, 2)])
ORDER1 = np.concatenate([2 * ORDER2, 2 * ORDER2 + 1])


def constants(nh):
    expand = np.zeros((128, 1152), np.float32)
    for a in range(3):
        for e in range(3):
            for c in range(4):
                for h in range(16):
                    col = a * 192 + e * 64 + c * 16 + h
                    row = lambda b: ((a * 3 + b) * 3 + e) * 4 + c
                    expand[row(1 + h % 2), col] = 1
                    if h % 2:
                        expand[row(0), 576 + col] = 1
    halo = np.zeros((128, 1024), np.float32)
    for i in range(4):
        for a in range(3):
            d = 2 * i - 1 + a
            s, plane = (0, d) if d >= 0 else (1, 7)
            for e in range(3):
                for c in range(4):
                    row = (a * 9 + e) * 4 + c
                    halo[row, i * 256 + e * 64 + s * 32 + plane * 4 + c] = 1
    columns = np.zeros((512, 768), np.float32)
    for e in range(3):
        for p in range(256):
            w = 2 * ORDER1[p] - 1 + e
            if w >= 0:
                columns[w, e * 256 + p] = 1
    where2 = {int(l): q for q, l in enumerate(ORDER2)}
    shift2 = np.zeros((128, 128), np.float32)
    for p in range(128):
        if ORDER2[p] >= 1:
            shift2[where2[int(ORDER2[p]) - 1], p] = 1
    taps3 = np.zeros((256, 384), np.float32)
    for jj in range(2):
        for e in range(3):
            for l in range(64):
                w = 2 * l - 1 + e
                if w >= 0:
                    taps3[jj * 128 + where2[w], e * 128 + jj * 64 + l] = 1
    last = np.zeros((32, 512), np.float32)
    for d in range(8):
        for c in range(4):
            last[d * 4 + c, c * 128 + d * 16 + 15] = 1
    pb = 128 // nh
    rows = np.zeros((256, 256), np.float32)
    for jj in range(2):
        for q in range(nh):
            for ch in range(pb):
                rows[(jj * nh + q) * pb + ch, ch * 2 * nh + 2 * q + jj] = 1
    made = (expand, halo, columns, shift2, taps3, last, np.eye(64), rows)
    return [jnp.asarray(x, BF) for x in made]


class Plan:
    def __init__(self, nd, nh):
        self.nd, self.nh = nd, nh
        self.nc = 2 if nd > 1 else 1
        self.nz = nd // self.nc
        self.pb = 128 // nh
        self.mb = 64 // nh
        self.r2 = 512 // (self.nc * nh)
        self.half = 1792 // self.nc
        self.sem = {}
        count = 0
        names = ["vd0", "vd1", "vd2", "vd3", "vh", "vc", "adi", "adj", "ahi", "ahj", "ac", "bd", "bh", "bc", "3d", "3h", "3c", "sd", "sh", "sc"]
        for name in names + ["w3c", "g3c", "g3p"]:
            self.sem[name] = count
            count += 1
        for name in ["w3", "cot", "out", "g3h"]:
            self.sem[name] = count
            count += nh - 1
        for name in ["g2h", "g2z", "g1h"]:
            self.sem[name] = count
            count += nh * self.nc - 1
        for name in ["g3d", "g2d", "g1d"]:
            self.sem[name] = count
            count += self.nz - 1
        self.count = count

    def scratch(self):
        nd, nh, nc, pb, mb = self.nd, self.nh, self.nc, self.pb, self.mb
        v = pltpu.VMEM
        return dict(
            V0=v((64, 512), BF),
            HS=v((32, 512), BF),
            HR=v((2, 32, 512), BF),
            T1=v((9, 192, 256), BF),
            TH=v((192, 256), BF),
            W1F=v((128, 32), F32),
            WT=v((256, 576), BF),
            WH=v((4, 32, 192), BF),
            PH=v((4, 32, 256), F32),
            Z0=v((4, 32, 256), F32),
            A1=v((5, 288, 256), BF),
            S1=v((4, 256, 256), F32),
            T2=v((5, 864, 128), BF),
            W2T=v((3, 64, 288), BF),
            A2=v((3, 320, 128), BF),
            S2=v((2, 256, 128), F32),
            T3=v((3, 576, 128), BF),
            W3A=v((pb, 1792), BF),
            W3=v((nh, pb, 1792), BF),
            W3T=v((1792, 128), BF),
            CS=v((nh, pb, 128), BF),
            COT=v((nh, pb, 128), BF),
            OS=v((nh, pb, 128), BF),
            OR=v((nh, pb, 128), BF),
            D3=v((128, 128), BF),
            D3D=v((128, 128), BF),
            D3P=v((64, 128), BF),
            D3H=v((64, 128), BF),
            D3C=v((64, 128), BF),
            SS=v((2, 256, 128), BF),
            SD=v((256, 128), BF),
            SH=v((2, 64, 128), BF),
            SC=v((64, 128), BF),
            B2=v((3, 320, 128), F32),
            DL2=v((3, 320, 128), BF),
            Y=v((5, 288, 128), F32),
            B1=v((4, 256, 256), F32),
            DL1=v((4, 256, 256), BF),
            G3F=v((nh, pb, 1792), F32),
            G3S=v((nh, pb, 1792), BF),
            R3C=v((nh, pb, self.half), BF),
            G3T=v((nh, pb, self.half), F32),
            G3U=v((nh, pb, self.half), BF),
            R3H=v((nh, pb, self.half), BF),
            P3S=v((pb, self.half), BF),
            R3D=v((self.nz, pb, self.half), BF),
            P3F=v((pb, self.half), F32),
            F3=v((nc, pb, self.half), F32),
            G2F=v((nc, nh, self.r2, 128), F32),
            G2S=v((nc, nh, self.r2, 128), BF),
            R2H=v((nc * nh, self.r2, 128), BF),
            G2D=v((self.r2, 128), BF),
            R2D=v((self.nz, self.r2, 128), BF),
            F2=v((self.r2, 128), BF),
            F2H=v((nc, nh, self.r2, 128), BF),
            G1A=v((256, 576), F32),
            G1S=v((32, 128), BF),
            R1H=v((nc * nh, 32, 128), BF),
            G1D=v((32, 128), BF),
            R1D=v((self.nz, 32, 128), BF),
            G1O=v((32, 128), F32),
            ss=pltpu.SemaphoreType.DMA((self.count,)),
            rs=pltpu.SemaphoreType.DMA((self.count,)),
            ls=pltpu.SemaphoreType.DMA((16,)),
        )


INPUTS = ["vol", "w1", "w2", "w3", "cot", "expand", "halo", "columns", "shift2", "taps3", "last", "eye", "rows"]


def kernel(plan, names, *refs):
    nd, nh, nc, nz, pb, mb, half = plan.nd, plan.nh, plan.nc, plan.nz, plan.pb, plan.mb, plan.half
    inputs = dict(zip(INPUTS, refs[: len(INPUTS)]))
    o3, g1o, g2o, g3o = refs[len(INPUTS) : len(INPUTS) + 4]
    s = types.SimpleNamespace(**dict(zip(names, refs[len(INPUTS) + 4 :])))
    ss, rs = s.ss, s.rs
    dev, ha = lax.axis_index("dev"), lax.axis_index("ha")
    core, zy = (dev & 1, dev >> 1) if nc == 2 else (dev * 0, dev)
    up_d, up_h = dev < nd - 1, ha < nh - 1
    lo_d, lo_h = dev > 0, ha > 0
    up_c, lo_c = up_d & up_h, lo_d & lo_h

    order = ["vol", "w3", "last", "columns", "w1", "expand", "halo", "cot", "rows", "w2", "eye", "shift2", "taps3"]
    copies = {}
    for k, name in enumerate(order):
        copies[name] = pltpu.make_async_copy(inputs[name], getattr(s, "i_" + name), s.ls.at[k])
        copies[name].start()
    arrived = set()

    def take(name):
        if name not in arrived:
            arrived.add(name)
            copies[name].wait()
        return getattr(s, "i_" + name)

    sizes = {"h": nh, "a": nh * nc, "z": nz}

    def wrap(x, n):
        return x & (n - 1) if n & (n - 1) == 0 else lax.rem(x, n)

    peers = {"h": [(dev, wrap(ha + k, nh)) for k in range(nh)]}
    peers["z"] = [(wrap(zy + k, nz) * nc + core, ha) for k in range(nz)]
    peers["a"] = []
    for k in range(nh * nc):
        index = wrap(ha * nc + core + k, nh * nc)
        peers["a"].append((zy * nc + wrap(index, nc), index // nc if nc == 1 else index >> 1))

    def peer_of(group, k):
        return peers[group][k]

    if nd * nh > 1:
        barrier = pltpu.get_barrier_semaphore()
        count = 0
        for group in ("a", "z"):
            for k in range(1, sizes[group]):
                pl.semaphore_signal(barrier, inc=1, device_id=peer_of(group, k), device_id_type=MESH)
                count += 1
        last_core, first_core = core == nc - 1, core == 0
        for ok, target in (
            (up_d & last_core, (dev + 1, ha)),
            (lo_d & first_core, (dev - 1, ha)),
            (up_c & last_core, (dev + 1, ha + 1)),
            (lo_c & first_core, (dev - 1, ha - 1)),
        ):

            @pl.when(ok)
            def _():
                pl.semaphore_signal(barrier, inc=1, device_id=target, device_id_type=MESH)

            count = count + ok.astype(jnp.int32)

    def copy(src, dst, k, target):
        return pltpu.make_async_remote_copy(
            src_ref=src, dst_ref=dst, send_sem=ss.at[k], recv_sem=rs.at[k], device_id=target, device_id_type=MESH
        )

    routes = {
        "d": (up_d, lo_d, nd > 1, (jnp.minimum(dev + 1, nd - 1), ha)),
        "h": (up_h, lo_h, nh > 1, (dev, jnp.minimum(ha + 1, nh - 1))),
        "c": (up_c, lo_c, nd > 1 and nh > 1, (jnp.minimum(dev + 1, nd - 1), jnp.minimum(ha + 1, nh - 1))),
    }
    back = {
        "d": (lo_d, up_d, nd > 1, (jnp.maximum(dev - 1, 0), ha)),
        "h": (lo_h, up_h, nh > 1, (dev, jnp.maximum(ha - 1, 0))),
        "c": (lo_c, up_c, nd > 1 and nh > 1, (jnp.maximum(dev - 1, 0), jnp.maximum(ha - 1, 0))),
    }
    pending = []

    def send(name, src, dst, table=routes):
        can_send, can_receive, exists, target = table[name[1]]
        if not exists:
            return
        c = copy(src, dst, plan.sem[name], target)
        pl.when(can_send)(c.start)
        pending.append((can_send, c))

    def receive(name, src, dst, table=routes):
        can_send, can_receive, exists, target = table[name[1]]
        if not exists:
            return
        c = copy(src, dst, plan.sem[name], target)
        pl.when(can_receive)(c.wait_recv)

    def blank(kind, ref, table=routes):
        can_send, can_receive, exists, target = table[kind]

        @pl.when(jnp.logical_not(can_receive))
        def _():
            ref[...] = jnp.zeros(ref.shape, ref.dtype)

    def spread(group, name, src_of, dst, valid_send=None):
        made = []
        for k in range(1, sizes[group]):
            target = peer_of(group, k)
            c = copy(src_of(*target), dst(k), plan.sem[name] + k - 1, target)
            ok = None if valid_send is None else valid_send(target[0])
            if ok is None:
                c.start()
            else:
                pl.when(ok)(c.start)
            pending.append((ok, c))
            made.append((k, c))
        return made

    def gather(made, valid_receive=None):
        for k, c in made:
            if valid_receive is None:
                c.wait_recv()
            else:
                pl.when(valid_receive(lax.rem(zy + nz - k, nz)))(c.wait_recv)

    def to_partner(name, src, dst):
        c = copy(src, dst, plan.sem[name], (dev + 1 - 2 * core, ha))
        c.start()
        pending.append((None, c))
        return c

    blank("d", s.V0)
    blank("h", s.HR.at[0])
    s.HR[1, 0:16, :] = jnp.zeros((16, 512), BF)
    blank("c", s.HR.at[1, 16:32])
    blank("h", s.A1.at[1:5, 0:32])
    blank("d", s.A1.at[0, 32:288])
    blank("c", s.A1.at[0, 0:32])
    blank("h", s.A2.at[1:3, 0:64])
    blank("d", s.A2.at[0, 64:320])
    blank("c", s.A2.at[0, 0:64])
    blank("d", s.D3D, back)
    blank("h", s.D3H, back)
    blank("c", s.D3C, back)
    blank("d", s.SD, back)
    blank("h", s.SH, back)
    blank("c", s.SC, back)

    if nd * nh > 1:
        pl.semaphore_wait(barrier, count)
    halos_v = [("vd%d" % c, inputs["vol"].at[c, 7], s.V0.at[c * 16 : c * 16 + 16]) for c in range(4)]
    for halo_v in halos_v:
        send(*halo_v)
    w3_in = take("w3")
    for t in range(27):
        s.W3A[:, t * 64 : t * 64 + 64] = w3_in[t]
    s.W3A[:, 1728:1792] = jnp.zeros((pb, 64), BF)
    for c in range(nc):

        @pl.when(core == c)
        def _():
            s.W3[ha, :, c * half : c * half + half] = s.W3A[:, c * half : c * half + half]

    vol = take("vol")
    s.HS[...] = dot(take("last")[...], vol[...].reshape(512, 512)).astype(BF)
    halos_v = halos_v + [("vh", s.HS, s.HR.at[0]), ("vc", s.HS.at[16:32], s.HR.at[1, 16:32])]
    for halo_v in halos_v[4:]:
        send(*halo_v)

    def taps_of(rows):
        return dot(rows, take("columns")[...]).astype(BF)

    for c in range(4):
        taps = taps_of(vol[c].reshape(128, 512))
        for d in range(8):
            for e in range(3):
                s.T1[1 + d, e * 64 + c * 16 : e * 64 + c * 16 + 16, :] = taps[
                    d * 16 : d * 16 + 16, e * 256 : e * 256 + 256
                ]

    w1 = take("w1")
    s.W1F[96:128, :] = jnp.zeros((32, 32), F32)
    for t in range(27):
        s.W1F[4 * t : 4 * t + 4, :] = w1[t].astype(F32)
    w1b = s.W1F[...].astype(BF)
    base = dot_tn(w1b, take("expand")[...])
    base_a, base_b = base[:, 0:576], base[:, 576:1152]
    row_h = lax.broadcasted_iota(jnp.int32, (32, 576), 1) & 15

    def tap_masks(j):
        return (row_h >> 1) == j, ((row_h & 1) == 1) & (((row_h + 1) >> 1) == j)

    for j in range(8):
        mask_a, mask_b = tap_masks(j)
        s.WT[j * 32 : j * 32 + 32, :] = jnp.where(mask_a, base_a, jnp.where(mask_b, base_b, 0.0)).astype(BF)
    edge = dot_tn(w1b, take("halo")[...]).astype(BF)
    for i in range(4):
        s.WH[i] = edge[:, i * 256 : i * 256 + 192]

    def first(i):
        z = dot(s.WT[...], s.T1[pl.ds(2 * i, 3)].reshape(576, 256))
        s.Z0[i] = z[0:32]
        act, slope = leaky_and_slope(z[32:256])
        s.A1[i + 1, 64:288, :] = act.astype(BF)
        s.S1[i, 32:256, :] = slope

    def second_taps(plane, lo, hi):
        x = s.A1[plane, lo * 32 : hi * 32, :]
        moved = dot(x[:, 128:256], take("shift2")[...]).astype(BF)
        for j in range(lo, hi):
            r = (j - lo) * 32
            s.T2[plane, j * 96 : j * 96 + 32, :] = moved[r : r + 32]
            s.T2[plane, j * 96 + 32 : j * 96 + 64, :] = x[r : r + 32, 0:128]
            s.T2[plane, j * 96 + 64 : j * 96 + 96, :] = x[r : r + 32, 128:256]

    first(3)
    a1 = s.A1
    halo_adi = ("adi", a1.at[4, 64:288], a1.at[0, 64:288])
    halo_adj = ("adj", a1.at[4, 32:64], a1.at[0, 32:64])
    halo_ac = ("ac", a1.at[4, 256:288], a1.at[0, 0:32])
    halo_ahi = ("ahi", a1.at[2:5, 256:288], a1.at[2:5, 0:32])
    halo_ahj = ("ahj", a1.at[1, 256:288], a1.at[1, 0:32])
    send(*halo_adi)
    send(*halo_ac)

    def loop_first(i, carry):
        first(i)
        return carry

    lax.fori_loop(1, 3, loop_first, 0)
    send(*halo_ahi)

    my_half = pl.ds(pl.multiple_of(core * half, 128), half)
    made_w3 = spread("h", "w3", lambda d, h: s.W3A.at[:, my_half], lambda k: s.W3.at[ha, :, my_half])
    for halo_v in halos_v:
        receive(*halo_v)
    edges = taps_of(jnp.concatenate([s.V0[...], s.HR[...].reshape(64, 512)], 0))
    for e in range(3):
        s.T1[0, e * 64 : e * 64 + 64, :] = edges[0:64, e * 256 : e * 256 + 256]
        s.TH[e * 64 : e * 64 + 64, :] = edges[64:128, e * 256 : e * 256 + 256]
    s.PH[...] = dot(s.WH[...].reshape(128, 192), s.TH[...]).reshape(4, 32, 256)

    def top_rows(lo, hi):
        act, slope = leaky_and_slope(s.Z0[lo:hi] + s.PH[lo:hi])
        a1[lo + 1 : hi + 1, 32:64, :] = act.astype(BF)
        s.S1[lo:hi, 0:32, :] = slope

    top_rows(1, 4)
    send(*halo_adj)
    first(0)
    send(*halo_ahj)
    top_rows(0, 1)
    y = dot(take("rows")[...], take("cot")[...].reshape(256, 64)).astype(BF)
    s.CS[...] = jnp.concatenate([y[0:128], y[128:256]], 1).reshape(nh, pb, 128)
    s.COT[ha] = s.CS[ha]
    made_cot = spread("h", "cot", lambda d, h: s.CS.at[h], lambda k: s.COT.at[ha])
    take("shift2")

    def loop_taps(i, carry):
        second_taps(i, 2, 9)
        return carry

    lax.fori_loop(2, 5, loop_taps, 0)
    w2 = take("w2")
    take("eye")
    for a in range(3):
        s.W2T[a] = dot_nt(s.i_eye[...], w2[a * 288 : a * 288 + 288, :]).astype(BF)

    second_taps(1, 1, 9)
    for plane in (2, 3, 4):
        second_taps(plane, 1, 2)

    def second(i, j):
        z = None
        for a in range(3):
            term = dot(s.W2T[a], s.T2[2 * i + a, j * 192 : j * 192 + 288, :])
            z = term if z is None else z + term
        act, slope = leaky_and_slope(z)
        s.A2[i + 1, 64 + 64 * j : 128 + 64 * j, :] = act.astype(BF)
        s.S2[i, 64 * j : 64 * j + 64, :] = slope
        if i == 0 or j == 0:
            s.SS[i, 64 * j : 64 * j + 64, :] = slope.astype(BF)

    for j in (1, 2, 3):
        second(1, j)
    a2 = s.A2
    halo_bd = ("bd", a2.at[2, 64:320], a2.at[0, 64:320])
    halo_bc = ("bc", a2.at[2, 256:320], a2.at[0, 0:64])
    halo_bh = ("bh", a2.at[1:3, 256:320], a2.at[1:3, 0:64])
    halos_b = [halo_bd, halo_bc, halo_bh]
    send(*halo_bc)
    for halo_a in (halo_adi, halo_adj, halo_ac, halo_ahi, halo_ahj):
        receive(*halo_a)
    second_taps(0, 6, 9)
    second(0, 3)
    send(*halo_bh)
    for plane in (2, 3, 4):
        second_taps(plane, 0, 1)
    second(1, 0)
    send(*halo_bd)
    second_taps(0, 0, 6)
    second_taps(1, 0, 1)
    for j in (2, 1, 0):
        second(0, j)
    s2 = s.S2
    halos_s = [
        ("sd", s.SS.at[0], s.SD),
        ("sh", s.SS.at[0:2, 0:64], s.SH),
        ("sc", s.SS.at[0, 0:64], s.SC),
    ]
    for halo_s in halos_s:
        send(*halo_s, back)

    gather(made_w3)
    if nc == 2:
        other = pl.ds(pl.multiple_of((1 - core) * half, 128), half)
        to_partner("w3c", s.W3.at[:, :, my_half], s.W3.at[:, :, my_half])
        w3_other = copy(
            s.W3.at[:, :, other], s.W3.at[:, :, other], plan.sem["w3c"], (dev + 1 - 2 * core, ha)
        )

    def third_taps(blocks):
        x = [
            jnp.concatenate([a2[plane, b * 64 : b * 64 + 64, :], a2[plane, b * 64 + 128 : b * 64 + 192, :]], 1)
            for plane, b in blocks
        ]
        y = dot(jnp.concatenate(x, 0), take("taps3")[...]).astype(BF)
        for k, (plane, b) in enumerate(blocks):
            for e in range(3):
                s.T3[plane, b * 192 + e * 64 : b * 192 + e * 64 + 64, :] = y[
                    64 * k : 64 * k + 64, e * 128 : e * 128 + 128
                ]

    third_taps([(1, 1), (1, 2), (2, 1), (2, 2)])
    if nc == 2:
        w3_other.wait_recv()
    s.W3T[...] = s.W3[...].reshape(128, 1792).T
    for halo_b in halos_b:
        receive(*halo_b)
    gather(made_cot)
    third_taps([(0, 0), (0, 1), (0, 2), (1, 0), (2, 0)])
    t3 = s.T3[...].reshape(1728, 128)
    act, slope = leaky_and_slope(dot(s.W3[...].reshape(128, 1792)[:, 0:1728], t3))
    delta3 = (s.COT[...].reshape(128, 128).astype(F32) * slope).astype(BF)
    s.D3[...] = delta3
    s.OS[...] = act.astype(BF).reshape(nh, pb, 128)
    s.D3P[...] = jnp.concatenate([delta3[0:64, 0:64], delta3[64:128, 0:64]], 1)
    halos_3 = [("3d", s.D3, s.D3D), ("3h", s.D3P, s.D3H), ("3c", s.D3P, s.D3C)]
    for halo_3 in halos_3:
        send(*halo_3, back)

    lane3 = lax.broadcasted_iota(jnp.int32, (64, 128), 1)

    def third_back(parts):
        made = []
        for a, b, d in parts:
            r = a * 576 + b * 192
            x = dot(s.W3T[r : r + 192, :], d)
            even = x[64:128]
            odd = x[128:192] + jnp.where((lane3 & 63) == 63, 0.0, pltpu.roll(x[0:64], 127, 1))
            first_height = jnp.where(lane3 < 64, even, pltpu.roll(odd, 64, 1))
            made.append((first_height, jnp.where(lane3 < 64, pltpu.roll(even, 64, 1), odd)))
        return made

    b2 = s.B2
    one1, one2, two1, two2 = third_back([(1, 1, delta3), (1, 2, delta3), (2, 1, delta3), (2, 2, delta3)])
    for i, tap1, tap2 in ((0, one1, one2), (1, two1, two2)):
        b2[i, 0:64, :] = tap1[0]
        b2[i, 64:128, :] = tap2[0]
        b2[i, 128:192, :] = tap1[1]
        b2[i, 192:256, :] = tap2[1]
    g3 = dot_nt(delta3, t3)
    s.G3F[:, :, 1728:1792] = jnp.zeros((nh, pb, 64), F32)
    s.G3S[:, :, 1728:1792] = jnp.zeros((nh, pb, 64), BF)
    s.G3F[:, :, 0:1728] = g3.reshape(nh, pb, 1728)
    s.G3S[:, :, 0:1728] = g3.astype(BF).reshape(nh, pb, 1728)
    if nc == 2:
        g3c = to_partner("g3c", s.G3S.at[:, :, other], s.R3C)

    for c in range(nc):

        @pl.when(core == c)
        def _():
            total = s.G3F[:, :, c * half : c * half + half]
            if nc == 2:
                g3c.wait_recv()
                total = total + s.R3C[...].astype(F32)
            s.G3T[...] = total
            s.G3U[...] = total.astype(BF)

    made_g3h = spread("h", "g3h", lambda d, h: s.G3U.at[h], lambda k: s.R3H.at[k])

    for halo_3 in halos_3:
        receive(*halo_3, back)
    next_h = jnp.concatenate([s.D3H[:, 0:64], s.D3H[:, 64:128]], 0)
    next_c = jnp.concatenate([s.D3C[:, 0:64], s.D3C[:, 64:128]], 0)
    own = jnp.concatenate([delta3[:, 64:128], next_h], 1)
    deep = s.D3D[...]
    deep_next = jnp.concatenate([deep[:, 64:128], next_c], 1)
    beside = jnp.concatenate([next_h, next_c], 1)
    one0, two0, zero0, zero1, zero2 = third_back(
        [(1, 0, own), (2, 0, own), (0, 0, deep_next), (0, 1, deep), (0, 2, deep)]
    )
    deep0, deep1, deep2, side1, side2, side0 = third_back(
        [(1, 0, deep_next), (1, 1, deep), (1, 2, deep), (1, 1, beside), (2, 1, beside), (0, 1, beside)]
    )
    dl2 = s.DL2
    b2[0, 64:128, :] += one0[0]
    b2[0, 192:256, :] += one0[1]
    b2[0, 256:320, :] = side1[0]
    b2[1, 0:64, :] += zero1[0]
    b2[1, 64:128, :] += two0[0] + zero0[0] + zero2[0]
    b2[1, 128:192, :] += zero1[1]
    b2[1, 192:256, :] += two0[1] + zero0[1] + zero2[1]
    b2[1, 256:320, :] = side2[0] + side0[1]
    b2[2, 0:64, :] = deep1[0]
    b2[2, 64:128, :] = deep0[0] + deep2[0]
    b2[2, 128:192, :] = deep1[1]
    b2[2, 192:256, :] = deep0[1] + deep2[1]
    b2[2, 256:320, :] = side1[1]
    for halo_s in halos_s:
        receive(*halo_s, back)
    dl2[0:2, 0:256, :] = (b2[0:2, 0:256, :] * s2[...]).astype(BF)
    dl2[2, 0:256, :] = (b2[2, 0:256, :] * s.SD[...].astype(F32)).astype(BF)
    dl2[0:2, 256:320, :] = (b2[0:2, 256:320, :] * s.SH[...].astype(F32)).astype(BF)
    dl2[2, 256:320, :] = (b2[2, 256:320, :] * s.SC[...].astype(F32)).astype(BF)

    low = high = None
    none = jnp.zeros((64, 256), BF)
    for i in range(2):
        for j in (0, 2):
            x = jnp.concatenate([dl2[i, 64 * (j + t) : 64 * (j + t) + 64, :] for t in (0, 1)], 1)
            t2 = jnp.concatenate(
                [s.T2[2 * i : 2 * i + 3, 192 * (j + t) : 192 * (j + t) + 288, :].reshape(864, 128) for t in (0, 1)], 1
            )
            term = dot_nt(t2[0:512], jnp.concatenate([x, none], 0))
            low = term if low is None else low + term
            term = dot_nt(t2[512:864], jnp.concatenate([none, x], 0))
            high = term if high is None else high + term
    g2 = jnp.concatenate([low[0:352] + high, low[352:512]], 0).reshape(nc, nh, plan.r2, 128)
    s.G2F[...] = g2
    s.G2S[...] = g2.astype(BF)
    made_g2h = spread("a", "g2h", lambda d, h: s.G2S.at[d & (nc - 1), h], lambda k: s.R2H.at[k])
    made_out = spread("h", "out", lambda d, h: s.OS.at[h], lambda k: s.OR.at[ha])
    s.OR[ha] = s.OS[ha]

    lane = lax.broadcasted_iota(jnp.int32, (32, 128), 1)

    def second_back(plane, pairs, lo, hi):
        for j in range(lo // 2, hi // 2 + 1):
            y = None
            for a, i in pairs:
                term = dot(w2[a * 288 : a * 288 + 288, :], dl2[i, j * 64 : j * 64 + 64, :])
                y = term if y is None else y + term
            s.Y[j] = y
        for k in range(lo, hi):
            j = (k + 1) // 2
            d = s.Y[j, 0:96, :] + s.Y[j - 1, 192:288, :] if k % 2 else s.Y[j, 96:192, :]
            moved = jnp.where(lane < 64, pltpu.roll(d[0:32], 64, 1), pltpu.roll(d[0:32], 63, 1))
            moved = jnp.where(lane == 127, 0.0, moved)
            s.B1[plane, 32 * k : 32 * k + 32, 0:128] = d[32:64]
            s.B1[plane, 32 * k : 32 * k + 32, 128:256] = d[64:96] + moved

    planes = [[(1, 0)], [(2, 0), (0, 1)], [(1, 1)], [(2, 1), (0, 2)]]
    for plane in range(4):
        second_back(plane, planes[plane], 0, 8)

    s.G1A[...] = jnp.zeros((256, 576), F32)

    def loop_back(i, carry):
        d = (s.B1[i] * s.S1[i]).astype(BF)
        s.DL1[i] = d
        s.G1A[...] += dot_nt(d, s.T1[pl.ds(2 * i, 3)].reshape(576, 256))
        return carry

    lax.fori_loop(0, 4, loop_back, 0)
    def sum_parts(total, received, size):
        for k in range(1, size):
            total = total + received[k].astype(F32)
        return total

    gh = dot_nt(s.DL1[:, 0:32, :].reshape(128, 256), s.TH[...])
    sum_a = jnp.zeros((32, 576), F32)
    sum_b = jnp.zeros((32, 576), F32)
    for j in range(8):
        mask_a, mask_b = tap_masks(j)
        g = s.G1A[32 * j : 32 * j + 32, :]
        sum_a = sum_a + jnp.where(mask_a, g, 0.0)
        sum_b = sum_b + jnp.where(mask_b, g, 0.0)
    g1 = dot_nt(split_rows(sum_a), s.i_expand[:, 0:576])
    g1 = g1 + dot_nt(split_rows(sum_b), s.i_expand[:, 576:1152])
    for i in range(4):
        g1 = g1 + dot_nt(split_rows(gh[32 * i : 32 * i + 32]), s.i_halo[:, i * 256 : i * 256 + 192])
    g1 = g1[0:32] + g1[32:64]
    s.G1S[...] = g1.astype(BF)
    made_g1h = spread("a", "g1h", lambda d, h: s.G1S, lambda k: s.R1H.at[k])

    gather(made_g3h)
    total = sum_parts(s.G3T[ha], s.R3H, nh)
    s.P3F[...] = total
    s.P3S[...] = total.astype(BF)
    made_g3d = spread("z", "g3d", lambda d, h: s.P3S, lambda k: s.R3D.at[k])
    gather(made_g2h)
    g2 = sum_parts(s.G2F[core, ha], s.R2H, nh * nc)
    s.G2D[...] = g2.astype(BF)
    made_g2d = spread("z", "g2d", lambda d, h: s.G2D, lambda k: s.R2D.at[k])
    results = []

    def result(name, ref):
        c = pltpu.make_async_copy(getattr(s, name), ref, s.ls.at[len(results)])
        c.start()
        results.append(c)

    gather(made_out)
    result("OR", o3)
    gather(made_g1h)
    g1 = sum_parts(g1, s.R1H, nh * nc)
    s.G1D[...] = g1.astype(BF)
    made_g1d = spread("z", "g1d", lambda d, h: s.G1D, lambda k: s.R1D.at[k])
    gather(made_g2d)
    g2 = sum_parts(g2, s.R2D, nz)
    s.F2[...] = g2.astype(BF)
    s.F2H[core, ha] = g2.astype(BF)
    made_g2z = spread("a", "g2z", lambda d, h: s.F2, lambda k: s.F2H.at[core, ha])
    gather(made_g3d)
    s.F3[core] = sum_parts(s.P3F[...], s.R3D, nz)
    if nc == 2:
        to_partner("g3p", s.F3.at[core], s.F3.at[core])
        g3p = copy(s.F3.at[1 - core], s.F3.at[1 - core], plan.sem["g3p"], (dev + 1 - 2 * core, ha))
    gather(made_g1d)
    s.G1O[...] = sum_parts(g1, s.R1D, nz)
    result("G1O", g1o)
    gather(made_g2z)
    result("F2H", g2o)
    if nc == 2:
        g3p.wait_recv()
    result("F3", g3o)
    for c in results:
        c.wait()
    for ok, c in pending:
        if ok is None:
            c.wait_send()
        else:
            pl.when(ok)(c.wait_send)


def finish(plan, scales, *refs):
    nh, nc, pb = plan.nh, plan.nc, plan.pb
    out, g1, g2, g3 = refs[1:5]
    rows, o3, g1o, g2o, g3o, sem = refs[9:15]
    copied = pltpu.make_async_copy(refs[0], rows, sem.at[0])
    copied.start()
    sent = []

    def result(ref, to):
        c = pltpu.make_async_copy(ref, to, sem.at[len(sent) + 1])
        c.start()
        sent.append(c)

    x = g2[...].reshape(512, 128).astype(F32) * scales[1]
    g2o[0:512, :] = x[:, 0:64]
    g2o[512:864, :] = x[0:352, 64:128]
    result(g2o, refs[7])
    for t in range(27):
        c, r = divmod(64 * t, plan.half)
        g3o[t] = g3[c, :, r : r + 64] * scales[2]
    result(g3o, refs[8])
    x = (g1[...] * scales[0]).T
    for t in range(27):
        g1o[t] = x[4 * t : 4 * t + 4]
    result(g1o, refs[6])
    copied.wait()
    x = out[...].reshape(128, 128)
    x = jnp.concatenate([x[:, 0:64], x[:, 64:128]], 0)
    o3[...] = dot_tn(rows[...], x).astype(BF).reshape(pb, 2 * nh, 64)
    result(o3, refs[5])
    for c in sent:
        c.wait()


def local(nd, nh, volume, w_first, w_second, w_third, cotangent):
    plan = Plan(nd, nh)
    pb = plan.pb
    cells = volume.shape[1] * nd * volume.shape[2] * nh * volume.shape[3]
    scales = tuple(1.0 / math.sqrt(cells // 8**n) for n in (1, 2, 3))
    inputs = dict(
        vol=volume,
        w1=w_first.reshape(27, 4, 32),
        w2=w_second.reshape(864, 64),
        w3=jnp.transpose(w_third.reshape(27, 64, pb), (0, 2, 1)),
        cot=cotangent.reshape(pb, 2 * nh, 64),
    )
    inputs.update(zip(INPUTS[5:], constants(nh)))
    scratch = plan.scratch()
    for name in INPUTS:
        scratch["i_" + name] = pltpu.VMEM(inputs[name].shape, BF)
    names = list(scratch)
    vmem, hbm = pl.BlockSpec(memory_space=pltpu.VMEM), pl.BlockSpec(memory_space=pltpu.HBM)
    summed = pl.pallas_call(
        functools.partial(kernel, plan, names),
        out_shape=(
            pltpu.VMEM((nh, pb, 128), BF),
            pltpu.VMEM((32, 128), F32),
            pltpu.VMEM((plan.nc, nh, plan.r2, 128), BF),
            pltpu.VMEM((plan.nc, pb, plan.half), F32),
        ),
        in_specs=[hbm] * len(INPUTS),
        out_specs=(vmem,) * 4,
        scratch_shapes=[scratch[n] for n in names],
        compiler_params=pltpu.CompilerParams(
            collective_id=0 if nd * nh > 1 else None, has_side_effects=True, vmem_limit_bytes=48 * 2**20
        ),
        name="step",
    )(*[pltpu.with_memory_space_constraint(inputs[n], pltpu.HBM) for n in INPUTS])
    shapes = [((pb, 2 * nh, 64), BF), ((27, 4, 32), F32), ((864, 64), F32), ((27, pb, 64), F32)]
    out3, g1, g2, g3 = pl.pallas_call(
        functools.partial(finish, plan, scales),
        out_shape=[jax.ShapeDtypeStruct(*x) for x in shapes],
        in_specs=[hbm] + [vmem] * 4,
        out_specs=[hbm] * 4,
        scratch_shapes=[pltpu.VMEM((256, 256), BF)] + [pltpu.VMEM(*x) for x in shapes] + [pltpu.SemaphoreType.DMA((5,))],
        compiler_params=pltpu.CompilerParams(vmem_limit_bytes=48 * 2**20),
        name="finish",
    )(pltpu.with_memory_space_constraint(inputs["rows"], pltpu.HBM), *summed)
    return (
        out3.reshape(pb, 1, 2 * nh, 64),
        g1.reshape(3, 3, 3, 4, 32),
        g2.reshape(3, 3, 3, 32, 64),
        jnp.transpose(g3, (0, 2, 1)).reshape(3, 3, 3, 64, pb),
    )


def solution(mesh):
    placed = (
        P(None, "dev", "ha", None),
        P(),
        P(),
        P(None, None, None, None, "ha"),
        P("ha", "dev", None, None),
    )
    return jax.shard_map(
        functools.partial(local, mesh.shape["dev"], mesh.shape["ha"]),
        mesh=mesh,
        in_specs=placed,
        out_specs=(P("ha", "dev", None, None), P(), P(), P(None, None, None, None, "ha")),
        check_vma=False,
    )
```

```python
import functools
import math
import types

import jax
import jax.numpy as jnp
import numpy as np
from jax import lax
from jax.experimental import pallas as pl
from jax.experimental.pallas import tpu as pltpu
from jax.sharding import PartitionSpec as P

MESH = pl.DeviceIdType.MESH
BF = jnp.bfloat16
F32 = jnp.float32


def dot(a, b):
    return lax.dot_general(a, b, (((1,), (0,)), ((), ())), preferred_element_type=F32)


def dot_nt(a, b):
    return lax.dot_general(a, b, (((1,), (1,)), ((), ())), preferred_element_type=F32)


def dot_tn(a, b):
    return lax.dot_general(a, b, (((0,), (0,)), ((), ())), preferred_element_type=F32)


def split_rows(x):
    high = x.astype(BF)
    low = (x - high.astype(F32)).astype(BF)
    return jnp.concatenate([high, low], 0)


def leaky_and_slope(z):
    soft = jnp.log(1.0 + jnp.exp(-4.0 * jnp.abs(z)))
    act = jnp.maximum(z, 0.3 * z) + 0.175 * soft
    return act, 0.65 + 0.35 * jnp.tanh(2.0 * z)


ORDER2 = np.concatenate([np.arange(0, 128, 2), np.arange(1, 128, 2)])
ORDER1 = np.concatenate([2 * ORDER2, 2 * ORDER2 + 1])


def constants(nh):
    expand = np.zeros((128, 1152), np.float32)
    for a in range(3):
        for e in range(3):
            for c in range(4):
                for h in range(16):
                    col = a * 192 + e * 64 + c * 16 + h
                    row = lambda b: ((a * 3 + b) * 3 + e) * 4 + c
                    expand[row(1 + h % 2), col] = 1
                    if h % 2:
                        expand[row(0), 576 + col] = 1
    halo = np.zeros((128, 1024), np.float32)
    for i in range(4):
        for a in range(3):
            d = 2 * i - 1 + a
            s, plane = (0, d) if d >= 0 else (1, 7)
            for e in range(3):
                for c in range(4):
                    row = (a * 9 + e) * 4 + c
                    halo[row, i * 256 + e * 64 + s * 32 + plane * 4 + c] = 1
    columns = np.zeros((512, 768), np.float32)
    for e in range(3):
        for p in range(256):
            w = 2 * ORDER1[p] - 1 + e
            if w >= 0:
                columns[w, e * 256 + p] = 1
    where2 = {int(l): q for q, l in enumerate(ORDER2)}
    shift2 = np.zeros((128, 128), np.float32)
    for p in range(128):
        if ORDER2[p] >= 1:
            shift2[where2[int(ORDER2[p]) - 1], p] = 1
    taps3 = np.zeros((256, 384), np.float32)
    for jj in range(2):
        for e in range(3):
            for l in range(64):
                w = 2 * l - 1 + e
                if w >= 0:
                    taps3[jj * 128 + where2[w], e * 128 + jj * 64 + l] = 1
    last = np.zeros((32, 512), np.float32)
    for d in range(8):
        for c in range(4):
            last[d * 4 + c, c * 128 + d * 16 + 15] = 1
    pb = 128 // nh
    rows = np.zeros((256, 256), np.float32)
    for jj in range(2):
        for q in range(nh):
            for ch in range(pb):
                rows[(jj * nh + q) * pb + ch, ch * 2 * nh + 2 * q + jj] = 1
    made = (expand, halo, columns, shift2, taps3, last, np.eye(64), rows)
    return [jnp.asarray(x, BF) for x in made]


class Plan:
    def __init__(self, nd, nh):
        self.nd, self.nh = nd, nh
        self.nc = 2 if nd > 1 else 1
        self.nz = nd // self.nc
        self.pb = 128 // nh
        self.mb = 64 // nh
        self.r2 = 512 // (self.nc * nh)
        self.half = 1792 // self.nc
        self.sem = {}
        count = 0
        names = ["vd0", "vd1", "vd2", "vd3", "vh", "vc", "adi", "adj", "ahi", "ahj", "ac", "bd", "bh", "bc", "3d", "3h", "3c", "sd", "sh", "sc"]
        for name in names + ["w3c", "g3c", "g3p"]:
            self.sem[name] = count
            count += 1
        for name in ["w3", "cot", "out", "g3h"]:
            self.sem[name] = count
            count += nh - 1
        for name in ["g2h", "g2z", "g1h"]:
            self.sem[name] = count
            count += nh * self.nc - 1
        for name in ["g3d", "g2d", "g1d"]:
            self.sem[name] = count
            count += self.nz - 1
        self.count = count

    def scratch(self):
        nd, nh, nc, pb, mb = self.nd, self.nh, self.nc, self.pb, self.mb
        v = pltpu.VMEM
        return dict(
            V0=v((64, 512), BF),
            HS=v((32, 512), BF),
            HR=v((2, 32, 512), BF),
            T1=v((9, 192, 256), BF),
            TH=v((192, 256), BF),
            W1F=v((128, 32), F32),
            WT=v((256, 576), BF),
            WH=v((4, 32, 192), BF),
            PH=v((4, 32, 256), F32),
            Z0=v((4, 32, 256), F32),
            A1=v((5, 288, 256), BF),
            S1=v((4, 256, 256), F32),
            T2=v((5, 864, 128), BF),
            W2T=v((3, 64, 288), BF),
            A2=v((3, 320, 128), BF),
            S2=v((2, 256, 128), F32),
            T3=v((3, 576, 128), BF),
            W3A=v((pb, 1792), BF),
            W3=v((nh, pb, 1792), BF),
            W3T=v((1792, 128), BF),
            CS=v((nh, pb, 128), BF),
            COT=v((nh, pb, 128), BF),
            OS=v((nh, pb, 128), BF),
            OR=v((nh, pb, 128), BF),
            D3=v((128, 128), BF),
            D3D=v((128, 128), BF),
            D3P=v((64, 128), BF),
            D3H=v((64, 128), BF),
            D3C=v((64, 128), BF),
            SS=v((2, 256, 128), BF),
            SD=v((256, 128), BF),
            SH=v((2, 64, 128), BF),
            SC=v((64, 128), BF),
            B2=v((3, 320, 128), F32),
            DL2=v((3, 320, 128), BF),
            Y=v((5, 288, 128), F32),
            B1=v((4, 256, 256), F32),
            DL1=v((4, 256, 256), BF),
            G3F=v((nh, pb, 1792), F32),
            G3S=v((nh, pb, 1792), BF),
            R3C=v((nh, pb, self.half), BF),
            G3T=v((nh, pb, self.half), F32),
            G3U=v((nh, pb, self.half), BF),
            R3H=v((nh, pb, self.half), BF),
            P3S=v((pb, self.half), BF),
            R3D=v((self.nz, pb, self.half), BF),
            P3F=v((pb, self.half), F32),
            F3=v((nc, pb, self.half), F32),
            G2F=v((nc, nh, self.r2, 128), F32),
            G2S=v((nc, nh, self.r2, 128), BF),
            R2H=v((nc * nh, self.r2, 128), BF),
            G2D=v((self.r2, 128), BF),
            R2D=v((self.nz, self.r2, 128), BF),
            F2=v((self.r2, 128), BF),
            F2H=v((nc, nh, self.r2, 128), BF),
            G1A=v((256, 576), F32),
            G1S=v((32, 128), BF),
            R1H=v((nc * nh, 32, 128), BF),
            G1D=v((32, 128), BF),
            R1D=v((self.nz, 32, 128), BF),
            ss=pltpu.SemaphoreType.DMA((self.count,)),
            rs=pltpu.SemaphoreType.DMA((self.count,)),
            ls=pltpu.SemaphoreType.DMA((16,)),
        )


INPUTS = ["vol", "w1", "w2", "w3", "cot", "expand", "halo", "columns", "shift2", "taps3", "last", "eye", "rows"]


def kernel(plan, names, scales, *refs):
    nd, nh, nc, nz, pb, mb, half = plan.nd, plan.nh, plan.nc, plan.nz, plan.pb, plan.mb, plan.half
    inputs = dict(zip(INPUTS, refs[: len(INPUTS)]))
    o3, g1o, g2o, g3o = refs[len(INPUTS) : len(INPUTS) + 4]
    s = types.SimpleNamespace(**dict(zip(names, refs[len(INPUTS) + 4 :])))
    ss, rs = s.ss, s.rs
    dev, ha = lax.axis_index("dev"), lax.axis_index("ha")
    core, zy = (dev & 1, dev >> 1) if nc == 2 else (dev * 0, dev)
    up_d, up_h = dev < nd - 1, ha < nh - 1
    lo_d, lo_h = dev > 0, ha > 0
    up_c, lo_c = up_d & up_h, lo_d & lo_h

    order = ["vol", "w3", "last", "columns", "w1", "expand", "halo", "cot", "rows", "w2", "eye", "shift2", "taps3"]
    copies = {}
    for k, name in enumerate(order):
        copies[name] = pltpu.make_async_copy(inputs[name], getattr(s, "i_" + name), s.ls.at[k])
        copies[name].start()
    arrived = set()

    def take(name):
        if name not in arrived:
            arrived.add(name)
            copies[name].wait()
        return getattr(s, "i_" + name)

    sizes = {"h": nh, "a": nh * nc, "z": nz}

    def wrap(x, n):
        return x & (n - 1) if n & (n - 1) == 0 else lax.rem(x, n)

    peers = {"h": [(dev, wrap(ha + k, nh)) for k in range(nh)]}
    peers["z"] = [(wrap(zy + k, nz) * nc + core, ha) for k in range(nz)]
    peers["a"] = []
    for k in range(nh * nc):
        index = wrap(ha * nc + core + k, nh * nc)
        peers["a"].append((zy * nc + wrap(index, nc), index // nc if nc == 1 else index >> 1))

    def peer_of(group, k):
        return peers[group][k]

    if nd * nh > 1:
        barrier = pltpu.get_barrier_semaphore()
        count = 0
        for group in ("a", "z"):
            for k in range(1, sizes[group]):
                pl.semaphore_signal(barrier, inc=1, device_id=peer_of(group, k), device_id_type=MESH)
                count += 1
        last_core, first_core = core == nc - 1, core == 0
        for ok, target in (
            (up_d & last_core, (dev + 1, ha)),
            (lo_d & first_core, (dev - 1, ha)),
            (up_c & last_core, (dev + 1, ha + 1)),
            (lo_c & first_core, (dev - 1, ha - 1)),
        ):

            @pl.when(ok)
            def _():
                pl.semaphore_signal(barrier, inc=1, device_id=target, device_id_type=MESH)

            count = count + ok.astype(jnp.int32)

    def copy(src, dst, k, target):
        return pltpu.make_async_remote_copy(
            src_ref=src, dst_ref=dst, send_sem=ss.at[k], recv_sem=rs.at[k], device_id=target, device_id_type=MESH
        )

    routes = {
        "d": (up_d, lo_d, nd > 1, (jnp.minimum(dev + 1, nd - 1), ha)),
        "h": (up_h, lo_h, nh > 1, (dev, jnp.minimum(ha + 1, nh - 1))),
        "c": (up_c, lo_c, nd > 1 and nh > 1, (jnp.minimum(dev + 1, nd - 1), jnp.minimum(ha + 1, nh - 1))),
    }
    back = {
        "d": (lo_d, up_d, nd > 1, (jnp.maximum(dev - 1, 0), ha)),
        "h": (lo_h, up_h, nh > 1, (dev, jnp.maximum(ha - 1, 0))),
        "c": (lo_c, up_c, nd > 1 and nh > 1, (jnp.maximum(dev - 1, 0), jnp.maximum(ha - 1, 0))),
    }
    pending = []

    def send(name, src, dst, table=routes):
        can_send, can_receive, exists, target = table[name[1]]
        if not exists:
            return
        c = copy(src, dst, plan.sem[name], target)
        pl.when(can_send)(c.start)
        pending.append((can_send, c))

    def receive(name, src, dst, table=routes):
        can_send, can_receive, exists, target = table[name[1]]
        if not exists:
            return
        c = copy(src, dst, plan.sem[name], target)
        pl.when(can_receive)(c.wait_recv)

    def blank(kind, ref, table=routes):
        can_send, can_receive, exists, target = table[kind]

        @pl.when(jnp.logical_not(can_receive))
        def _():
            ref[...] = jnp.zeros(ref.shape, ref.dtype)

    def spread(group, name, src_of, dst, valid_send=None):
        made = []
        for k in range(1, sizes[group]):
            target = peer_of(group, k)
            c = copy(src_of(*target), dst(k), plan.sem[name] + k - 1, target)
            ok = None if valid_send is None else valid_send(target[0])
            if ok is None:
                c.start()
            else:
                pl.when(ok)(c.start)
            pending.append((ok, c))
            made.append((k, c))
        return made

    def gather(made, valid_receive=None):
        for k, c in made:
            if valid_receive is None:
                c.wait_recv()
            else:
                pl.when(valid_receive(lax.rem(zy + nz - k, nz)))(c.wait_recv)

    def to_partner(name, src, dst):
        c = copy(src, dst, plan.sem[name], (dev + 1 - 2 * core, ha))
        c.start()
        pending.append((None, c))
        return c

    blank("d", s.V0)
    blank("h", s.HR.at[0])
    s.HR[1, 0:16, :] = jnp.zeros((16, 512), BF)
    blank("c", s.HR.at[1, 16:32])
    blank("h", s.A1.at[1:5, 0:32])
    blank("d", s.A1.at[0, 32:288])
    blank("c", s.A1.at[0, 0:32])
    blank("h", s.A2.at[1:3, 0:64])
    blank("d", s.A2.at[0, 64:320])
    blank("c", s.A2.at[0, 0:64])
    blank("d", s.D3D, back)
    blank("h", s.D3H, back)
    blank("c", s.D3C, back)
    blank("d", s.SD, back)
    blank("h", s.SH, back)
    blank("c", s.SC, back)

    w3_in = take("w3")
    for t in range(27):
        s.W3A[:, t * 64 : t * 64 + 64] = w3_in[t]
    s.W3A[:, 1728:1792] = jnp.zeros((pb, 64), BF)
    for c in range(nc):

        @pl.when(core == c)
        def _():
            s.W3[ha, :, c * half : c * half + half] = s.W3A[:, c * half : c * half + half]

    vol = take("vol")
    s.HS[...] = dot(take("last")[...], vol[...].reshape(512, 512)).astype(BF)
    if nd * nh > 1:
        pl.semaphore_wait(barrier, count)
    halos_v = [("vh", s.HS, s.HR.at[0]), ("vc", s.HS.at[16:32], s.HR.at[1, 16:32])]
    halos_v = halos_v + [("vd%d" % c, vol.at[c, 7], s.V0.at[c * 16 : c * 16 + 16]) for c in range(4)]
    for halo_v in halos_v:
        send(*halo_v)

    def taps_of(rows):
        return dot(rows, take("columns")[...]).astype(BF)

    for c in range(4):
        taps = taps_of(vol[c].reshape(128, 512))
        for d in range(8):
            for e in range(3):
                s.T1[1 + d, e * 64 + c * 16 : e * 64 + c * 16 + 16, :] = taps[
                    d * 16 : d * 16 + 16, e * 256 : e * 256 + 256
                ]

    w1 = take("w1")
    s.W1F[96:128, :] = jnp.zeros((32, 32), F32)
    for t in range(27):
        s.W1F[4 * t : 4 * t + 4, :] = w1[t].astype(F32)
    w1b = s.W1F[...].astype(BF)
    base = dot_tn(w1b, take("expand")[...])
    base_a, base_b = base[:, 0:576], base[:, 576:1152]
    row_h = lax.broadcasted_iota(jnp.int32, (32, 576), 1) & 15

    def tap_masks(j):
        return (row_h >> 1) == j, ((row_h & 1) == 1) & (((row_h + 1) >> 1) == j)

    for j in range(8):
        mask_a, mask_b = tap_masks(j)
        s.WT[j * 32 : j * 32 + 32, :] = jnp.where(mask_a, base_a, jnp.where(mask_b, base_b, 0.0)).astype(BF)
    edge = dot_tn(w1b, take("halo")[...]).astype(BF)
    for i in range(4):
        s.WH[i] = edge[:, i * 256 : i * 256 + 192]

    def first(i):
        z = dot(s.WT[...], s.T1[pl.ds(2 * i, 3)].reshape(576, 256))
        s.Z0[i] = z[0:32]
        act, slope = leaky_and_slope(z[32:256])
        s.A1[i + 1, 64:288, :] = act.astype(BF)
        s.S1[i, 32:256, :] = slope

    def second_taps(plane, lo, hi):
        x = s.A1[plane, lo * 32 : hi * 32, :]
        moved = dot(x[:, 128:256], take("shift2")[...]).astype(BF)
        for j in range(lo, hi):
            r = (j - lo) * 32
            s.T2[plane, j * 96 : j * 96 + 32, :] = moved[r : r + 32]
            s.T2[plane, j * 96 + 32 : j * 96 + 64, :] = x[r : r + 32, 0:128]
            s.T2[plane, j * 96 + 64 : j * 96 + 96, :] = x[r : r + 32, 128:256]

    first(3)
    a1 = s.A1
    halo_adi = ("adi", a1.at[4, 64:288], a1.at[0, 64:288])
    halo_adj = ("adj", a1.at[4, 32:64], a1.at[0, 32:64])
    halo_ac = ("ac", a1.at[4, 256:288], a1.at[0, 0:32])
    halo_ahi = ("ahi", a1.at[2:5, 256:288], a1.at[2:5, 0:32])
    halo_ahj = ("ahj", a1.at[1, 256:288], a1.at[1, 0:32])
    send(*halo_adi)
    send(*halo_ac)

    def loop_first(i, carry):
        first(i)
        return carry

    lax.fori_loop(1, 3, loop_first, 0)
    send(*halo_ahi)

    my_half = pl.ds(pl.multiple_of(core * half, 128), half)
    made_w3 = spread("h", "w3", lambda d, h: s.W3A.at[:, my_half], lambda k: s.W3.at[ha, :, my_half])
    for halo_v in halos_v:
        receive(*halo_v)
    edges = taps_of(jnp.concatenate([s.V0[...], s.HR[...].reshape(64, 512)], 0))
    for e in range(3):
        s.T1[0, e * 64 : e * 64 + 64, :] = edges[0:64, e * 256 : e * 256 + 256]
        s.TH[e * 64 : e * 64 + 64, :] = edges[64:128, e * 256 : e * 256 + 256]
    s.PH[...] = dot(s.WH[...].reshape(128, 192), s.TH[...]).reshape(4, 32, 256)

    def top_rows(lo, hi):
        act, slope = leaky_and_slope(s.Z0[lo:hi] + s.PH[lo:hi])
        a1[lo + 1 : hi + 1, 32:64, :] = act.astype(BF)
        s.S1[lo:hi, 0:32, :] = slope

    top_rows(1, 4)
    send(*halo_adj)
    first(0)
    send(*halo_ahj)
    top_rows(0, 1)
    y = dot(take("rows")[...], take("cot")[...].reshape(256, 64)).astype(BF)
    s.CS[...] = jnp.concatenate([y[0:128], y[128:256]], 1).reshape(nh, pb, 128)
    s.COT[ha] = s.CS[ha]
    made_cot = spread("h", "cot", lambda d, h: s.CS.at[h], lambda k: s.COT.at[ha])
    take("shift2")

    def loop_taps(i, carry):
        second_taps(i, 2, 9)
        return carry

    lax.fori_loop(2, 5, loop_taps, 0)
    w2 = take("w2")
    take("eye")
    for a in range(3):
        s.W2T[a] = dot_nt(s.i_eye[...], w2[a * 288 : a * 288 + 288, :]).astype(BF)

    second_taps(1, 1, 9)
    for plane in (2, 3, 4):
        second_taps(plane, 1, 2)

    def second(i, j):
        z = None
        for a in range(3):
            term = dot(s.W2T[a], s.T2[2 * i + a, j * 192 : j * 192 + 288, :])
            z = term if z is None else z + term
        act, slope = leaky_and_slope(z)
        s.A2[i + 1, 64 + 64 * j : 128 + 64 * j, :] = act.astype(BF)
        s.S2[i, 64 * j : 64 * j + 64, :] = slope
        if i == 0 or j == 0:
            s.SS[i, 64 * j : 64 * j + 64, :] = slope.astype(BF)

    for j in (1, 2, 3):
        second(1, j)
    a2 = s.A2
    halo_bd = ("bd", a2.at[2, 64:320], a2.at[0, 64:320])
    halo_bc = ("bc", a2.at[2, 256:320], a2.at[0, 0:64])
    halo_bh = ("bh", a2.at[1:3, 256:320], a2.at[1:3, 0:64])
    halos_b = [halo_bd, halo_bc, halo_bh]
    send(*halo_bc)
    for halo_a in (halo_adi, halo_adj, halo_ac, halo_ahi, halo_ahj):
        receive(*halo_a)
    second_taps(0, 6, 9)
    second(0, 3)
    send(*halo_bh)
    for plane in (2, 3, 4):
        second_taps(plane, 0, 1)
    second(1, 0)
    send(*halo_bd)
    second_taps(0, 0, 6)
    second_taps(1, 0, 1)
    for j in (2, 1, 0):
        second(0, j)
    s2 = s.S2
    halos_s = [
        ("sd", s.SS.at[0], s.SD),
        ("sh", s.SS.at[0:2, 0:64], s.SH),
        ("sc", s.SS.at[0, 0:64], s.SC),
    ]
    for halo_s in halos_s:
        send(*halo_s, back)

    gather(made_w3)
    if nc == 2:
        other = pl.ds(pl.multiple_of((1 - core) * half, 128), half)
        to_partner("w3c", s.W3.at[:, :, my_half], s.W3.at[:, :, my_half])
        w3_other = copy(
            s.W3.at[:, :, other], s.W3.at[:, :, other], plan.sem["w3c"], (dev + 1 - 2 * core, ha)
        )

    def third_taps(blocks):
        x = [
            jnp.concatenate([a2[plane, b * 64 : b * 64 + 64, :], a2[plane, b * 64 + 128 : b * 64 + 192, :]], 1)
            for plane, b in blocks
        ]
        y = dot(jnp.concatenate(x, 0), take("taps3")[...]).astype(BF)
        for k, (plane, b) in enumerate(blocks):
            for e in range(3):
                s.T3[plane, b * 192 + e * 64 : b * 192 + e * 64 + 64, :] = y[
                    64 * k : 64 * k + 64, e * 128 : e * 128 + 128
                ]

    third_taps([(1, 1), (1, 2), (2, 1), (2, 2)])
    if nc == 2:
        w3_other.wait_recv()
    s.W3T[...] = s.W3[...].reshape(128, 1792).T
    for halo_b in halos_b:
        receive(*halo_b)
    gather(made_cot)
    third_taps([(0, 0), (0, 1), (0, 2), (1, 0), (2, 0)])
    t3 = s.T3[...].reshape(1728, 128)
    act, slope = leaky_and_slope(dot(s.W3[...].reshape(128, 1792)[:, 0:1728], t3))
    delta3 = (s.COT[...].reshape(128, 128).astype(F32) * slope).astype(BF)
    s.D3[...] = delta3
    s.OS[...] = act.astype(BF).reshape(nh, pb, 128)
    s.D3P[...] = jnp.concatenate([delta3[0:64, 0:64], delta3[64:128, 0:64]], 1)
    halos_3 = [("3d", s.D3, s.D3D), ("3h", s.D3P, s.D3H), ("3c", s.D3P, s.D3C)]
    for halo_3 in halos_3:
        send(*halo_3, back)

    lane3 = lax.broadcasted_iota(jnp.int32, (64, 128), 1)

    def third_back(parts):
        made = []
        for a, b, d in parts:
            r = a * 576 + b * 192
            x = dot(s.W3T[r : r + 192, :], d)
            even = x[64:128]
            odd = x[128:192] + jnp.where((lane3 & 63) == 63, 0.0, pltpu.roll(x[0:64], 127, 1))
            first_height = jnp.where(lane3 < 64, even, pltpu.roll(odd, 64, 1))
            made.append((first_height, jnp.where(lane3 < 64, pltpu.roll(even, 64, 1), odd)))
        return made

    b2 = s.B2
    one1, one2, two1, two2 = third_back([(1, 1, delta3), (1, 2, delta3), (2, 1, delta3), (2, 2, delta3)])
    for i, tap1, tap2 in ((0, one1, one2), (1, two1, two2)):
        b2[i, 0:64, :] = tap1[0]
        b2[i, 64:128, :] = tap2[0]
        b2[i, 128:192, :] = tap1[1]
        b2[i, 192:256, :] = tap2[1]
    g3 = dot_nt(delta3, t3)
    s.G3F[:, :, 1728:1792] = jnp.zeros((nh, pb, 64), F32)
    s.G3S[:, :, 1728:1792] = jnp.zeros((nh, pb, 64), BF)
    s.G3F[:, :, 0:1728] = g3.reshape(nh, pb, 1728)
    s.G3S[:, :, 0:1728] = g3.astype(BF).reshape(nh, pb, 1728)
    if nc == 2:
        g3c = to_partner("g3c", s.G3S.at[:, :, other], s.R3C)

    for c in range(nc):

        @pl.when(core == c)
        def _():
            total = s.G3F[:, :, c * half : c * half + half]
            if nc == 2:
                g3c.wait_recv()
                total = total + s.R3C[...].astype(F32)
            s.G3T[...] = total
            s.G3U[...] = total.astype(BF)

    made_g3h = spread("h", "g3h", lambda d, h: s.G3U.at[h], lambda k: s.R3H.at[k])

    dl2 = s.DL2
    receive(*halos_3[1], back)
    for halo_s in halos_s:
        receive(*halo_s, back)
    next_h = jnp.concatenate([s.D3H[:, 0:64], s.D3H[:, 64:128]], 0)
    own = jnp.concatenate([delta3[:, 64:128], next_h], 1)
    one0, two0, side1, side2 = third_back([(1, 0, own), (2, 0, own), (1, 1, own), (2, 1, own)])
    b2[0, 64:128, :] += one0[0]
    b2[0, 192:256, :] += one0[1]
    b2[0, 256:320, :] = side1[1]
    b2[1, 64:128, :] += two0[0]
    b2[1, 192:256, :] += two0[1]
    b2[1, 256:320, :] = side2[1]
    dl2[0, 0:256, :] = (b2[0, 0:256, :] * s2[0]).astype(BF)
    dl2[0, 256:320, :] = (b2[0, 256:320, :] * s.SH[0].astype(F32)).astype(BF)

    none = jnp.zeros((64, 256), BF)

    def second_grad(i):
        low = high = None
        for j in (0, 2):
            x = jnp.concatenate([dl2[i, 64 * (j + t) : 64 * (j + t) + 64, :] for t in (0, 1)], 1)
            t2 = jnp.concatenate(
                [s.T2[2 * i : 2 * i + 3, 192 * (j + t) : 192 * (j + t) + 288, :].reshape(864, 128) for t in (0, 1)], 1
            )
            term = dot_nt(t2[0:512], jnp.concatenate([x, none], 0))
            low = term if low is None else low + term
            term = dot_nt(t2[512:864], jnp.concatenate([none, x], 0))
            high = term if high is None else high + term
        return jnp.concatenate([low[0:352] + high, low[352:512]], 0).reshape(nc, nh, plan.r2, 128)

    lane = lax.broadcasted_iota(jnp.int32, (32, 128), 1)

    def second_back(plane, pairs):
        for j in range(5):
            y = None
            for a, i in pairs:
                term = dot(w2[a * 288 : a * 288 + 288, :], dl2[i, j * 64 : j * 64 + 64, :])
                y = term if y is None else y + term
            s.Y[j] = y
        for k in range(8):
            j = (k + 1) // 2
            d = s.Y[j, 0:96, :] + s.Y[j - 1, 192:288, :] if k % 2 else s.Y[j, 96:192, :]
            moved = jnp.where(lane < 64, pltpu.roll(d[0:32], 64, 1), pltpu.roll(d[0:32], 63, 1))
            moved = jnp.where(lane == 127, 0.0, moved)
            s.B1[plane, 32 * k : 32 * k + 32, 0:128] = d[32:64]
            s.B1[plane, 32 * k : 32 * k + 32, 128:256] = d[64:96] + moved

    s.G2F[...] = second_grad(0)
    second_back(0, [(1, 0)])
    receive(*halos_3[0], back)
    receive(*halos_3[2], back)
    next_c = jnp.concatenate([s.D3C[:, 0:64], s.D3C[:, 64:128]], 0)
    deep = s.D3D[...]
    deep_next = jnp.concatenate([deep[:, 64:128], next_c], 1)
    zero0, zero1, zero2, side0 = third_back(
        [(0, 0, deep_next), (0, 1, deep), (0, 2, deep), (0, 1, deep_next)]
    )
    b2[1, 0:64, :] += zero1[0]
    b2[1, 64:128, :] += zero0[0] + zero2[0]
    b2[1, 128:192, :] += zero1[1]
    b2[1, 192:256, :] += zero0[1] + zero2[1]
    b2[1, 256:320, :] += side0[1]
    dl2[1, 0:256, :] = (b2[1, 0:256, :] * s2[1]).astype(BF)
    g2 = s.G2F[...] + second_grad(1)
    s.G2F[...] = g2
    s.G2S[...] = g2.astype(BF)
    made_g2h = spread("a", "g2h", lambda d, h: s.G2S.at[d & (nc - 1), h], lambda k: s.R2H.at[k])
    made_out = spread("h", "out", lambda d, h: s.OS.at[h], lambda k: s.OR.at[ha])
    s.OR[ha] = s.OS[ha]
    deep0, deep1, deep2, side3 = third_back(
        [(1, 0, deep_next), (1, 1, deep), (1, 2, deep), (1, 1, deep_next)]
    )
    b2[2, 0:64, :] = deep1[0]
    b2[2, 64:128, :] = deep0[0] + deep2[0]
    b2[2, 128:192, :] = deep1[1]
    b2[2, 192:256, :] = deep0[1] + deep2[1]
    b2[2, 256:320, :] = side3[1]
    dl2[2, 0:256, :] = (b2[2, 0:256, :] * s.SD[...].astype(F32)).astype(BF)
    dl2[1, 256:320, :] = (b2[1, 256:320, :] * s.SH[1].astype(F32)).astype(BF)
    dl2[2, 256:320, :] = (b2[2, 256:320, :] * s.SC[...].astype(F32)).astype(BF)

    second_back(1, [(2, 0), (0, 1)])
    second_back(2, [(1, 1)])
    second_back(3, [(2, 1), (0, 2)])

    s.G1A[...] = jnp.zeros((256, 576), F32)

    def loop_back(i, carry):
        d = (s.B1[i] * s.S1[i]).astype(BF)
        s.DL1[i] = d
        s.G1A[...] += dot_nt(d, s.T1[pl.ds(2 * i, 3)].reshape(576, 256))
        return carry

    lax.fori_loop(0, 4, loop_back, 0)
    def sum_parts(total, received, size):
        for k in range(1, size):
            total = total + received[k].astype(F32)
        return total

    gh = dot_nt(s.DL1[:, 0:32, :].reshape(128, 256), s.TH[...])
    sum_a = jnp.zeros((32, 576), F32)
    sum_b = jnp.zeros((32, 576), F32)
    for j in range(8):
        mask_a, mask_b = tap_masks(j)
        g = s.G1A[32 * j : 32 * j + 32, :]
        sum_a = sum_a + jnp.where(mask_a, g, 0.0)
        sum_b = sum_b + jnp.where(mask_b, g, 0.0)
    g1 = dot_nt(split_rows(sum_a), s.i_expand[:, 0:576])
    g1 = g1 + dot_nt(split_rows(sum_b), s.i_expand[:, 576:1152])
    for i in range(4):
        g1 = g1 + dot_nt(split_rows(gh[32 * i : 32 * i + 32]), s.i_halo[:, i * 256 : i * 256 + 192])
    g1 = g1[0:32] + g1[32:64]
    s.G1S[...] = g1.astype(BF)
    made_g1h = spread("a", "g1h", lambda d, h: s.G1S, lambda k: s.R1H.at[k])

    gather(made_g3h)
    total = sum_parts(s.G3T[ha], s.R3H, nh)
    s.P3F[...] = total
    s.P3S[...] = total.astype(BF)
    made_g3d = spread("z", "g3d", lambda d, h: s.P3S, lambda k: s.R3D.at[k])
    gather(made_g2h)
    g2 = sum_parts(s.G2F[core, ha], s.R2H, nh * nc)
    s.G2D[...] = g2.astype(BF)
    made_g2d = spread("z", "g2d", lambda d, h: s.G2D, lambda k: s.R2D.at[k])
    gather(made_out)
    x = s.OR[...].reshape(128, 128)
    x = jnp.concatenate([x[:, 0:64], x[:, 64:128]], 0)
    o3[...] = dot_tn(s.i_rows[...], x).astype(BF).reshape(pb, 2 * nh, 64)
    gather(made_g1h)
    g1 = sum_parts(g1, s.R1H, nh * nc)
    s.G1D[...] = g1.astype(BF)
    made_g1d = spread("z", "g1d", lambda d, h: s.G1D, lambda k: s.R1D.at[k])
    gather(made_g2d)
    g2 = sum_parts(g2, s.R2D, nz)
    s.F2[...] = g2.astype(BF)
    s.F2H[core, ha] = g2.astype(BF)
    made_g2z = spread("a", "g2z", lambda d, h: s.F2, lambda k: s.F2H.at[core, ha])
    gather(made_g3d)
    s.F3[core] = sum_parts(s.P3F[...], s.R3D, nz)
    if nc == 2:
        to_partner("g3p", s.F3.at[core], s.F3.at[core])
        g3p = copy(s.F3.at[1 - core], s.F3.at[1 - core], plan.sem["g3p"], (dev + 1 - 2 * core, ha))
    gather(made_g1d)
    x = (sum_parts(g1, s.R1D, nz) * scales[0]).T
    for t in range(27):
        g1o[t] = x[4 * t : 4 * t + 4]
    if nc == 2:
        g3p.wait_recv()
    for t in range(27):
        c, r = divmod(64 * t, half)
        g3o[t] = s.F3[c, :, r : r + 64] * scales[2]
    gather(made_g2z)
    x = s.F2H[...].reshape(512, 128).astype(F32) * scales[1]
    g2o[0:512, :] = x[:, 0:64]
    g2o[512:864, :] = x[0:352, 64:128]
    for ok, c in pending:
        if ok is None:
            c.wait_send()
        else:
            pl.when(ok)(c.wait_send)


def finish(*refs):
    copies = [pltpu.make_async_copy(refs[k], refs[4 + k], refs[8].at[k]) for k in range(4)]
    for c in copies:
        c.start()
    for c in copies:
        c.wait()


def local(nd, nh, volume, w_first, w_second, w_third, cotangent):
    plan = Plan(nd, nh)
    pb = plan.pb
    cells = volume.shape[1] * nd * volume.shape[2] * nh * volume.shape[3]
    scales = tuple(1.0 / math.sqrt(cells // 8**n) for n in (1, 2, 3))
    inputs = dict(
        vol=volume,
        w1=w_first.reshape(27, 4, 32),
        w2=w_second.reshape(864, 64),
        w3=jnp.transpose(w_third.reshape(27, 64, pb), (0, 2, 1)),
        cot=cotangent.reshape(pb, 2 * nh, 64),
    )
    inputs.update(zip(INPUTS[5:], constants(nh)))
    scratch = plan.scratch()
    for name in INPUTS:
        scratch["i_" + name] = pltpu.VMEM(inputs[name].shape, BF)
    names = list(scratch)
    vmem, hbm = pl.BlockSpec(memory_space=pltpu.VMEM), pl.BlockSpec(memory_space=pltpu.HBM)
    shapes = [((pb, 2 * nh, 64), BF), ((27, 4, 32), F32), ((864, 64), F32), ((27, pb, 64), F32)]
    made = pl.pallas_call(
        functools.partial(kernel, plan, names, scales),
        out_shape=[pltpu.VMEM(*x) for x in shapes],
        in_specs=[hbm] * len(INPUTS),
        out_specs=[vmem] * 4,
        scratch_shapes=[scratch[n] for n in names],
        compiler_params=pltpu.CompilerParams(
            collective_id=0 if nd * nh > 1 else None, has_side_effects=True, vmem_limit_bytes=48 * 2**20
        ),
        name="step",
    )(*[pltpu.with_memory_space_constraint(inputs[n], pltpu.HBM) for n in INPUTS])
    out3, g1, g2, g3 = pl.pallas_call(
        finish,
        out_shape=[jax.ShapeDtypeStruct(*x) for x in shapes],
        in_specs=[vmem] * 4,
        out_specs=[hbm] * 4,
        scratch_shapes=[pltpu.SemaphoreType.DMA((4,))],
        compiler_params=pltpu.CompilerParams(vmem_limit_bytes=48 * 2**20),
        name="finish",
    )(*made)
    return (
        out3.reshape(pb, 1, 2 * nh, 64),
        g1.reshape(3, 3, 3, 4, 32),
        g2.reshape(3, 3, 3, 32, 64),
        jnp.transpose(g3, (0, 2, 1)).reshape(3, 3, 3, 64, pb),
    )


def solution(mesh):
    placed = (
        P(None, "dev", "ha", None),
        P(),
        P(),
        P(None, None, None, None, "ha"),
        P("ha", "dev", None, None),
    )
    return jax.shard_map(
        functools.partial(local, mesh.shape["dev"], mesh.shape["ha"]),
        mesh=mesh,
        in_specs=placed,
        out_specs=(P("ha", "dev", None, None), P(), P(), P(None, None, None, None, "ha")),
        check_vma=False,
    )
```

```python
import functools
import math
import types

import jax
import jax.numpy as jnp
import numpy as np
from jax import lax
from jax.experimental import pallas as pl
from jax.experimental.pallas import tpu as pltpu
from jax.sharding import PartitionSpec as P

MESH = pl.DeviceIdType.MESH
BF = jnp.bfloat16
F32 = jnp.float32


def dot(a, b):
    return lax.dot_general(a, b, (((1,), (0,)), ((), ())), preferred_element_type=F32)


def dot_nt(a, b):
    return lax.dot_general(a, b, (((1,), (1,)), ((), ())), preferred_element_type=F32)


def dot_tn(a, b):
    return lax.dot_general(a, b, (((0,), (0,)), ((), ())), preferred_element_type=F32)


def split_rows(x):
    high = x.astype(BF)
    low = (x - high.astype(F32)).astype(BF)
    return jnp.concatenate([high, low], 0)


def leaky_and_slope(z):
    soft = jnp.log(1.0 + jnp.exp(-4.0 * jnp.abs(z)))
    act = jnp.maximum(z, 0.3 * z) + 0.175 * soft
    return act, 0.65 + 0.35 * jnp.tanh(2.0 * z)


ORDER2 = np.concatenate([np.arange(0, 128, 2), np.arange(1, 128, 2)])
ORDER1 = np.concatenate([2 * ORDER2, 2 * ORDER2 + 1])


def constants(nh):
    expand = np.zeros((128, 1152), np.float32)
    for a in range(3):
        for e in range(3):
            for c in range(4):
                for h in range(16):
                    col = a * 192 + e * 64 + c * 16 + h
                    row = lambda b: ((a * 3 + b) * 3 + e) * 4 + c
                    expand[row(1 + h % 2), col] = 1
                    if h % 2:
                        expand[row(0), 576 + col] = 1
    halo = np.zeros((128, 1024), np.float32)
    for i in range(4):
        for a in range(3):
            d = 2 * i - 1 + a
            s, plane = (0, d) if d >= 0 else (1, 7)
            for e in range(3):
                for c in range(4):
                    row = (a * 9 + e) * 4 + c
                    halo[row, i * 256 + s * 96 + e * 32 + plane * 4 + c] = 1
    columns = np.zeros((512, 768), np.float32)
    for e in range(3):
        for p in range(256):
            w = 2 * ORDER1[p] - 1 + e
            if w >= 0:
                columns[w, e * 256 + p] = 1
    where2 = {int(l): q for q, l in enumerate(ORDER2)}
    shift2 = np.zeros((128, 128), np.float32)
    for p in range(128):
        if ORDER2[p] >= 1:
            shift2[where2[int(ORDER2[p]) - 1], p] = 1
    taps3 = np.zeros((256, 384), np.float32)
    for jj in range(2):
        for e in range(3):
            for l in range(64):
                w = 2 * l - 1 + e
                if w >= 0:
                    taps3[jj * 128 + where2[w], e * 128 + jj * 64 + l] = 1
    last = np.zeros((32, 512), np.float32)
    for d in range(8):
        for c in range(4):
            last[d * 4 + c, c * 128 + d * 16 + 15] = 1
    pb = 128 // nh
    rows = np.zeros((256, 256), np.float32)
    for jj in range(2):
        for q in range(nh):
            for ch in range(pb):
                rows[(jj * nh + q) * pb + ch, ch * 2 * nh + 2 * q + jj] = 1
    made = (expand, halo, columns, shift2, taps3, last, np.eye(64), rows)
    return [jnp.asarray(x, BF) for x in made]


class Plan:
    def __init__(self, nd, nh):
        self.nd, self.nh = nd, nh
        self.nc = 2 if nd > 1 else 1
        self.nz = nd // self.nc
        self.pb = 128 // nh
        self.mb = 64 // nh
        self.r2 = 512 // (self.nc * nh)
        self.half = 1792 // self.nc
        self.sem = {}
        count = 0
        names = ["vd0", "vd1", "vd2", "vd3", "vh", "vc", "adi", "adj", "ahi", "ahj", "ac", "bd", "bh", "bc", "3d", "3h", "3c", "sd", "sh", "sc"]
        for name in names + ["w3c", "g3c", "g3p"]:
            self.sem[name] = count
            count += 1
        for name in ["w3", "cot", "out", "g3h"]:
            self.sem[name] = count
            count += nh - 1
        for name in ["g2h", "g2z", "g1h"]:
            self.sem[name] = count
            count += nh * self.nc - 1
        for name in ["g3d", "g2d", "g1d"]:
            self.sem[name] = count
            count += self.nz - 1
        self.count = count

    def scratch(self):
        nd, nh, nc, pb, mb = self.nd, self.nh, self.nc, self.pb, self.mb
        v = pltpu.VMEM
        return dict(
            V0=v((64, 512), BF),
            HS=v((32, 512), BF),
            HR=v((2, 32, 512), BF),
            T1=v((9, 192, 256), BF),
            TH=v((192, 256), BF),
            W1F=v((128, 32), F32),
            WT=v((256, 576), BF),
            WH=v((4, 32, 96), BF),
            WC=v((32, 96), BF),
            PH=v((4, 32, 256), F32),
            Z0=v((4, 32, 256), F32),
            A1=v((5, 288, 256), BF),
            S1=v((4, 256, 256), F32),
            T2=v((5, 864, 128), BF),
            W2T=v((3, 64, 288), BF),
            A2=v((3, 320, 128), BF),
            S2=v((2, 256, 128), F32),
            T3=v((3, 576, 128), BF),
            W3A=v((pb, 1792), BF),
            W3=v((nh, pb, 1792), BF),
            W3T=v((1792, 128), BF),
            CS=v((nh, pb, 128), BF),
            COT=v((nh, pb, 128), BF),
            OS=v((nh, pb, 128), BF),
            OR=v((nh, pb, 128), BF),
            D3=v((128, 128), BF),
            D3D=v((128, 128), BF),
            D3P=v((64, 128), BF),
            D3H=v((64, 128), BF),
            D3C=v((64, 128), BF),
            SS=v((2, 256, 128), BF),
            SD=v((256, 128), BF),
            SH=v((2, 64, 128), BF),
            SC=v((64, 128), BF),
            B2=v((3, 320, 128), F32),
            DL2=v((3, 320, 128), BF),
            Y=v((5, 288, 128), F32),
            B1=v((4, 256, 256), F32),
            DL1=v((4, 256, 256), BF),
            G3F=v((nh, pb, 1792), F32),
            G3S=v((nh, pb, 1792), BF),
            R3C=v((nh, pb, self.half), BF),
            G3T=v((nh, pb, self.half), F32),
            G3U=v((nh, pb, self.half), BF),
            R3H=v((nh, pb, self.half), BF),
            P3S=v((pb, self.half), BF),
            R3D=v((self.nz, pb, self.half), BF),
            P3F=v((pb, self.half), F32),
            F3=v((nc, pb, self.half), F32),
            G2F=v((nc, nh, self.r2, 128), F32),
            G2S=v((nc, nh, self.r2, 128), BF),
            R2H=v((nc * nh, self.r2, 128), BF),
            G2D=v((self.r2, 128), BF),
            R2D=v((self.nz, self.r2, 128), BF),
            F2=v((self.r2, 128), BF),
            F2H=v((nc, nh, self.r2, 128), BF),
            G1A=v((256, 576), F32),
            G1S=v((32, 128), BF),
            R1H=v((nc * nh, 32, 128), BF),
            G1D=v((32, 128), BF),
            R1D=v((self.nz, 32, 128), BF),
            ss=pltpu.SemaphoreType.DMA((self.count,)),
            rs=pltpu.SemaphoreType.DMA((self.count,)),
            ls=pltpu.SemaphoreType.DMA((16,)),
        )


INPUTS = ["vol", "w1", "w2", "w3", "cot", "expand", "halo", "columns", "shift2", "taps3", "last", "eye", "rows"]


def kernel(plan, names, scales, *refs):
    nd, nh, nc, nz, pb, mb, half = plan.nd, plan.nh, plan.nc, plan.nz, plan.pb, plan.mb, plan.half
    inputs = dict(zip(INPUTS, refs[: len(INPUTS)]))
    o3, g1o, g2o, g3o = refs[len(INPUTS) : len(INPUTS) + 4]
    s = types.SimpleNamespace(**dict(zip(names, refs[len(INPUTS) + 4 :])))
    ss, rs = s.ss, s.rs
    dev, ha = lax.axis_index("dev"), lax.axis_index("ha")
    core, zy = (dev & 1, dev >> 1) if nc == 2 else (dev * 0, dev)
    up_d, up_h = dev < nd - 1, ha < nh - 1
    lo_d, lo_h = dev > 0, ha > 0
    up_c, lo_c = up_d & up_h, lo_d & lo_h

    order = ["vol", "w3", "last", "columns", "w1", "expand", "halo", "cot", "rows", "w2", "eye", "shift2", "taps3"]
    copies = {}
    for k, name in enumerate(order):
        copies[name] = pltpu.make_async_copy(inputs[name], getattr(s, "i_" + name), s.ls.at[k])
        copies[name].start()
    arrived = set()

    def take(name):
        if name not in arrived:
            arrived.add(name)
            copies[name].wait()
        return getattr(s, "i_" + name)

    sizes = {"h": nh, "a": nh * nc, "z": nz}

    def wrap(x, n):
        return x & (n - 1) if n & (n - 1) == 0 else lax.rem(x, n)

    peers = {"h": [(dev, wrap(ha + k, nh)) for k in range(nh)]}
    peers["z"] = [(wrap(zy + k, nz) * nc + core, ha) for k in range(nz)]
    peers["a"] = []
    for k in range(nh * nc):
        index = wrap(ha * nc + core + k, nh * nc)
        peers["a"].append((zy * nc + wrap(index, nc), index // nc if nc == 1 else index >> 1))

    def peer_of(group, k):
        return peers[group][k]

    if nd * nh > 1:
        barrier = pltpu.get_barrier_semaphore()
        count = 0
        for group in ("a", "z"):
            for k in range(1, sizes[group]):
                pl.semaphore_signal(barrier, inc=1, device_id=peer_of(group, k), device_id_type=MESH)
                count += 1
        last_core, first_core = core == nc - 1, core == 0
        for ok, target in (
            (up_d & last_core, (dev + 1, ha)),
            (lo_d & first_core, (dev - 1, ha)),
            (up_c & last_core, (dev + 1, ha + 1)),
            (lo_c & first_core, (dev - 1, ha - 1)),
        ):

            @pl.when(ok)
            def _():
                pl.semaphore_signal(barrier, inc=1, device_id=target, device_id_type=MESH)

            count = count + ok.astype(jnp.int32)

    def copy(src, dst, k, target):
        return pltpu.make_async_remote_copy(
            src_ref=src, dst_ref=dst, send_sem=ss.at[k], recv_sem=rs.at[k], device_id=target, device_id_type=MESH
        )

    routes = {
        "d": (up_d, lo_d, nd > 1, (jnp.minimum(dev + 1, nd - 1), ha)),
        "h": (up_h, lo_h, nh > 1, (dev, jnp.minimum(ha + 1, nh - 1))),
        "c": (up_c, lo_c, nd > 1 and nh > 1, (jnp.minimum(dev + 1, nd - 1), jnp.minimum(ha + 1, nh - 1))),
    }
    back = {
        "d": (lo_d, up_d, nd > 1, (jnp.maximum(dev - 1, 0), ha)),
        "h": (lo_h, up_h, nh > 1, (dev, jnp.maximum(ha - 1, 0))),
        "c": (lo_c, up_c, nd > 1 and nh > 1, (jnp.maximum(dev - 1, 0), jnp.maximum(ha - 1, 0))),
    }
    pending = []

    def finish_sends(copies):
        for ok, c in copies:
            if ok is None:
                c.wait_send()
            else:
                pl.when(ok)(c.wait_send)

    def send(name, src, dst, table=routes):
        can_send, can_receive, exists, target = table[name[1]]
        if not exists:
            return
        c = copy(src, dst, plan.sem[name], target)
        pl.when(can_send)(c.start)
        pending.append((can_send, c))

    def receive(name, src, dst, table=routes):
        can_send, can_receive, exists, target = table[name[1]]
        if not exists:
            return
        c = copy(src, dst, plan.sem[name], target)
        pl.when(can_receive)(c.wait_recv)

    def blank(kind, ref, table=routes):
        can_send, can_receive, exists, target = table[kind]

        @pl.when(jnp.logical_not(can_receive))
        def _():
            ref[...] = jnp.zeros(ref.shape, ref.dtype)

    def spread(group, name, src_of, dst, valid_send=None, part=(1, 99)):
        made = []
        for k in range(part[0], min(part[1], sizes[group])):
            target = peer_of(group, k)
            c = copy(src_of(*target), dst(k), plan.sem[name] + k - 1, target)
            ok = None if valid_send is None else valid_send(target[0])
            if ok is None:
                c.start()
            else:
                pl.when(ok)(c.start)
            pending.append((ok, c))
            made.append((k, c))
        return made

    def gather(made, valid_receive=None):
        for k, c in made:
            if valid_receive is None:
                c.wait_recv()
            else:
                pl.when(valid_receive(lax.rem(zy + nz - k, nz)))(c.wait_recv)

    def to_partner(name, src, dst):
        c = copy(src, dst, plan.sem[name], (dev + 1 - 2 * core, ha))
        c.start()
        pending.append((None, c))
        return c

    blank("d", s.V0)
    blank("h", s.HR.at[0])
    s.HR[1, 0:16, :] = jnp.zeros((16, 512), BF)
    blank("c", s.HR.at[1, 16:32])
    blank("h", s.A1.at[1:5, 0:32])
    blank("d", s.A1.at[0, 32:288])
    blank("c", s.A1.at[0, 0:32])
    blank("h", s.A2.at[1:3, 0:64])
    blank("d", s.A2.at[0, 64:320])
    blank("c", s.A2.at[0, 0:64])
    blank("d", s.D3D, back)
    blank("h", s.D3H, back)
    blank("c", s.D3C, back)
    blank("d", s.SD, back)
    blank("h", s.SH, back)
    blank("c", s.SC, back)

    w3_in = take("w3")
    for t in range(27):
        s.W3A[:, t * 64 : t * 64 + 64] = w3_in[t]
    s.W3A[:, 1728:1792] = jnp.zeros((pb, 64), BF)
    for c in range(nc):

        @pl.when(core == c)
        def _():
            s.W3[ha, :, c * half : c * half + half] = s.W3A[:, c * half : c * half + half]

    vol = take("vol")
    s.HS[...] = dot(take("last")[...], vol[...].reshape(512, 512)).astype(BF)
    if nd * nh > 1:
        pl.semaphore_wait(barrier, count)
    halos_v = [("vh", s.HS, s.HR.at[0]), ("vc", s.HS.at[16:32], s.HR.at[1, 16:32])]
    halos_v = halos_v + [("vd%d" % c, vol.at[c, 7], s.V0.at[c * 16 : c * 16 + 16]) for c in range(4)]
    for halo_v in halos_v:
        send(*halo_v)

    def taps_of(rows):
        return dot(rows, take("columns")[...]).astype(BF)

    for c in range(4):
        taps = taps_of(vol[c].reshape(128, 512))
        for d in range(8):
            for e in range(3):
                s.T1[1 + d, e * 64 + c * 16 : e * 64 + c * 16 + 16, :] = taps[
                    d * 16 : d * 16 + 16, e * 256 : e * 256 + 256
                ]

    w1 = take("w1")
    s.W1F[96:128, :] = jnp.zeros((32, 32), F32)
    for t in range(27):
        s.W1F[4 * t : 4 * t + 4, :] = w1[t].astype(F32)
    w1b = s.W1F[...].astype(BF)
    base = dot_tn(w1b, take("expand")[...])
    base_a, base_b = base[:, 0:576], base[:, 576:1152]
    row_h = lax.broadcasted_iota(jnp.int32, (32, 576), 1) & 15

    def tap_masks(j):
        return (row_h >> 1) == j, ((row_h & 1) == 1) & (((row_h + 1) >> 1) == j)

    for j in range(8):
        mask_a, mask_b = tap_masks(j)
        s.WT[j * 32 : j * 32 + 32, :] = jnp.where(mask_a, base_a, jnp.where(mask_b, base_b, 0.0)).astype(BF)
    edge = dot_tn(w1b, take("halo")[...]).astype(BF)
    for i in range(4):
        s.WH[i] = edge[:, i * 256 : i * 256 + 96]
    s.WC[...] = edge[:, 96:192]

    def first(i):
        z = dot(s.WT[...], s.T1[pl.ds(2 * i, 3)].reshape(576, 256))
        s.Z0[i] = z[0:32]
        act, slope = leaky_and_slope(z[32:256])
        s.A1[i + 1, 64:288, :] = act.astype(BF)
        s.S1[i, 32:256, :] = slope

    def second_taps(plane, lo, hi):
        x = s.A1[plane, lo * 32 : hi * 32, :]
        moved = dot(x[:, 128:256], take("shift2")[...]).astype(BF)
        for j in range(lo, hi):
            r = (j - lo) * 32
            s.T2[plane, j * 96 : j * 96 + 32, :] = moved[r : r + 32]
            s.T2[plane, j * 96 + 32 : j * 96 + 64, :] = x[r : r + 32, 0:128]
            s.T2[plane, j * 96 + 64 : j * 96 + 96, :] = x[r : r + 32, 128:256]

    first(3)
    a1 = s.A1
    halo_adi = ("adi", a1.at[4, 64:288], a1.at[0, 64:288])
    halo_adj = ("adj", a1.at[4, 32:64], a1.at[0, 32:64])
    halo_ac = ("ac", a1.at[4, 256:288], a1.at[0, 0:32])
    halo_ahi = ("ahi", a1.at[2:5, 256:288], a1.at[2:5, 0:32])
    halo_ahj = ("ahj", a1.at[1, 256:288], a1.at[1, 0:32])
    send(*halo_adi)
    send(*halo_ac)

    def loop_first(i, carry):
        first(i)
        return carry

    lax.fori_loop(1, 3, loop_first, 0)
    send(*halo_ahi)

    my_half = pl.ds(pl.multiple_of(core * half, 128), half)
    made_w3 = spread(
        "h", "w3", lambda d, h: s.W3A.at[:, my_half], lambda k: s.W3.at[ha, :, my_half], part=(1, 4)
    )
    halo_vc = halos_v.pop(1)
    for halo_v in halos_v:
        receive(*halo_v)
    edges = taps_of(jnp.concatenate([s.V0[...], s.HR[0]], 0))
    for e in range(3):
        s.T1[0, e * 64 : e * 64 + 64, :] = edges[0:64, e * 256 : e * 256 + 256]
        s.TH[e * 32 : e * 32 + 32, :] = edges[64:96, e * 256 : e * 256 + 256]
    s.PH[...] = dot(s.WH[...].reshape(128, 96), s.TH[0:96, :]).reshape(4, 32, 256)

    def top_rows(lo, hi):
        act, slope = leaky_and_slope(s.Z0[lo:hi] + s.PH[lo:hi])
        a1[lo + 1 : hi + 1, 32:64, :] = act.astype(BF)
        s.S1[lo:hi, 0:32, :] = slope

    top_rows(1, 4)
    send(*halo_adj)
    first(0)
    send(*halo_ahj)
    made_w3 += spread(
        "h", "w3", lambda d, h: s.W3A.at[:, my_half], lambda k: s.W3.at[ha, :, my_half], part=(4, 99)
    )
    y = dot(take("rows")[...], take("cot")[...].reshape(256, 64)).astype(BF)
    s.CS[...] = jnp.concatenate([y[0:128], y[128:256]], 1).reshape(nh, pb, 128)
    s.COT[ha] = s.CS[ha]
    made_cot = spread("h", "cot", lambda d, h: s.CS.at[h], lambda k: s.COT.at[ha])
    take("shift2")

    def loop_taps(i, carry):
        second_taps(i, 2, 9)
        return carry

    lax.fori_loop(2, 5, loop_taps, 0)
    w2 = take("w2")
    take("eye")
    for a in range(3):
        s.W2T[a] = dot_nt(s.i_eye[...], w2[a * 288 : a * 288 + 288, :]).astype(BF)

    receive(*halo_vc)
    edges = taps_of(s.HR[1])
    for e in range(3):
        s.TH[96 + e * 32 : 128 + e * 32, :] = edges[:, e * 256 : e * 256 + 256]
    s.PH[0] += dot(s.WC[...], s.TH[96:192, :])
    top_rows(0, 1)
    second_taps(1, 1, 9)
    for plane in (2, 3, 4):
        second_taps(plane, 1, 2)

    def second(i, j):
        z = None
        for a in range(3):
            term = dot(s.W2T[a], s.T2[2 * i + a, j * 192 : j * 192 + 288, :])
            z = term if z is None else z + term
        act, slope = leaky_and_slope(z)
        s.A2[i + 1, 64 + 64 * j : 128 + 64 * j, :] = act.astype(BF)
        s.S2[i, 64 * j : 64 * j + 64, :] = slope
        if i == 0 or j == 0:
            s.SS[i, 64 * j : 64 * j + 64, :] = slope.astype(BF)

    for j in (1, 2, 3):
        second(1, j)
    a2 = s.A2
    halo_bd = ("bd", a2.at[2, 64:320], a2.at[0, 64:320])
    halo_bc = ("bc", a2.at[2, 256:320], a2.at[0, 0:64])
    halo_bh = ("bh", a2.at[1:3, 256:320], a2.at[1:3, 0:64])
    halos_b = [halo_bd, halo_bc, halo_bh]
    send(*halo_bc)
    for halo_a in (halo_adi, halo_adj, halo_ac, halo_ahi, halo_ahj):
        receive(*halo_a)
    second_taps(0, 6, 9)
    second(0, 3)
    send(*halo_bh)
    for plane in (2, 3, 4):
        second_taps(plane, 0, 1)
    second(1, 0)
    send(*halo_bd)
    second_taps(0, 0, 6)
    second_taps(1, 0, 1)
    for j in (2, 1, 0):
        second(0, j)
    s2 = s.S2
    halos_s = [
        ("sd", s.SS.at[0], s.SD),
        ("sh", s.SS.at[0:2, 0:64], s.SH),
        ("sc", s.SS.at[0, 0:64], s.SC),
    ]
    for halo_s in halos_s:
        send(*halo_s, back)

    def third_taps(blocks):
        x = [
            jnp.concatenate([a2[plane, b * 64 : b * 64 + 64, :], a2[plane, b * 64 + 128 : b * 64 + 192, :]], 1)
            for plane, b in blocks
        ]
        y = dot(jnp.concatenate(x, 0), take("taps3")[...]).astype(BF)
        for k, (plane, b) in enumerate(blocks):
            for e in range(3):
                s.T3[plane, b * 192 + e * 64 : b * 192 + e * 64 + 64, :] = y[
                    64 * k : 64 * k + 64, e * 128 : e * 128 + 128
                ]

    third_taps([(1, 1), (1, 2), (2, 1), (2, 2)])
    gather(made_w3)
    if nc == 2:
        other = pl.ds(pl.multiple_of((1 - core) * half, 128), half)
        to_partner("w3c", s.W3.at[:, :, my_half], s.W3.at[:, :, my_half])
        w3_other = copy(
            s.W3.at[:, :, other], s.W3.at[:, :, other], plan.sem["w3c"], (dev + 1 - 2 * core, ha)
        )

    for halo_b in halos_b:
        receive(*halo_b)
    gather(made_cot)
    third_taps([(0, 0), (0, 1), (0, 2), (1, 0), (2, 0)])
    if nc == 2:
        w3_other.wait_recv()
    t3 = s.T3[...].reshape(1728, 128)
    act, slope = leaky_and_slope(dot(s.W3[...].reshape(128, 1792)[:, 0:1728], t3))
    delta3 = (s.COT[...].reshape(128, 128).astype(F32) * slope).astype(BF)
    s.D3[...] = delta3
    s.OS[...] = act.astype(BF).reshape(nh, pb, 128)
    s.D3P[...] = jnp.concatenate([delta3[0:64, 0:64], delta3[64:128, 0:64]], 1)
    halos_3 = [("3d", s.D3, s.D3D), ("3h", s.D3P, s.D3H), ("3c", s.D3P, s.D3C)]
    for halo_3 in halos_3:
        send(*halo_3, back)

    lane3 = lax.broadcasted_iota(jnp.int32, (64, 128), 1)

    def third_back(parts):
        made = []
        for a, b, d in parts:
            r = a * 576 + b * 192
            x = dot(s.W3T[r : r + 192, :], d)
            even = x[64:128]
            odd = x[128:192] + jnp.where((lane3 & 63) == 63, 0.0, pltpu.roll(x[0:64], 127, 1))
            first_height = jnp.where(lane3 < 64, even, pltpu.roll(odd, 64, 1))
            made.append((first_height, jnp.where(lane3 < 64, pltpu.roll(even, 64, 1), odd)))
        return made

    s.W3T[...] = s.W3[...].reshape(128, 1792).T
    b2 = s.B2
    one1, one2, two1, two2 = third_back([(1, 1, delta3), (1, 2, delta3), (2, 1, delta3), (2, 2, delta3)])
    for i, tap1, tap2 in ((0, one1, one2), (1, two1, two2)):
        b2[i, 0:64, :] = tap1[0]
        b2[i, 64:128, :] = tap2[0]
        b2[i, 128:192, :] = tap1[1]
        b2[i, 192:256, :] = tap2[1]
    g3 = dot_nt(delta3, t3)
    s.G3F[:, :, 1728:1792] = jnp.zeros((nh, pb, 64), F32)
    s.G3S[:, :, 1728:1792] = jnp.zeros((nh, pb, 64), BF)
    s.G3F[:, :, 0:1728] = g3.reshape(nh, pb, 1728)
    s.G3S[:, :, 0:1728] = g3.astype(BF).reshape(nh, pb, 1728)
    if nc == 2:
        g3c = to_partner("g3c", s.G3S.at[:, :, other], s.R3C)

    for c in range(nc):

        @pl.when(core == c)
        def _():
            total = s.G3F[:, :, c * half : c * half + half]
            if nc == 2:
                g3c.wait_recv()
                total = total + s.R3C[...].astype(F32)
            s.G3T[...] = total
            s.G3U[...] = total.astype(BF)

    made_g3h = spread("h", "g3h", lambda d, h: s.G3U.at[h], lambda k: s.R3H.at[k])

    dl2 = s.DL2
    receive(*halos_3[1], back)
    for halo_s in halos_s:
        receive(*halo_s, back)
    next_h = jnp.concatenate([s.D3H[:, 0:64], s.D3H[:, 64:128]], 0)
    own = jnp.concatenate([delta3[:, 64:128], next_h], 1)
    one0, two0, side1, side2 = third_back([(1, 0, own), (2, 0, own), (1, 1, own), (2, 1, own)])
    b2[0, 64:128, :] += one0[0]
    b2[0, 192:256, :] += one0[1]
    b2[0, 256:320, :] = side1[1]
    b2[1, 64:128, :] += two0[0]
    b2[1, 192:256, :] += two0[1]
    b2[1, 256:320, :] = side2[1]
    dl2[0, 0:256, :] = (b2[0, 0:256, :] * s2[0]).astype(BF)
    dl2[0, 256:320, :] = (b2[0, 256:320, :] * s.SH[0].astype(F32)).astype(BF)

    none = jnp.zeros((64, 256), BF)

    def second_grad(i, j):
        x = jnp.concatenate([dl2[i, 64 * (j + t) : 64 * (j + t) + 64, :] for t in (0, 1)], 1)
        t2 = jnp.concatenate(
            [s.T2[2 * i : 2 * i + 3, 192 * (j + t) : 192 * (j + t) + 288, :].reshape(864, 128) for t in (0, 1)], 1
        )
        low = dot_nt(t2[0:512], jnp.concatenate([x, none], 0))
        high = dot_nt(t2[512:864], jnp.concatenate([none, x], 0))
        return jnp.concatenate([low[0:352] + high, low[352:512]], 0).reshape(nc, nh, plan.r2, 128)

    lane = lax.broadcasted_iota(jnp.int32, (32, 128), 1)

    def second_back(plane, pairs):
        for j in range(5):
            y = None
            for a, i in pairs:
                term = dot(w2[a * 288 : a * 288 + 288, :], dl2[i, j * 64 : j * 64 + 64, :])
                y = term if y is None else y + term
            s.Y[j] = y
        for k in range(8):
            j = (k + 1) // 2
            d = s.Y[j, 0:96, :] + s.Y[j - 1, 192:288, :] if k % 2 else s.Y[j, 96:192, :]
            moved = jnp.where(lane < 64, pltpu.roll(d[0:32], 64, 1), pltpu.roll(d[0:32], 63, 1))
            moved = jnp.where(lane == 127, 0.0, moved)
            s.B1[plane, 32 * k : 32 * k + 32, 0:128] = d[32:64]
            s.B1[plane, 32 * k : 32 * k + 32, 128:256] = d[64:96] + moved

    s.G2F[...] = second_grad(0, 0) + second_grad(0, 2)
    second_back(0, [(1, 0)])
    receive(*halos_3[0], back)
    deep = s.D3D[...]
    zero0, zero1, zero2 = third_back([(0, 0, deep), (0, 1, deep), (0, 2, deep)])
    b2[1, 0:64, :] += zero1[0]
    b2[1, 64:128, :] += zero0[1] + zero2[0]
    b2[1, 128:192, :] += zero1[1]
    dl2[1, 0:192, :] = (b2[1, 0:192, :] * s2[1, 0:192, :]).astype(BF)
    s.G2F[...] += second_grad(1, 0)
    receive(*halos_3[2], back)
    next_c = jnp.concatenate([s.D3C[:, 0:64], s.D3C[:, 64:128]], 0)
    deep_next = jnp.concatenate([deep[:, 64:128], next_c], 1)
    corner0, side0 = third_back([(0, 0, deep_next), (0, 1, deep_next)])
    b2[1, 192:256, :] += corner0[1] + zero2[1]
    b2[1, 256:320, :] += side0[1]
    dl2[1, 192:256, :] = (b2[1, 192:256, :] * s2[1, 192:256, :]).astype(BF)
    g2 = s.G2F[...] + second_grad(1, 2)
    s.G2F[...] = g2
    s.G2S[...] = g2.astype(BF)
    made_g2h = spread("a", "g2h", lambda d, h: s.G2S.at[d & (nc - 1), h], lambda k: s.R2H.at[k])
    made_out = spread("h", "out", lambda d, h: s.OS.at[h], lambda k: s.OR.at[ha])
    s.OR[ha] = s.OS[ha]
    deep0, deep1, deep2, side3 = third_back(
        [(1, 0, deep_next), (1, 1, deep), (1, 2, deep), (1, 1, deep_next)]
    )
    b2[2, 0:64, :] = deep1[0]
    b2[2, 64:128, :] = deep0[0] + deep2[0]
    b2[2, 128:192, :] = deep1[1]
    b2[2, 192:256, :] = deep0[1] + deep2[1]
    b2[2, 256:320, :] = side3[1]
    dl2[2, 0:256, :] = (b2[2, 0:256, :] * s.SD[...].astype(F32)).astype(BF)
    dl2[1, 256:320, :] = (b2[1, 256:320, :] * s.SH[1].astype(F32)).astype(BF)
    dl2[2, 256:320, :] = (b2[2, 256:320, :] * s.SC[...].astype(F32)).astype(BF)

    second_back(1, [(2, 0), (0, 1)])
    second_back(2, [(1, 1)])
    second_back(3, [(2, 1), (0, 2)])

    s.G1A[...] = jnp.zeros((256, 576), F32)

    def loop_back(i, carry):
        d = (s.B1[i] * s.S1[i]).astype(BF)
        s.DL1[i] = d
        s.G1A[...] += dot_nt(d, s.T1[pl.ds(2 * i, 3)].reshape(576, 256))
        return carry

    lax.fori_loop(0, 4, loop_back, 0)
    def sum_parts(total, received, size):
        for k in range(1, size):
            total = total + received[k].astype(F32)
        return total

    gh = dot_nt(s.DL1[:, 0:32, :].reshape(128, 256), s.TH[...])
    sum_a = jnp.zeros((32, 576), F32)
    sum_b = jnp.zeros((32, 576), F32)
    for j in range(8):
        mask_a, mask_b = tap_masks(j)
        g = s.G1A[32 * j : 32 * j + 32, :]
        sum_a = sum_a + jnp.where(mask_a, g, 0.0)
        sum_b = sum_b + jnp.where(mask_b, g, 0.0)
    g1 = dot_nt(split_rows(sum_a), s.i_expand[:, 0:576])
    g1 = g1 + dot_nt(split_rows(sum_b), s.i_expand[:, 576:1152])
    for i in range(4):
        g1 = g1 + dot_nt(split_rows(gh[32 * i : 32 * i + 32]), s.i_halo[:, i * 256 : i * 256 + 192])
    g1 = g1[0:32] + g1[32:64]
    s.G1S[...] = g1.astype(BF)
    made_g1h = spread("a", "g1h", lambda d, h: s.G1S, lambda k: s.R1H.at[k])

    gather(made_g3h)
    total = sum_parts(s.G3T[ha], s.R3H, nh)
    s.P3F[...] = total
    s.P3S[...] = total.astype(BF)
    made_g3d = spread("z", "g3d", lambda d, h: s.P3S, lambda k: s.R3D.at[k])
    gather(made_g2h)
    g2 = sum_parts(s.G2F[core, ha], s.R2H, nh * nc)
    s.G2D[...] = g2.astype(BF)
    made_g2d = spread("z", "g2d", lambda d, h: s.G2D, lambda k: s.R2D.at[k])
    gather(made_out)
    x = s.OR[...].reshape(128, 128)
    x = jnp.concatenate([x[:, 0:64], x[:, 64:128]], 0)
    o3[...] = dot_tn(s.i_rows[...], x).astype(BF).reshape(pb, 2 * nh, 64)
    gather(made_g1h)
    g1 = sum_parts(g1, s.R1H, nh * nc)
    s.G1D[...] = g1.astype(BF)
    made_g1d = spread("z", "g1d", lambda d, h: s.G1D, lambda k: s.R1D.at[k])
    gather(made_g2d)
    g2 = sum_parts(g2, s.R2D, nz)
    s.F2[...] = g2.astype(BF)
    s.F2H[core, ha] = g2.astype(BF)
    settled = len(pending)
    made_g2z = spread("a", "g2z", lambda d, h: s.F2, lambda k: s.F2H.at[core, ha])
    gather(made_g3d)
    s.F3[core] = sum_parts(s.P3F[...], s.R3D, nz)
    if nc == 2:
        to_partner("g3p", s.F3.at[core], s.F3.at[core])
        g3p = copy(s.F3.at[1 - core], s.F3.at[1 - core], plan.sem["g3p"], (dev + 1 - 2 * core, ha))
    gather(made_g1d)
    x = (sum_parts(g1, s.R1D, nz) * scales[0]).T
    for t in range(27):
        g1o[t] = x[4 * t : 4 * t + 4]
    if nc == 2:
        g3p.wait_recv()
    for t in range(27):
        c, r = divmod(64 * t, half)
        g3o[t] = s.F3[c, :, r : r + 64] * scales[2]
    finish_sends(pending[:settled])
    gather(made_g2z)
    x = s.F2H[...].reshape(512, 128).astype(F32) * scales[1]
    g2o[0:512, :] = x[:, 0:64]
    g2o[512:864, :] = x[0:352, 64:128]
    finish_sends(pending[settled:])


def finish(*refs):
    copies = [pltpu.make_async_copy(refs[k], refs[4 + k], refs[8].at[k]) for k in range(4)]
    for c in copies:
        c.start()
    for c in copies:
        c.wait()


def local(nd, nh, volume, w_first, w_second, w_third, cotangent):
    plan = Plan(nd, nh)
    pb = plan.pb
    cells = volume.shape[1] * nd * volume.shape[2] * nh * volume.shape[3]
    scales = tuple(1.0 / math.sqrt(cells // 8**n) for n in (1, 2, 3))
    inputs = dict(
        vol=volume,
        w1=w_first.reshape(27, 4, 32),
        w2=w_second.reshape(864, 64),
        w3=jnp.transpose(w_third.reshape(27, 64, pb), (0, 2, 1)),
        cot=cotangent.reshape(pb, 2 * nh, 64),
    )
    inputs.update(zip(INPUTS[5:], constants(nh)))
    scratch = plan.scratch()
    for name in INPUTS:
        scratch["i_" + name] = pltpu.VMEM(inputs[name].shape, BF)
    names = list(scratch)
    vmem, hbm = pl.BlockSpec(memory_space=pltpu.VMEM), pl.BlockSpec(memory_space=pltpu.HBM)
    shapes = [((pb, 2 * nh, 64), BF), ((27, 4, 32), F32), ((864, 64), F32), ((27, pb, 64), F32)]
    made = pl.pallas_call(
        functools.partial(kernel, plan, names, scales),
        out_shape=[pltpu.VMEM(*x) for x in shapes],
        in_specs=[hbm] * len(INPUTS),
        out_specs=[vmem] * 4,
        scratch_shapes=[scratch[n] for n in names],
        compiler_params=pltpu.CompilerParams(
            collective_id=0 if nd * nh > 1 else None, has_side_effects=True, vmem_limit_bytes=48 * 2**20
        ),
        name="step",
    )(*[pltpu.with_memory_space_constraint(inputs[n], pltpu.HBM) for n in INPUTS])
    out3, g1, g2, g3 = pl.pallas_call(
        finish,
        out_shape=[jax.ShapeDtypeStruct(*x) for x in shapes],
        in_specs=[vmem] * 4,
        out_specs=[hbm] * 4,
        scratch_shapes=[pltpu.SemaphoreType.DMA((4,))],
        compiler_params=pltpu.CompilerParams(vmem_limit_bytes=48 * 2**20),
        name="finish",
    )(*made)
    return (
        out3.reshape(pb, 1, 2 * nh, 64),
        g1.reshape(3, 3, 3, 4, 32),
        g2.reshape(3, 3, 3, 32, 64),
        jnp.transpose(g3, (0, 2, 1)).reshape(3, 3, 3, 64, pb),
    )


def solution(mesh):
    placed = (
        P(None, "dev", "ha", None),
        P(),
        P(),
        P(None, None, None, None, "ha"),
        P("ha", "dev", None, None),
    )
    return jax.shard_map(
        functools.partial(local, mesh.shape["dev"], mesh.shape["ha"]),
        mesh=mesh,
        in_specs=placed,
        out_specs=(P("ha", "dev", None, None), P(), P(), P(None, None, None, None, "ha")),
        check_vma=False,
    )
```

```python
import functools
import math
import types

import jax
import jax.numpy as jnp
import numpy as np
from jax import lax
from jax.experimental import pallas as pl
from jax.experimental.pallas import tpu as pltpu
from jax.sharding import PartitionSpec as P

MESH = pl.DeviceIdType.MESH
BF = jnp.bfloat16
F32 = jnp.float32


def dot(a, b):
    return lax.dot_general(a, b, (((1,), (0,)), ((), ())), preferred_element_type=F32)


def dot_nt(a, b):
    return lax.dot_general(a, b, (((1,), (1,)), ((), ())), preferred_element_type=F32)


def dot_tn(a, b):
    return lax.dot_general(a, b, (((0,), (0,)), ((), ())), preferred_element_type=F32)


def split_rows(x):
    high = x.astype(BF)
    low = (x - high.astype(F32)).astype(BF)
    return jnp.concatenate([high, low], 0)


def leaky_and_slope(z):
    soft = jnp.log(1.0 + jnp.exp(-4.0 * jnp.abs(z)))
    act = jnp.maximum(z, 0.3 * z) + 0.175 * soft
    return act, 0.65 + 0.35 * jnp.tanh(2.0 * z)


ORDER2 = np.concatenate([np.arange(0, 128, 2), np.arange(1, 128, 2)])
ORDER1 = np.concatenate([2 * ORDER2, 2 * ORDER2 + 1])


def constants(nh):
    expand = np.zeros((128, 1152), np.float32)
    for a in range(3):
        for e in range(3):
            for c in range(4):
                for h in range(16):
                    col = a * 192 + e * 64 + c * 16 + h
                    row = lambda b: ((a * 3 + b) * 3 + e) * 4 + c
                    expand[row(1 + h % 2), col] = 1
                    if h % 2:
                        expand[row(0), 576 + col] = 1
    halo = np.zeros((128, 1024), np.float32)
    for i in range(4):
        for a in range(3):
            d = 2 * i - 1 + a
            s, plane = (0, d) if d >= 0 else (1, 7)
            for e in range(3):
                for c in range(4):
                    row = (a * 9 + e) * 4 + c
                    halo[row, i * 256 + s * 96 + e * 32 + plane * 4 + c] = 1
    columns = np.zeros((512, 768), np.float32)
    for e in range(3):
        for p in range(256):
            w = 2 * ORDER1[p] - 1 + e
            if w >= 0:
                columns[w, e * 256 + p] = 1
    where2 = {int(l): q for q, l in enumerate(ORDER2)}
    shift2 = np.zeros((128, 128), np.float32)
    for p in range(128):
        if ORDER2[p] >= 1:
            shift2[where2[int(ORDER2[p]) - 1], p] = 1
    taps3 = np.zeros((256, 384), np.float32)
    for jj in range(2):
        for e in range(3):
            for l in range(64):
                w = 2 * l - 1 + e
                if w >= 0:
                    taps3[jj * 128 + where2[w], e * 128 + jj * 64 + l] = 1
    last = np.zeros((32, 512), np.float32)
    for d in range(8):
        for c in range(4):
            last[d * 4 + c, c * 128 + d * 16 + 15] = 1
    pb = 128 // nh
    rows = np.zeros((256, 256), np.float32)
    for jj in range(2):
        for q in range(nh):
            for ch in range(pb):
                rows[(jj * nh + q) * pb + ch, ch * 2 * nh + 2 * q + jj] = 1
    made = (expand, halo, columns, shift2, taps3, last, np.eye(64), rows)
    return [jnp.asarray(x, BF) for x in made]


class Plan:
    def __init__(self, nd, nh):
        self.nd, self.nh = nd, nh
        self.nc = 2 if nd > 1 else 1
        self.nz = nd // self.nc
        self.pb = 128 // nh
        self.mb = 64 // nh
        self.r2 = 512 // (self.nc * nh)
        self.half = 1792 // self.nc
        self.sem = {}
        count = 0
        names = ["vd0", "vd1", "vd2", "vd3", "vh", "vc", "adi", "adj", "ahi", "ahj", "ac", "bd", "bh", "bc", "3d", "3h", "3c", "sd", "sh", "sc"]
        for name in names + ["w3c", "g3c", "g3p"]:
            self.sem[name] = count
            count += 1
        for name in ["w3", "cot", "out", "g3h"]:
            self.sem[name] = count
            count += nh - 1
        for name in ["g2h", "g2z", "g1h"]:
            self.sem[name] = count
            count += nh * self.nc - 1
        for name in ["g3d", "g2d", "g1d"]:
            self.sem[name] = count
            count += self.nz - 1
        self.count = count

    def scratch(self):
        nd, nh, nc, pb, mb = self.nd, self.nh, self.nc, self.pb, self.mb
        v = pltpu.VMEM
        return dict(
            V0=v((64, 512), BF),
            HS=v((32, 512), BF),
            HR=v((2, 32, 512), BF),
            T1=v((9, 192, 256), BF),
            TH=v((192, 256), BF),
            W1F=v((128, 32), F32),
            WT=v((256, 576), BF),
            WH=v((4, 32, 96), BF),
            WC=v((32, 96), BF),
            PH=v((4, 32, 256), F32),
            Z0=v((4, 32, 256), F32),
            A1=v((5, 288, 256), BF),
            S1=v((4, 256, 256), F32),
            T2=v((5, 864, 128), BF),
            W2T=v((3, 64, 288), BF),
            A2=v((3, 320, 128), BF),
            S2=v((2, 256, 128), F32),
            T3=v((3, 576, 128), BF),
            W3A=v((pb, 1792), BF),
            W3=v((nh, pb, 1792), BF),
            W3T=v((1792, 128), BF),
            CS=v((nh, pb, 128), BF),
            COT=v((nh, pb, 128), BF),
            OS=v((nh, pb, 128), BF),
            OR=v((nh, pb, 128), BF),
            D3=v((128, 128), BF),
            D3D=v((128, 128), BF),
            D3P=v((64, 128), BF),
            D3H=v((64, 128), BF),
            D3C=v((64, 128), BF),
            SS=v((2, 256, 128), BF),
            SD=v((256, 128), BF),
            SH=v((2, 64, 128), BF),
            SC=v((64, 128), BF),
            B2=v((3, 320, 128), F32),
            DL2=v((3, 320, 128), BF),
            Y=v((5, 288, 128), F32),
            B1=v((4, 256, 256), F32),
            DL1=v((4, 256, 256), BF),
            G3F=v((nh, pb, 1792), F32),
            G3S=v((nh, pb, 1792), BF),
            R3C=v((nh, pb, self.half), BF),
            G3T=v((nh, pb, self.half), F32),
            G3U=v((nh, pb, self.half), BF),
            R3H=v((nh, pb, self.half), BF),
            P3S=v((pb, self.half), BF),
            R3D=v((self.nz, pb, self.half), BF),
            P3F=v((pb, self.half), F32),
            F3=v((nc, pb, self.half), F32),
            G2F=v((nc, nh, self.r2, 128), F32),
            G2S=v((nc, nh, self.r2, 128), BF),
            R2H=v((nc * nh, self.r2, 128), BF),
            G2D=v((self.r2, 128), BF),
            R2D=v((self.nz, self.r2, 128), BF),
            F2=v((self.r2, 128), BF),
            F2H=v((nc, nh, self.r2, 128), BF),
            G1A=v((256, 576), F32),
            G1S=v((32, 128), BF),
            R1H=v((nc * nh, 32, 128), BF),
            G1D=v((32, 128), BF),
            R1D=v((self.nz, 32, 128), BF),
            ss=pltpu.SemaphoreType.DMA((self.count,)),
            rs=pltpu.SemaphoreType.DMA((self.count,)),
            ls=pltpu.SemaphoreType.DMA((16,)),
        )


INPUTS = ["vol", "w1", "w2", "w3", "cot", "expand", "halo", "columns", "shift2", "taps3", "last", "eye", "rows"]


def kernel(plan, names, scales, *refs):
    nd, nh, nc, nz, pb, mb, half = plan.nd, plan.nh, plan.nc, plan.nz, plan.pb, plan.mb, plan.half
    inputs = dict(zip(INPUTS, refs[: len(INPUTS)]))
    o3, g1o, g2o, g3o = refs[len(INPUTS) : len(INPUTS) + 4]
    s = types.SimpleNamespace(**dict(zip(names, refs[len(INPUTS) + 4 :])))
    ss, rs = s.ss, s.rs
    dev, ha = lax.axis_index("dev"), lax.axis_index("ha")
    core, zy = (dev & 1, dev >> 1) if nc == 2 else (dev * 0, dev)
    up_d, up_h = dev < nd - 1, ha < nh - 1
    lo_d, lo_h = dev > 0, ha > 0
    up_c, lo_c = up_d & up_h, lo_d & lo_h

    order = ["vol", "w3", "last", "columns", "w1", "expand", "halo", "cot", "rows", "w2", "eye", "shift2", "taps3"]
    copies = {}
    for k, name in enumerate(order):
        copies[name] = pltpu.make_async_copy(inputs[name], getattr(s, "i_" + name), s.ls.at[k])
        copies[name].start()
    arrived = set()

    def take(name):
        if name not in arrived:
            arrived.add(name)
            copies[name].wait()
        return getattr(s, "i_" + name)

    sizes = {"h": nh, "a": nh * nc, "z": nz}

    def wrap(x, n):
        return x & (n - 1) if n & (n - 1) == 0 else lax.rem(x, n)

    peers = {"h": [(dev, wrap(ha + k, nh)) for k in range(nh)]}
    peers["z"] = [(wrap(zy + k, nz) * nc + core, ha) for k in range(nz)]
    peers["a"] = []
    for k in range(nh * nc):
        index = wrap(ha * nc + core + k, nh * nc)
        peers["a"].append((zy * nc + wrap(index, nc), index // nc if nc == 1 else index >> 1))

    def peer_of(group, k):
        return peers[group][k]

    if nd * nh > 1:
        barrier = pltpu.get_barrier_semaphore()
        count = 0
        for group in ("a", "z"):
            for k in range(1, sizes[group]):
                pl.semaphore_signal(barrier, inc=1, device_id=peer_of(group, k), device_id_type=MESH)
                count += 1
        last_core, first_core = core == nc - 1, core == 0
        for ok, target in (
            (up_d & last_core, (dev + 1, ha)),
            (lo_d & first_core, (dev - 1, ha)),
            (up_c & last_core, (dev + 1, ha + 1)),
            (lo_c & first_core, (dev - 1, ha - 1)),
        ):

            @pl.when(ok)
            def _():
                pl.semaphore_signal(barrier, inc=1, device_id=target, device_id_type=MESH)

            count = count + ok.astype(jnp.int32)

    def copy(src, dst, k, target):
        return pltpu.make_async_remote_copy(
            src_ref=src, dst_ref=dst, send_sem=ss.at[k], recv_sem=rs.at[k], device_id=target, device_id_type=MESH
        )

    routes = {
        "d": (up_d, lo_d, nd > 1, (jnp.minimum(dev + 1, nd - 1), ha)),
        "h": (up_h, lo_h, nh > 1, (dev, jnp.minimum(ha + 1, nh - 1))),
        "c": (up_c, lo_c, nd > 1 and nh > 1, (jnp.minimum(dev + 1, nd - 1), jnp.minimum(ha + 1, nh - 1))),
    }
    back = {
        "d": (lo_d, up_d, nd > 1, (jnp.maximum(dev - 1, 0), ha)),
        "h": (lo_h, up_h, nh > 1, (dev, jnp.maximum(ha - 1, 0))),
        "c": (lo_c, up_c, nd > 1 and nh > 1, (jnp.maximum(dev - 1, 0), jnp.maximum(ha - 1, 0))),
    }
    pending = []

    def finish_sends(copies):
        for ok, c in copies:
            if ok is None:
                c.wait_send()
            else:
                pl.when(ok)(c.wait_send)

    def send(name, src, dst, table=routes):
        can_send, can_receive, exists, target = table[name[1]]
        if not exists:
            return
        c = copy(src, dst, plan.sem[name], target)
        pl.when(can_send)(c.start)
        pending.append((can_send, c))

    def receive(name, src, dst, table=routes):
        can_send, can_receive, exists, target = table[name[1]]
        if not exists:
            return
        c = copy(src, dst, plan.sem[name], target)
        pl.when(can_receive)(c.wait_recv)

    def blank(kind, ref, table=routes):
        can_send, can_receive, exists, target = table[kind]

        @pl.when(jnp.logical_not(can_receive))
        def _():
            ref[...] = jnp.zeros(ref.shape, ref.dtype)

    def spread(group, name, src_of, dst, valid_send=None, part=(1, 99)):
        made = []
        for k in range(part[0], min(part[1], sizes[group])):
            target = peer_of(group, k)
            c = copy(src_of(*target), dst(k), plan.sem[name] + k - 1, target)
            ok = None if valid_send is None else valid_send(target[0])
            if ok is None:
                c.start()
            else:
                pl.when(ok)(c.start)
            pending.append((ok, c))
            made.append((k, c))
        return made

    def gather(made, valid_receive=None):
        for k, c in made:
            if valid_receive is None:
                c.wait_recv()
            else:
                pl.when(valid_receive(lax.rem(zy + nz - k, nz)))(c.wait_recv)

    def to_partner(name, src, dst):
        c = copy(src, dst, plan.sem[name], (dev + 1 - 2 * core, ha))
        c.start()
        pending.append((None, c))
        return c

    blank("d", s.V0)
    blank("h", s.HR.at[0])
    s.HR[1, 0:16, :] = jnp.zeros((16, 512), BF)
    blank("c", s.HR.at[1, 16:32])
    blank("h", s.A1.at[1:5, 0:32])
    blank("d", s.A1.at[0, 32:288])
    blank("c", s.A1.at[0, 0:32])
    blank("h", s.A2.at[1:3, 0:64])
    blank("d", s.A2.at[0, 64:320])
    blank("c", s.A2.at[0, 0:64])
    blank("d", s.D3D, back)
    blank("h", s.D3H, back)
    blank("c", s.D3C, back)
    blank("d", s.SD, back)
    blank("h", s.SH, back)
    blank("c", s.SC, back)

    w3_in = take("w3")
    for t in range(27):
        s.W3A[:, t * 64 : t * 64 + 64] = w3_in[t]
    s.W3A[:, 1728:1792] = jnp.zeros((pb, 64), BF)
    for c in range(nc):

        @pl.when(core == c)
        def _():
            s.W3[ha, :, c * half : c * half + half] = s.W3A[:, c * half : c * half + half]

    vol = take("vol")
    s.HS[...] = dot(take("last")[...], vol[...].reshape(512, 512)).astype(BF)
    if nd * nh > 1:
        pl.semaphore_wait(barrier, count)
    halos_v = [("vh", s.HS, s.HR.at[0]), ("vc", s.HS.at[16:32], s.HR.at[1, 16:32])]
    halos_v = halos_v + [("vd%d" % c, vol.at[c, 7], s.V0.at[c * 16 : c * 16 + 16]) for c in range(4)]
    for halo_v in halos_v:
        send(*halo_v)

    def taps_of(rows):
        return dot(rows, take("columns")[...]).astype(BF)

    for c in range(4):
        taps = taps_of(vol[c].reshape(128, 512))
        for d in range(8):
            for e in range(3):
                s.T1[1 + d, e * 64 + c * 16 : e * 64 + c * 16 + 16, :] = taps[
                    d * 16 : d * 16 + 16, e * 256 : e * 256 + 256
                ]

    w1 = take("w1")
    s.W1F[96:128, :] = jnp.zeros((32, 32), F32)
    for t in range(27):
        s.W1F[4 * t : 4 * t + 4, :] = w1[t].astype(F32)
    w1b = s.W1F[...].astype(BF)
    base = dot_tn(w1b, take("expand")[...])
    base_a, base_b = base[:, 0:576], base[:, 576:1152]
    row_h = lax.broadcasted_iota(jnp.int32, (32, 576), 1) & 15

    def tap_masks(j):
        return (row_h >> 1) == j, ((row_h & 1) == 1) & (((row_h + 1) >> 1) == j)

    for j in range(8):
        mask_a, mask_b = tap_masks(j)
        s.WT[j * 32 : j * 32 + 32, :] = jnp.where(mask_a, base_a, jnp.where(mask_b, base_b, 0.0)).astype(BF)
    edge = dot_tn(w1b, take("halo")[...]).astype(BF)
    for i in range(4):
        s.WH[i] = edge[:, i * 256 : i * 256 + 96]
    s.WC[...] = edge[:, 96:192]

    def first(i):
        z = dot(s.WT[...], s.T1[pl.ds(2 * i, 3)].reshape(576, 256))
        s.Z0[i] = z[0:32]
        act, slope = leaky_and_slope(z[32:256])
        s.A1[i + 1, 64:288, :] = act.astype(BF)
        s.S1[i, 32:256, :] = slope

    def second_taps(plane, lo, hi):
        x = s.A1[plane, lo * 32 : hi * 32, :]
        moved = dot(x[:, 128:256], take("shift2")[...]).astype(BF)
        for j in range(lo, hi):
            r = (j - lo) * 32
            s.T2[plane, j * 96 : j * 96 + 32, :] = moved[r : r + 32]
            s.T2[plane, j * 96 + 32 : j * 96 + 64, :] = x[r : r + 32, 0:128]
            s.T2[plane, j * 96 + 64 : j * 96 + 96, :] = x[r : r + 32, 128:256]

    first(3)
    a1 = s.A1
    halo_adi = ("adi", a1.at[4, 64:288], a1.at[0, 64:288])
    halo_adj = ("adj", a1.at[4, 32:64], a1.at[0, 32:64])
    halo_ac = ("ac", a1.at[4, 256:288], a1.at[0, 0:32])
    halo_ahi = ("ahi", a1.at[2:5, 256:288], a1.at[2:5, 0:32])
    halo_ahj = ("ahj", a1.at[1, 256:288], a1.at[1, 0:32])
    send(*halo_adi)
    send(*halo_ac)

    def loop_first(i, carry):
        first(i)
        return carry

    lax.fori_loop(1, 3, loop_first, 0)
    send(*halo_ahi)

    my_half = pl.ds(pl.multiple_of(core * half, 128), half)
    made_w3 = spread(
        "h", "w3", lambda d, h: s.W3A.at[:, my_half], lambda k: s.W3.at[ha, :, my_half], part=(1, 5)
    )
    halo_vc = halos_v.pop(1)
    for halo_v in halos_v:
        receive(*halo_v)
    edges = taps_of(jnp.concatenate([s.V0[...], s.HR[0]], 0))
    for e in range(3):
        s.T1[0, e * 64 : e * 64 + 64, :] = edges[0:64, e * 256 : e * 256 + 256]
        s.TH[e * 32 : e * 32 + 32, :] = edges[64:96, e * 256 : e * 256 + 256]
    s.PH[...] = dot(s.WH[...].reshape(128, 96), s.TH[0:96, :]).reshape(4, 32, 256)

    def top_rows(lo, hi):
        act, slope = leaky_and_slope(s.Z0[lo:hi] + s.PH[lo:hi])
        a1[lo + 1 : hi + 1, 32:64, :] = act.astype(BF)
        s.S1[lo:hi, 0:32, :] = slope

    top_rows(1, 4)
    send(*halo_adj)
    first(0)
    send(*halo_ahj)
    made_w3 += spread(
        "h", "w3", lambda d, h: s.W3A.at[:, my_half], lambda k: s.W3.at[ha, :, my_half], part=(5, 99)
    )
    y = dot(take("rows")[...], take("cot")[...].reshape(256, 64)).astype(BF)
    s.CS[...] = jnp.concatenate([y[0:128], y[128:256]], 1).reshape(nh, pb, 128)
    s.COT[ha] = s.CS[ha]
    made_cot = spread("h", "cot", lambda d, h: s.CS.at[h], lambda k: s.COT.at[ha])
    take("shift2")

    def loop_taps(i, carry):
        second_taps(i, 2, 9)
        return carry

    lax.fori_loop(2, 5, loop_taps, 0)
    w2 = take("w2")
    take("eye")
    for a in range(3):
        s.W2T[a] = dot_nt(s.i_eye[...], w2[a * 288 : a * 288 + 288, :]).astype(BF)

    receive(*halo_vc)
    edges = taps_of(s.HR[1])
    for e in range(3):
        s.TH[96 + e * 32 : 128 + e * 32, :] = edges[:, e * 256 : e * 256 + 256]
    s.PH[0] += dot(s.WC[...], s.TH[96:192, :])
    top_rows(0, 1)
    second_taps(1, 1, 9)
    for plane in (2, 3, 4):
        second_taps(plane, 1, 2)

    def second(i, j):
        z = None
        for a in range(3):
            term = dot(s.W2T[a], s.T2[2 * i + a, j * 192 : j * 192 + 288, :])
            z = term if z is None else z + term
        act, slope = leaky_and_slope(z)
        s.A2[i + 1, 64 + 64 * j : 128 + 64 * j, :] = act.astype(BF)
        s.S2[i, 64 * j : 64 * j + 64, :] = slope
        if i == 0 or j == 0:
            s.SS[i, 64 * j : 64 * j + 64, :] = slope.astype(BF)

    for j in (1, 2, 3):
        second(1, j)
    a2 = s.A2
    halo_bd = ("bd", a2.at[2, 64:320], a2.at[0, 64:320])
    halo_bc = ("bc", a2.at[2, 256:320], a2.at[0, 0:64])
    halo_bh = ("bh", a2.at[1:3, 256:320], a2.at[1:3, 0:64])
    halos_b = [halo_bd, halo_bc, halo_bh]
    send(*halo_bc)
    for halo_a in (halo_adi, halo_adj, halo_ac, halo_ahi, halo_ahj):
        receive(*halo_a)
    second_taps(0, 6, 9)
    second(0, 3)
    send(*halo_bh)
    for plane in (2, 3, 4):
        second_taps(plane, 0, 1)
    second(1, 0)
    send(*halo_bd)
    second_taps(0, 0, 6)
    second_taps(1, 0, 1)
    for j in (2, 1, 0):
        second(0, j)
    s2 = s.S2
    halos_s = [
        ("sd", s.SS.at[0], s.SD),
        ("sh", s.SS.at[0:2, 0:64], s.SH),
        ("sc", s.SS.at[0, 0:64], s.SC),
    ]
    for halo_s in halos_s:
        send(*halo_s, back)

    def third_taps(blocks):
        x = [
            jnp.concatenate([a2[plane, b * 64 : b * 64 + 64, :], a2[plane, b * 64 + 128 : b * 64 + 192, :]], 1)
            for plane, b in blocks
        ]
        y = dot(jnp.concatenate(x, 0), take("taps3")[...]).astype(BF)
        for k, (plane, b) in enumerate(blocks):
            for e in range(3):
                s.T3[plane, b * 192 + e * 64 : b * 192 + e * 64 + 64, :] = y[
                    64 * k : 64 * k + 64, e * 128 : e * 128 + 128
                ]

    third_taps([(1, 1), (1, 2), (2, 1), (2, 2)])
    gather(made_w3)
    if nc == 2:
        other = pl.ds(pl.multiple_of((1 - core) * half, 128), half)
        to_partner("w3c", s.W3.at[:, :, my_half], s.W3.at[:, :, my_half])
        w3_other = copy(
            s.W3.at[:, :, other], s.W3.at[:, :, other], plan.sem["w3c"], (dev + 1 - 2 * core, ha)
        )

    for halo_b in halos_b:
        receive(*halo_b)
    gather(made_cot)
    third_taps([(0, 0), (0, 1), (0, 2), (1, 0), (2, 0)])
    if nc == 2:
        w3_other.wait_recv()
    t3 = s.T3[...].reshape(1728, 128)
    act, slope = leaky_and_slope(dot(s.W3[...].reshape(128, 1792)[:, 0:1728], t3))
    delta3 = (s.COT[...].reshape(128, 128).astype(F32) * slope).astype(BF)
    s.D3[...] = delta3
    s.OS[...] = act.astype(BF).reshape(nh, pb, 128)
    s.D3P[...] = jnp.concatenate([delta3[0:64, 0:64], delta3[64:128, 0:64]], 1)
    halos_3 = [("3d", s.D3, s.D3D), ("3h", s.D3P, s.D3H), ("3c", s.D3P, s.D3C)]
    for halo_3 in halos_3:
        send(*halo_3, back)

    lane3 = lax.broadcasted_iota(jnp.int32, (64, 128), 1)

    def third_back(parts):
        made = []
        for a, b, d in parts:
            r = a * 576 + b * 192
            x = dot(s.W3T[r : r + 192, :], d)
            even = x[64:128]
            odd = x[128:192] + jnp.where((lane3 & 63) == 63, 0.0, pltpu.roll(x[0:64], 127, 1))
            first_height = jnp.where(lane3 < 64, even, pltpu.roll(odd, 64, 1))
            made.append((first_height, jnp.where(lane3 < 64, pltpu.roll(even, 64, 1), odd)))
        return made

    s.W3T[...] = s.W3[...].reshape(128, 1792).T
    b2 = s.B2
    one1, one2, two1, two2 = third_back([(1, 1, delta3), (1, 2, delta3), (2, 1, delta3), (2, 2, delta3)])
    for i, tap1, tap2 in ((0, one1, one2), (1, two1, two2)):
        b2[i, 0:64, :] = tap1[0]
        b2[i, 64:128, :] = tap2[0]
        b2[i, 128:192, :] = tap1[1]
        b2[i, 192:256, :] = tap2[1]
    g3 = dot_nt(delta3, t3)
    s.G3F[:, :, 1728:1792] = jnp.zeros((nh, pb, 64), F32)
    s.G3S[:, :, 1728:1792] = jnp.zeros((nh, pb, 64), BF)
    s.G3F[:, :, 0:1728] = g3.reshape(nh, pb, 1728)
    s.G3S[:, :, 0:1728] = g3.astype(BF).reshape(nh, pb, 1728)
    if nc == 2:
        g3c = to_partner("g3c", s.G3S.at[:, :, other], s.R3C)

    for c in range(nc):

        @pl.when(core == c)
        def _():
            total = s.G3F[:, :, c * half : c * half + half]
            if nc == 2:
                g3c.wait_recv()
                total = total + s.R3C[...].astype(F32)
            s.G3T[...] = total
            s.G3U[...] = total.astype(BF)

    made_g3h = spread("h", "g3h", lambda d, h: s.G3U.at[h], lambda k: s.R3H.at[k])

    dl2 = s.DL2
    receive(*halos_3[1], back)
    for halo_s in halos_s:
        receive(*halo_s, back)
    next_h = jnp.concatenate([s.D3H[:, 0:64], s.D3H[:, 64:128]], 0)
    own = jnp.concatenate([delta3[:, 64:128], next_h], 1)
    one0, two0, side1, side2 = third_back([(1, 0, own), (2, 0, own), (1, 1, own), (2, 1, own)])
    b2[0, 64:128, :] += one0[0]
    b2[0, 192:256, :] += one0[1]
    b2[0, 256:320, :] = side1[1]
    b2[1, 64:128, :] += two0[0]
    b2[1, 192:256, :] += two0[1]
    b2[1, 256:320, :] = side2[1]
    dl2[0, 0:256, :] = (b2[0, 0:256, :] * s2[0]).astype(BF)
    dl2[0, 256:320, :] = (b2[0, 256:320, :] * s.SH[0].astype(F32)).astype(BF)

    none = jnp.zeros((64, 256), BF)

    def second_grad(i, j):
        x = jnp.concatenate([dl2[i, 64 * (j + t) : 64 * (j + t) + 64, :] for t in (0, 1)], 1)
        t2 = jnp.concatenate(
            [s.T2[2 * i : 2 * i + 3, 192 * (j + t) : 192 * (j + t) + 288, :].reshape(864, 128) for t in (0, 1)], 1
        )
        low = dot_nt(t2[0:512], jnp.concatenate([x, none], 0))
        high = dot_nt(t2[512:864], jnp.concatenate([none, x], 0))
        return jnp.concatenate([low[0:352] + high, low[352:512]], 0).reshape(nc, nh, plan.r2, 128)

    lane = lax.broadcasted_iota(jnp.int32, (32, 128), 1)

    def second_back(plane, pairs):
        for j in range(5):
            y = None
            for a, i in pairs:
                term = dot(w2[a * 288 : a * 288 + 288, :], dl2[i, j * 64 : j * 64 + 64, :])
                y = term if y is None else y + term
            s.Y[j] = y
        for k in range(8):
            j = (k + 1) // 2
            d = s.Y[j, 0:96, :] + s.Y[j - 1, 192:288, :] if k % 2 else s.Y[j, 96:192, :]
            moved = jnp.where(lane < 64, pltpu.roll(d[0:32], 64, 1), pltpu.roll(d[0:32], 63, 1))
            moved = jnp.where(lane == 127, 0.0, moved)
            s.B1[plane, 32 * k : 32 * k + 32, 0:128] = d[32:64]
            s.B1[plane, 32 * k : 32 * k + 32, 128:256] = d[64:96] + moved

    s.G2F[...] = second_grad(0, 0) + second_grad(0, 2)
    second_back(0, [(1, 0)])
    receive(*halos_3[0], back)
    deep = s.D3D[...]
    zero0, zero1, zero2 = third_back([(0, 0, deep), (0, 1, deep), (0, 2, deep)])
    b2[1, 0:64, :] += zero1[0]
    b2[1, 64:128, :] += zero0[1] + zero2[0]
    b2[1, 128:192, :] += zero1[1]
    dl2[1, 0:192, :] = (b2[1, 0:192, :] * s2[1, 0:192, :]).astype(BF)
    s.G2F[...] += second_grad(1, 0)
    receive(*halos_3[2], back)
    next_c = jnp.concatenate([s.D3C[:, 0:64], s.D3C[:, 64:128]], 0)
    deep_next = jnp.concatenate([deep[:, 64:128], next_c], 1)
    corner0, side0 = third_back([(0, 0, deep_next), (0, 1, deep_next)])
    b2[1, 192:256, :] += corner0[1] + zero2[1]
    b2[1, 256:320, :] += side0[1]
    dl2[1, 192:256, :] = (b2[1, 192:256, :] * s2[1, 192:256, :]).astype(BF)
    g2 = s.G2F[...] + second_grad(1, 2)
    s.G2F[...] = g2
    s.G2S[...] = g2.astype(BF)
    made_g2h = spread("a", "g2h", lambda d, h: s.G2S.at[d & (nc - 1), h], lambda k: s.R2H.at[k])
    made_out = spread("h", "out", lambda d, h: s.OS.at[h], lambda k: s.OR.at[ha])
    s.OR[ha] = s.OS[ha]
    deep0, deep1, deep2, side3 = third_back(
        [(1, 0, deep_next), (1, 1, deep), (1, 2, deep), (1, 1, deep_next)]
    )
    b2[2, 0:64, :] = deep1[0]
    b2[2, 64:128, :] = deep0[0] + deep2[0]
    b2[2, 128:192, :] = deep1[1]
    b2[2, 192:256, :] = deep0[1] + deep2[1]
    b2[2, 256:320, :] = side3[1]
    dl2[2, 0:256, :] = (b2[2, 0:256, :] * s.SD[...].astype(F32)).astype(BF)
    dl2[1, 256:320, :] = (b2[1, 256:320, :] * s.SH[1].astype(F32)).astype(BF)
    dl2[2, 256:320, :] = (b2[2, 256:320, :] * s.SC[...].astype(F32)).astype(BF)

    second_back(1, [(2, 0), (0, 1)])
    second_back(2, [(1, 1)])
    second_back(3, [(2, 1), (0, 2)])

    s.G1A[...] = jnp.zeros((256, 576), F32)

    def loop_back(i, carry):
        d = (s.B1[i] * s.S1[i]).astype(BF)
        s.DL1[i] = d
        s.G1A[...] += dot_nt(d, s.T1[pl.ds(2 * i, 3)].reshape(576, 256))
        return carry

    lax.fori_loop(0, 4, loop_back, 0)
    def sum_parts(total, received, size):
        for k in range(1, size):
            total = total + received[k].astype(F32)
        return total

    gh = dot_nt(s.DL1[:, 0:32, :].reshape(128, 256), s.TH[...])
    sum_a = jnp.zeros((32, 576), F32)
    sum_b = jnp.zeros((32, 576), F32)
    for j in range(8):
        mask_a, mask_b = tap_masks(j)
        g = s.G1A[32 * j : 32 * j + 32, :]
        sum_a = sum_a + jnp.where(mask_a, g, 0.0)
        sum_b = sum_b + jnp.where(mask_b, g, 0.0)
    g1 = dot_nt(split_rows(sum_a), s.i_expand[:, 0:576])
    g1 = g1 + dot_nt(split_rows(sum_b), s.i_expand[:, 576:1152])
    for i in range(4):
        g1 = g1 + dot_nt(split_rows(gh[32 * i : 32 * i + 32]), s.i_halo[:, i * 256 : i * 256 + 192])
    g1 = g1[0:32] + g1[32:64]
    s.G1S[...] = g1.astype(BF)
    made_g1h = spread("a", "g1h", lambda d, h: s.G1S, lambda k: s.R1H.at[k])

    gather(made_g3h)
    total = sum_parts(s.G3T[ha], s.R3H, nh)
    s.P3F[...] = total
    s.P3S[...] = total.astype(BF)
    made_g3d = spread("z", "g3d", lambda d, h: s.P3S, lambda k: s.R3D.at[k])
    gather(made_g2h)
    g2 = sum_parts(s.G2F[core, ha], s.R2H, nh * nc)
    s.G2D[...] = g2.astype(BF)
    made_g2d = spread("z", "g2d", lambda d, h: s.G2D, lambda k: s.R2D.at[k])
    gather(made_out)
    x = s.OR[...].reshape(128, 128)
    x = jnp.concatenate([x[:, 0:64], x[:, 64:128]], 0)
    o3[...] = dot_tn(s.i_rows[...], x).astype(BF).reshape(pb, 2 * nh, 64)
    gather(made_g1h)
    g1 = sum_parts(g1, s.R1H, nh * nc)
    s.G1D[...] = g1.astype(BF)
    made_g1d = spread("z", "g1d", lambda d, h: s.G1D, lambda k: s.R1D.at[k])
    gather(made_g2d)
    g2 = sum_parts(g2, s.R2D, nz)
    s.F2[...] = g2.astype(BF)
    s.F2H[core, ha] = g2.astype(BF)
    settled = len(pending)
    made_g2z = spread("a", "g2z", lambda d, h: s.F2, lambda k: s.F2H.at[core, ha])
    gather(made_g3d)
    s.F3[core] = sum_parts(s.P3F[...], s.R3D, nz)
    if nc == 2:
        to_partner("g3p", s.F3.at[core], s.F3.at[core])
        g3p = copy(s.F3.at[1 - core], s.F3.at[1 - core], plan.sem["g3p"], (dev + 1 - 2 * core, ha))
    gather(made_g1d)
    x = (sum_parts(g1, s.R1D, nz) * scales[0]).T
    for t in range(27):
        g1o[t] = x[4 * t : 4 * t + 4]
    if nc == 2:
        g3p.wait_recv()
    for t in range(27):
        c, r = divmod(64 * t, half)
        g3o[t] = s.F3[c, :, r : r + 64] * scales[2]
    finish_sends(pending[:settled])
    gather(made_g2z)
    x = s.F2H[...].reshape(512, 128).astype(F32) * scales[1]
    g2o[0:512, :] = x[:, 0:64]
    g2o[512:864, :] = x[0:352, 64:128]
    finish_sends(pending[settled:])


def finish(*refs):
    copies = [pltpu.make_async_copy(refs[k], refs[4 + k], refs[8].at[k]) for k in range(4)]
    for c in copies:
        c.start()
    for c in copies:
        c.wait()


def local(nd, nh, volume, w_first, w_second, w_third, cotangent):
    plan = Plan(nd, nh)
    pb = plan.pb
    cells = volume.shape[1] * nd * volume.shape[2] * nh * volume.shape[3]
    scales = tuple(1.0 / math.sqrt(cells // 8**n) for n in (1, 2, 3))
    inputs = dict(
        vol=volume,
        w1=w_first.reshape(27, 4, 32),
        w2=w_second.reshape(864, 64),
        w3=jnp.transpose(w_third.reshape(27, 64, pb), (0, 2, 1)),
        cot=cotangent.reshape(pb, 2 * nh, 64),
    )
    inputs.update(zip(INPUTS[5:], constants(nh)))
    scratch = plan.scratch()
    for name in INPUTS:
        scratch["i_" + name] = pltpu.VMEM(inputs[name].shape, BF)
    names = list(scratch)
    vmem, hbm = pl.BlockSpec(memory_space=pltpu.VMEM), pl.BlockSpec(memory_space=pltpu.HBM)
    shapes = [((pb, 2 * nh, 64), BF), ((27, 4, 32), F32), ((864, 64), F32), ((27, pb, 64), F32)]
    made = pl.pallas_call(
        functools.partial(kernel, plan, names, scales),
        out_shape=[pltpu.VMEM(*x) for x in shapes],
        in_specs=[hbm] * len(INPUTS),
        out_specs=[vmem] * 4,
        scratch_shapes=[scratch[n] for n in names],
        compiler_params=pltpu.CompilerParams(
            collective_id=0 if nd * nh > 1 else None, has_side_effects=True, vmem_limit_bytes=48 * 2**20
        ),
        name="step",
    )(*[pltpu.with_memory_space_constraint(inputs[n], pltpu.HBM) for n in INPUTS])
    out3, g1, g2, g3 = pl.pallas_call(
        finish,
        out_shape=[jax.ShapeDtypeStruct(*x) for x in shapes],
        in_specs=[vmem] * 4,
        out_specs=[hbm] * 4,
        scratch_shapes=[pltpu.SemaphoreType.DMA((4,))],
        compiler_params=pltpu.CompilerParams(vmem_limit_bytes=48 * 2**20),
        name="finish",
    )(*made)
    return (
        out3.reshape(pb, 1, 2 * nh, 64),
        g1.reshape(3, 3, 3, 4, 32),
        g2.reshape(3, 3, 3, 32, 64),
        jnp.transpose(g3, (0, 2, 1)).reshape(3, 3, 3, 64, pb),
    )


def solution(mesh):
    placed = (
        P(None, "dev", "ha", None),
        P(),
        P(),
        P(None, None, None, None, "ha"),
        P("ha", "dev", None, None),
    )
    return jax.shard_map(
        functools.partial(local, mesh.shape["dev"], mesh.shape["ha"]),
        mesh=mesh,
        in_specs=placed,
        out_specs=(P("ha", "dev", None, None), P(), P(), P(None, None, None, None, "ha")),
        check_vma=False,
    )
```

```python
import functools
import math
import types

import jax
import jax.numpy as jnp
import numpy as np
from jax import lax
from jax.experimental import pallas as pl
from jax.experimental.pallas import tpu as pltpu
from jax.sharding import PartitionSpec as P

MESH = pl.DeviceIdType.MESH
BF = jnp.bfloat16
F32 = jnp.float32


def dot(a, b):
    return lax.dot_general(a, b, (((1,), (0,)), ((), ())), preferred_element_type=F32)


def dot_nt(a, b):
    return lax.dot_general(a, b, (((1,), (1,)), ((), ())), preferred_element_type=F32)


def dot_tn(a, b):
    return lax.dot_general(a, b, (((0,), (0,)), ((), ())), preferred_element_type=F32)


def split_rows(x):
    high = x.astype(BF)
    low = (x - high.astype(F32)).astype(BF)
    return jnp.concatenate([high, low], 0)


def leaky_and_slope(z):
    soft = jnp.log(1.0 + jnp.exp(-4.0 * jnp.abs(z)))
    act = jnp.maximum(z, 0.3 * z) + 0.175 * soft
    return act, 0.65 + 0.35 * jnp.tanh(2.0 * z)


ORDER2 = np.concatenate([np.arange(0, 128, 2), np.arange(1, 128, 2)])
ORDER1 = np.concatenate([2 * ORDER2, 2 * ORDER2 + 1])


def constants(nh):
    expand = np.zeros((128, 1152), np.float32)
    for a in range(3):
        for e in range(3):
            for c in range(4):
                for h in range(16):
                    col = a * 192 + e * 64 + c * 16 + h
                    row = lambda b: ((a * 3 + b) * 3 + e) * 4 + c
                    expand[row(1 + h % 2), col] = 1
                    if h % 2:
                        expand[row(0), 576 + col] = 1
    halo = np.zeros((128, 1024), np.float32)
    for i in range(4):
        for a in range(3):
            d = 2 * i - 1 + a
            s, plane = (0, d) if d >= 0 else (1, 7)
            for e in range(3):
                for c in range(4):
                    row = (a * 9 + e) * 4 + c
                    halo[row, i * 256 + s * 96 + e * 32 + plane * 4 + c] = 1
    columns = np.zeros((512, 768), np.float32)
    for e in range(3):
        for p in range(256):
            w = 2 * ORDER1[p] - 1 + e
            if w >= 0:
                columns[w, e * 256 + p] = 1
    where2 = {int(l): q for q, l in enumerate(ORDER2)}
    shift2 = np.zeros((128, 128), np.float32)
    for p in range(128):
        if ORDER2[p] >= 1:
            shift2[where2[int(ORDER2[p]) - 1], p] = 1
    taps3 = np.zeros((256, 384), np.float32)
    for jj in range(2):
        for e in range(3):
            for l in range(64):
                w = 2 * l - 1 + e
                if w >= 0:
                    taps3[jj * 128 + where2[w], e * 128 + jj * 64 + l] = 1
    last = np.zeros((32, 512), np.float32)
    for d in range(8):
        for c in range(4):
            last[d * 4 + c, c * 128 + d * 16 + 15] = 1
    pb = 128 // nh
    rows = np.zeros((256, 256), np.float32)
    for jj in range(2):
        for q in range(nh):
            for ch in range(pb):
                rows[(jj * nh + q) * pb + ch, ch * 2 * nh + 2 * q + jj] = 1
    made = (expand, halo, columns, shift2, taps3, last, np.eye(64), rows)
    return [jnp.asarray(x, BF) for x in made]


class Plan:
    def __init__(self, nd, nh):
        self.nd, self.nh = nd, nh
        self.nc = 2 if nd > 1 else 1
        self.nz = nd // self.nc
        self.pb = 128 // nh
        self.mb = 64 // nh
        self.r2 = 512 // (self.nc * nh)
        self.half = 1792 // self.nc
        self.sem = {}
        count = 0
        names = ["vd0", "vd1", "vd2", "vd3", "vh", "vc", "adi", "adj", "ahi", "ahj", "ac", "bd", "bh", "bc", "3d", "3h", "3c", "sd", "sh", "sc"]
        for name in names + ["w3c", "g3c", "g3p"]:
            self.sem[name] = count
            count += 1
        for name in ["w3", "cot", "out", "g3h"]:
            self.sem[name] = count
            count += nh - 1
        for name in ["g2h", "g2z", "g1h"]:
            self.sem[name] = count
            count += nh * self.nc - 1
        for name in ["g3d", "g2d", "g1d"]:
            self.sem[name] = count
            count += self.nz - 1
        self.count = count

    def scratch(self):
        nd, nh, nc, pb, mb = self.nd, self.nh, self.nc, self.pb, self.mb
        v = pltpu.VMEM
        return dict(
            V0=v((64, 512), BF),
            HS=v((32, 512), BF),
            HR=v((2, 32, 512), BF),
            T1=v((9, 192, 256), BF),
            TH=v((192, 256), BF),
            W1F=v((128, 32), F32),
            WT=v((256, 576), BF),
            WH=v((4, 32, 96), BF),
            WC=v((32, 96), BF),
            PH=v((4, 32, 256), F32),
            Z0=v((4, 32, 256), F32),
            A1=v((5, 288, 256), BF),
            S1=v((4, 256, 256), F32),
            T2=v((5, 864, 128), BF),
            W2T=v((3, 64, 288), BF),
            A2=v((3, 320, 128), BF),
            S2=v((2, 256, 128), F32),
            T3=v((3, 576, 128), BF),
            W3A=v((pb, 1792), BF),
            W3=v((nh, pb, 1792), BF),
            W3T=v((1792, 128), BF),
            CS=v((nh, pb, 128), BF),
            COT=v((nh, pb, 128), BF),
            OS=v((nh, pb, 128), BF),
            OR=v((nh, pb, 128), BF),
            D3=v((128, 128), BF),
            D3D=v((128, 128), BF),
            D3P=v((64, 128), BF),
            D3H=v((64, 128), BF),
            D3C=v((64, 128), BF),
            SS=v((2, 256, 128), BF),
            SD=v((256, 128), BF),
            SH=v((2, 64, 128), BF),
            SC=v((64, 128), BF),
            B2=v((3, 320, 128), F32),
            DL2=v((3, 320, 128), BF),
            Y=v((5, 288, 128), F32),
            B1=v((4, 256, 256), F32),
            DL1=v((4, 256, 256), BF),
            G3F=v((nh, pb, 1792), F32),
            G3S=v((nh, pb, 1792), BF),
            R3C=v((nh, pb, self.half), BF),
            G3T=v((nh, pb, self.half), F32),
            G3U=v((nh, pb, self.half), BF),
            R3H=v((nh, pb, self.half), BF),
            P3S=v((pb, self.half), BF),
            R3D=v((self.nz, pb, self.half), BF),
            P3F=v((pb, self.half), F32),
            F3=v((nc, pb, self.half), F32),
            G2F=v((nc, nh, self.r2, 128), F32),
            G2S=v((nc, nh, self.r2, 128), BF),
            R2H=v((nc * nh, self.r2, 128), BF),
            G2D=v((self.r2, 128), BF),
            R2D=v((self.nz, self.r2, 128), BF),
            F2=v((self.r2, 128), BF),
            F2H=v((nc, nh, self.r2, 128), BF),
            G1A=v((256, 576), F32),
            G1S=v((32, 128), BF),
            R1H=v((nc * nh, 32, 128), BF),
            G1D=v((32, 128), BF),
            R1D=v((self.nz, 32, 128), BF),
            ss=pltpu.SemaphoreType.DMA((self.count,)),
            rs=pltpu.SemaphoreType.DMA((self.count,)),
            ls=pltpu.SemaphoreType.DMA((16,)),
        )


INPUTS = ["vol", "w1", "w2", "w3", "cot", "expand", "halo", "columns", "shift2", "taps3", "last", "eye", "rows"]


def kernel(plan, names, scales, *refs):
    nd, nh, nc, nz, pb, mb, half = plan.nd, plan.nh, plan.nc, plan.nz, plan.pb, plan.mb, plan.half
    inputs = dict(zip(INPUTS, refs[: len(INPUTS)]))
    o3, g1o, g2o, g3o = refs[len(INPUTS) : len(INPUTS) + 4]
    s = types.SimpleNamespace(**dict(zip(names, refs[len(INPUTS) + 4 :])))
    ss, rs = s.ss, s.rs
    dev, ha = lax.axis_index("dev"), lax.axis_index("ha")
    core, zy = (dev & 1, dev >> 1) if nc == 2 else (dev * 0, dev)
    up_d, up_h = dev < nd - 1, ha < nh - 1
    lo_d, lo_h = dev > 0, ha > 0
    up_c, lo_c = up_d & up_h, lo_d & lo_h

    order = ["vol", "w3", "last", "columns", "w1", "expand", "halo", "cot", "rows", "w2", "eye", "shift2", "taps3"]
    copies = {}
    for k, name in enumerate(order):
        copies[name] = pltpu.make_async_copy(inputs[name], getattr(s, "i_" + name), s.ls.at[k])
        copies[name].start()
    arrived = set()

    def take(name):
        if name not in arrived:
            arrived.add(name)
            copies[name].wait()
        return getattr(s, "i_" + name)

    sizes = {"h": nh, "a": nh * nc, "z": nz}

    def wrap(x, n):
        return x & (n - 1) if n & (n - 1) == 0 else lax.rem(x, n)

    peers = {"h": [(dev, wrap(ha + k, nh)) for k in range(nh)]}
    peers["z"] = [(wrap(zy + k, nz) * nc + core, ha) for k in range(nz)]
    peers["a"] = []
    for k in range(nh * nc):
        index = wrap(ha * nc + core + k, nh * nc)
        peers["a"].append((zy * nc + wrap(index, nc), index // nc if nc == 1 else index >> 1))

    def peer_of(group, k):
        return peers[group][k]

    if nd * nh > 1:
        barrier = pltpu.get_barrier_semaphore()
        count = 0
        for group in ("a", "z"):
            for k in range(1, sizes[group]):
                pl.semaphore_signal(barrier, inc=1, device_id=peer_of(group, k), device_id_type=MESH)
                count += 1
        last_core, first_core = core == nc - 1, core == 0
        for ok, target in (
            (up_d & last_core, (dev + 1, ha)),
            (lo_d & first_core, (dev - 1, ha)),
            (up_c & last_core, (dev + 1, ha + 1)),
            (lo_c & first_core, (dev - 1, ha - 1)),
        ):

            @pl.when(ok)
            def _():
                pl.semaphore_signal(barrier, inc=1, device_id=target, device_id_type=MESH)

            count = count + ok.astype(jnp.int32)

    def copy(src, dst, k, target):
        return pltpu.make_async_remote_copy(
            src_ref=src, dst_ref=dst, send_sem=ss.at[k], recv_sem=rs.at[k], device_id=target, device_id_type=MESH
        )

    routes = {
        "d": (up_d, lo_d, nd > 1, (jnp.minimum(dev + 1, nd - 1), ha)),
        "h": (up_h, lo_h, nh > 1, (dev, jnp.minimum(ha + 1, nh - 1))),
        "c": (up_c, lo_c, nd > 1 and nh > 1, (jnp.minimum(dev + 1, nd - 1), jnp.minimum(ha + 1, nh - 1))),
    }
    back = {
        "d": (lo_d, up_d, nd > 1, (jnp.maximum(dev - 1, 0), ha)),
        "h": (lo_h, up_h, nh > 1, (dev, jnp.maximum(ha - 1, 0))),
        "c": (lo_c, up_c, nd > 1 and nh > 1, (jnp.maximum(dev - 1, 0), jnp.maximum(ha - 1, 0))),
    }
    pending = []

    def finish_sends(copies):
        for ok, c in copies:
            if ok is None:
                c.wait_send()
            else:
                pl.when(ok)(c.wait_send)

    def send(name, src, dst, table=routes):
        can_send, can_receive, exists, target = table[name[1]]
        if not exists:
            return
        c = copy(src, dst, plan.sem[name], target)
        pl.when(can_send)(c.start)
        pending.append((can_send, c))

    def receive(name, src, dst, table=routes):
        can_send, can_receive, exists, target = table[name[1]]
        if not exists:
            return
        c = copy(src, dst, plan.sem[name], target)
        pl.when(can_receive)(c.wait_recv)

    def blank(kind, ref, table=routes):
        can_send, can_receive, exists, target = table[kind]

        @pl.when(jnp.logical_not(can_receive))
        def _():
            ref[...] = jnp.zeros(ref.shape, ref.dtype)

    def spread(group, name, src_of, dst, valid_send=None, part=(1, 99)):
        made = []
        for k in range(part[0], min(part[1], sizes[group])):
            target = peer_of(group, k)
            c = copy(src_of(*target), dst(k), plan.sem[name] + k - 1, target)
            ok = None if valid_send is None else valid_send(target[0])
            if ok is None:
                c.start()
            else:
                pl.when(ok)(c.start)
            pending.append((ok, c))
            made.append((k, c))
        return made

    def gather(made, valid_receive=None):
        for k, c in made:
            if valid_receive is None:
                c.wait_recv()
            else:
                pl.when(valid_receive(lax.rem(zy + nz - k, nz)))(c.wait_recv)

    def to_partner(name, src, dst):
        c = copy(src, dst, plan.sem[name], (dev + 1 - 2 * core, ha))
        c.start()
        pending.append((None, c))
        return c

    blank("d", s.V0)
    blank("h", s.HR.at[0])
    s.HR[1, 0:16, :] = jnp.zeros((16, 512), BF)
    blank("c", s.HR.at[1, 16:32])
    blank("h", s.A1.at[1:5, 0:32])
    blank("d", s.A1.at[0, 32:288])
    blank("c", s.A1.at[0, 0:32])
    blank("h", s.A2.at[1:3, 0:64])
    blank("d", s.A2.at[0, 64:320])
    blank("c", s.A2.at[0, 0:64])
    blank("d", s.D3D, back)
    blank("h", s.D3H, back)
    blank("c", s.D3C, back)
    blank("d", s.SD, back)
    blank("h", s.SH, back)
    blank("c", s.SC, back)

    w3_in = take("w3")
    for t in range(27):
        s.W3A[:, t * 64 : t * 64 + 64] = w3_in[t]
    s.W3A[:, 1728:1792] = jnp.zeros((pb, 64), BF)
    for c in range(nc):

        @pl.when(core == c)
        def _():
            s.W3[ha, :, c * half : c * half + half] = s.W3A[:, c * half : c * half + half]

    vol = take("vol")
    s.HS[...] = dot(take("last")[...], vol[...].reshape(512, 512)).astype(BF)
    if nd * nh > 1:
        pl.semaphore_wait(barrier, count)
    halos_v = [("vh", s.HS, s.HR.at[0]), ("vc", s.HS.at[16:32], s.HR.at[1, 16:32])]
    halos_v = halos_v + [("vd%d" % c, vol.at[c, 7], s.V0.at[c * 16 : c * 16 + 16]) for c in range(4)]
    for halo_v in halos_v:
        send(*halo_v)

    def taps_of(rows):
        return dot(rows, take("columns")[...]).astype(BF)

    for c in range(4):
        taps = taps_of(vol[c].reshape(128, 512))
        for d in range(8):
            for e in range(3):
                s.T1[1 + d, e * 64 + c * 16 : e * 64 + c * 16 + 16, :] = taps[
                    d * 16 : d * 16 + 16, e * 256 : e * 256 + 256
                ]

    w1 = take("w1")
    s.W1F[96:128, :] = jnp.zeros((32, 32), F32)
    for t in range(27):
        s.W1F[4 * t : 4 * t + 4, :] = w1[t].astype(F32)
    w1b = s.W1F[...].astype(BF)
    base = dot_tn(w1b, take("expand")[...])
    base_a, base_b = base[:, 0:576], base[:, 576:1152]
    row_h = lax.broadcasted_iota(jnp.int32, (32, 576), 1) & 15

    def tap_masks(j):
        return (row_h >> 1) == j, ((row_h & 1) == 1) & (((row_h + 1) >> 1) == j)

    for j in range(8):
        mask_a, mask_b = tap_masks(j)
        s.WT[j * 32 : j * 32 + 32, :] = jnp.where(mask_a, base_a, jnp.where(mask_b, base_b, 0.0)).astype(BF)
    edge = dot_tn(w1b, take("halo")[...]).astype(BF)
    for i in range(4):
        s.WH[i] = edge[:, i * 256 : i * 256 + 96]
    s.WC[...] = edge[:, 96:192]

    def first(i):
        z = dot(s.WT[...], s.T1[pl.ds(2 * i, 3)].reshape(576, 256))
        s.Z0[i] = z[0:32]
        act, slope = leaky_and_slope(z[32:256])
        s.A1[i + 1, 64:288, :] = act.astype(BF)
        s.S1[i, 32:256, :] = slope

    def second_taps(plane, lo, hi):
        x = s.A1[plane, lo * 32 : hi * 32, :]
        moved = dot(x[:, 128:256], take("shift2")[...]).astype(BF)
        for j in range(lo, hi):
            r = (j - lo) * 32
            s.T2[plane, j * 96 : j * 96 + 32, :] = moved[r : r + 32]
            s.T2[plane, j * 96 + 32 : j * 96 + 64, :] = x[r : r + 32, 0:128]
            s.T2[plane, j * 96 + 64 : j * 96 + 96, :] = x[r : r + 32, 128:256]

    first(3)
    a1 = s.A1
    halo_adi = ("adi", a1.at[4, 64:288], a1.at[0, 64:288])
    halo_adj = ("adj", a1.at[4, 32:64], a1.at[0, 32:64])
    halo_ac = ("ac", a1.at[4, 256:288], a1.at[0, 0:32])
    halo_ahi = ("ahi", a1.at[2:5, 256:288], a1.at[2:5, 0:32])
    halo_ahj = ("ahj", a1.at[1, 256:288], a1.at[1, 0:32])
    send(*halo_adi)
    send(*halo_ac)

    def loop_first(i, carry):
        first(i)
        return carry

    lax.fori_loop(1, 3, loop_first, 0)
    send(*halo_ahi)

    my_half = pl.ds(pl.multiple_of(core * half, 128), half)
    made_w3 = spread(
        "h", "w3", lambda d, h: s.W3A.at[:, my_half], lambda k: s.W3.at[ha, :, my_half], part=(1, 4)
    )
    halo_vc = halos_v.pop(1)
    for halo_v in halos_v:
        receive(*halo_v)
    edges = taps_of(jnp.concatenate([s.V0[...], s.HR[0]], 0))
    for e in range(3):
        s.T1[0, e * 64 : e * 64 + 64, :] = edges[0:64, e * 256 : e * 256 + 256]
        s.TH[e * 32 : e * 32 + 32, :] = edges[64:96, e * 256 : e * 256 + 256]
    s.PH[...] = dot(s.WH[...].reshape(128, 96), s.TH[0:96, :]).reshape(4, 32, 256)

    def top_rows(lo, hi):
        act, slope = leaky_and_slope(s.Z0[lo:hi] + s.PH[lo:hi])
        a1[lo + 1 : hi + 1, 32:64, :] = act.astype(BF)
        s.S1[lo:hi, 0:32, :] = slope

    top_rows(1, 4)
    send(*halo_adj)
    first(0)
    send(*halo_ahj)
    made_w3 += spread(
        "h", "w3", lambda d, h: s.W3A.at[:, my_half], lambda k: s.W3.at[ha, :, my_half], part=(4, 99)
    )
    y = dot(take("rows")[...], take("cot")[...].reshape(256, 64)).astype(BF)
    s.CS[...] = jnp.concatenate([y[0:128], y[128:256]], 1).reshape(nh, pb, 128)
    s.COT[ha] = s.CS[ha]
    made_cot = spread("h", "cot", lambda d, h: s.CS.at[h], lambda k: s.COT.at[ha])
    take("shift2")

    def loop_taps(i, carry):
        second_taps(i, 2, 9)
        return carry

    lax.fori_loop(2, 5, loop_taps, 0)
    w2 = take("w2")
    take("eye")
    for a in range(3):
        s.W2T[a] = dot_nt(s.i_eye[...], w2[a * 288 : a * 288 + 288, :]).astype(BF)

    receive(*halo_vc)
    edges = taps_of(s.HR[1])
    for e in range(3):
        s.TH[96 + e * 32 : 128 + e * 32, :] = edges[:, e * 256 : e * 256 + 256]
    s.PH[0] += dot(s.WC[...], s.TH[96:192, :])
    top_rows(0, 1)
    second_taps(1, 1, 9)
    for plane in (2, 3, 4):
        second_taps(plane, 1, 2)

    def second(i, j):
        z = None
        for a in range(3):
            term = dot(s.W2T[a], s.T2[2 * i + a, j * 192 : j * 192 + 288, :])
            z = term if z is None else z + term
        act, slope = leaky_and_slope(z)
        s.A2[i + 1, 64 + 64 * j : 128 + 64 * j, :] = act.astype(BF)
        s.S2[i, 64 * j : 64 * j + 64, :] = slope
        if i == 0 or j == 0:
            s.SS[i, 64 * j : 64 * j + 64, :] = slope.astype(BF)

    for j in (1, 2, 3):
        second(1, j)
    a2 = s.A2
    halo_bd = ("bd", a2.at[2, 64:320], a2.at[0, 64:320])
    halo_bc = ("bc", a2.at[2, 256:320], a2.at[0, 0:64])
    halo_bh = ("bh", a2.at[1:3, 256:320], a2.at[1:3, 0:64])
    halos_b = [halo_bd, halo_bc, halo_bh]
    send(*halo_bc)
    for halo_a in (halo_adi, halo_adj, halo_ac, halo_ahi, halo_ahj):
        receive(*halo_a)
    second_taps(0, 6, 9)
    second(0, 3)
    send(*halo_bh)
    for plane in (2, 3, 4):
        second_taps(plane, 0, 1)
    second(1, 0)
    send(*halo_bd)
    second_taps(0, 0, 6)
    second_taps(1, 0, 1)
    for j in (2, 1, 0):
        second(0, j)
    s2 = s.S2
    halos_s = [
        ("sd", s.SS.at[0], s.SD),
        ("sh", s.SS.at[0:2, 0:64], s.SH),
        ("sc", s.SS.at[0, 0:64], s.SC),
    ]
    for halo_s in halos_s:
        send(*halo_s, back)

    def third_taps(blocks):
        x = [
            jnp.concatenate([a2[plane, b * 64 : b * 64 + 64, :], a2[plane, b * 64 + 128 : b * 64 + 192, :]], 1)
            for plane, b in blocks
        ]
        y = dot(jnp.concatenate(x, 0), take("taps3")[...]).astype(BF)
        for k, (plane, b) in enumerate(blocks):
            for e in range(3):
                s.T3[plane, b * 192 + e * 64 : b * 192 + e * 64 + 64, :] = y[
                    64 * k : 64 * k + 64, e * 128 : e * 128 + 128
                ]

    third_taps([(1, 1), (1, 2), (2, 1), (2, 2)])
    gather(made_w3)
    if nc == 2:
        other = pl.ds(pl.multiple_of((1 - core) * half, 128), half)
        to_partner("w3c", s.W3.at[:, :, my_half], s.W3.at[:, :, my_half])
        w3_other = copy(
            s.W3.at[:, :, other], s.W3.at[:, :, other], plan.sem["w3c"], (dev + 1 - 2 * core, ha)
        )

    for halo_b in halos_b:
        receive(*halo_b)
    gather(made_cot)
    third_taps([(0, 0), (0, 1), (0, 2), (1, 0), (2, 0)])
    if nc == 2:
        w3_other.wait_recv()
    t3 = s.T3[...].reshape(1728, 128)
    act, slope = leaky_and_slope(dot(s.W3[...].reshape(128, 1792)[:, 0:1728], t3))
    delta3 = (s.COT[...].reshape(128, 128).astype(F32) * slope).astype(BF)
    s.D3[...] = delta3
    s.OS[...] = act.astype(BF).reshape(nh, pb, 128)
    s.D3P[...] = jnp.concatenate([delta3[0:64, 0:64], delta3[64:128, 0:64]], 1)
    halos_3 = [("3d", s.D3, s.D3D), ("3h", s.D3P, s.D3H), ("3c", s.D3P, s.D3C)]
    for halo_3 in halos_3:
        send(*halo_3, back)

    lane3 = lax.broadcasted_iota(jnp.int32, (64, 128), 1)

    def third_back(parts):
        made = []
        for a, b, d in parts:
            r = a * 576 + b * 192
            x = dot(s.W3T[r : r + 192, :], d)
            even = x[64:128]
            odd = x[128:192] + jnp.where((lane3 & 63) == 63, 0.0, pltpu.roll(x[0:64], 127, 1))
            first_height = jnp.where(lane3 < 64, even, pltpu.roll(odd, 64, 1))
            made.append((first_height, jnp.where(lane3 < 64, pltpu.roll(even, 64, 1), odd)))
        return made

    s.W3T[...] = s.W3[...].reshape(128, 1792).T
    b2 = s.B2
    one1, one2, two1, two2 = third_back([(1, 1, delta3), (1, 2, delta3), (2, 1, delta3), (2, 2, delta3)])
    for i, tap1, tap2 in ((0, one1, one2), (1, two1, two2)):
        b2[i, 0:64, :] = tap1[0]
        b2[i, 64:128, :] = tap2[0]
        b2[i, 128:192, :] = tap1[1]
        b2[i, 192:256, :] = tap2[1]
    g3 = dot_nt(delta3, t3)
    s.G3F[:, :, 1728:1792] = jnp.zeros((nh, pb, 64), F32)
    s.G3S[:, :, 1728:1792] = jnp.zeros((nh, pb, 64), BF)
    s.G3F[:, :, 0:1728] = g3.reshape(nh, pb, 1728)
    s.G3S[:, :, 0:1728] = g3.astype(BF).reshape(nh, pb, 1728)
    if nc == 2:
        g3c = to_partner("g3c", s.G3S.at[:, :, other], s.R3C)

    for c in range(nc):

        @pl.when(core == c)
        def _():
            total = s.G3F[:, :, c * half : c * half + half]
            if nc == 2:
                g3c.wait_recv()
                total = total + s.R3C[...].astype(F32)
            s.G3T[...] = total
            s.G3U[...] = total.astype(BF)

    made_g3h = spread("h", "g3h", lambda d, h: s.G3U.at[h], lambda k: s.R3H.at[k])

    dl2 = s.DL2
    receive(*halos_3[1], back)
    for halo_s in halos_s:
        receive(*halo_s, back)
    next_h = jnp.concatenate([s.D3H[:, 0:64], s.D3H[:, 64:128]], 0)
    own = jnp.concatenate([delta3[:, 64:128], next_h], 1)
    one0, two0, side1, side2 = third_back([(1, 0, own), (2, 0, own), (1, 1, own), (2, 1, own)])
    b2[0, 64:128, :] += one0[0]
    b2[0, 192:256, :] += one0[1]
    b2[0, 256:320, :] = side1[1]
    b2[1, 64:128, :] += two0[0]
    b2[1, 192:256, :] += two0[1]
    b2[1, 256:320, :] = side2[1]
    dl2[0, 0:256, :] = (b2[0, 0:256, :] * s2[0]).astype(BF)
    dl2[0, 256:320, :] = (b2[0, 256:320, :] * s.SH[0].astype(F32)).astype(BF)

    none = jnp.zeros((64, 256), BF)

    def second_grad(i, j):
        x = jnp.concatenate([dl2[i, 64 * (j + t) : 64 * (j + t) + 64, :] for t in (0, 1)], 1)
        t2 = jnp.concatenate(
            [s.T2[2 * i : 2 * i + 3, 192 * (j + t) : 192 * (j + t) + 288, :].reshape(864, 128) for t in (0, 1)], 1
        )
        low = dot_nt(t2[0:512], jnp.concatenate([x, none], 0))
        high = dot_nt(t2[512:864], jnp.concatenate([none, x], 0))
        return jnp.concatenate([low[0:352] + high, low[352:512]], 0).reshape(nc, nh, plan.r2, 128)

    lane = lax.broadcasted_iota(jnp.int32, (32, 128), 1)

    def second_back(plane, pairs):
        for j in range(5):
            y = None
            for a, i in pairs:
                term = dot(w2[a * 288 : a * 288 + 288, :], dl2[i, j * 64 : j * 64 + 64, :])
                y = term if y is None else y + term
            s.Y[j] = y
        for k in range(8):
            j = (k + 1) // 2
            d = s.Y[j, 0:96, :] + s.Y[j - 1, 192:288, :] if k % 2 else s.Y[j, 96:192, :]
            moved = jnp.where(lane < 64, pltpu.roll(d[0:32], 64, 1), pltpu.roll(d[0:32], 63, 1))
            moved = jnp.where(lane == 127, 0.0, moved)
            s.B1[plane, 32 * k : 32 * k + 32, 0:128] = d[32:64]
            s.B1[plane, 32 * k : 32 * k + 32, 128:256] = d[64:96] + moved

    s.G2F[...] = second_grad(0, 0) + second_grad(0, 2)
    second_back(0, [(1, 0)])
    receive(*halos_3[0], back)
    deep = s.D3D[...]
    zero0, zero1, zero2 = third_back([(0, 0, deep), (0, 1, deep), (0, 2, deep)])
    b2[1, 0:64, :] += zero1[0]
    b2[1, 64:128, :] += zero0[1] + zero2[0]
    b2[1, 128:192, :] += zero1[1]
    dl2[1, 0:192, :] = (b2[1, 0:192, :] * s2[1, 0:192, :]).astype(BF)
    s.G2F[...] += second_grad(1, 0)
    receive(*halos_3[2], back)
    next_c = jnp.concatenate([s.D3C[:, 0:64], s.D3C[:, 64:128]], 0)
    deep_next = jnp.concatenate([deep[:, 64:128], next_c], 1)
    corner0, side0 = third_back([(0, 0, deep_next), (0, 1, deep_next)])
    b2[1, 192:256, :] += corner0[1] + zero2[1]
    b2[1, 256:320, :] += side0[1]
    dl2[1, 192:256, :] = (b2[1, 192:256, :] * s2[1, 192:256, :]).astype(BF)
    g2 = s.G2F[...] + second_grad(1, 2)
    s.G2F[...] = g2
    s.G2S[...] = g2.astype(BF)
    made_g2h = spread("a", "g2h", lambda d, h: s.G2S.at[d & (nc - 1), h], lambda k: s.R2H.at[k])
    deep0, deep1, deep2, side3 = third_back(
        [(1, 0, deep_next), (1, 1, deep), (1, 2, deep), (1, 1, deep_next)]
    )
    b2[2, 0:64, :] = deep1[0]
    b2[2, 64:128, :] = deep0[0] + deep2[0]
    b2[2, 128:192, :] = deep1[1]
    b2[2, 192:256, :] = deep0[1] + deep2[1]
    b2[2, 256:320, :] = side3[1]
    dl2[2, 0:256, :] = (b2[2, 0:256, :] * s.SD[...].astype(F32)).astype(BF)
    dl2[1, 256:320, :] = (b2[1, 256:320, :] * s.SH[1].astype(F32)).astype(BF)
    dl2[2, 256:320, :] = (b2[2, 256:320, :] * s.SC[...].astype(F32)).astype(BF)

    second_back(1, [(2, 0), (0, 1)])
    second_back(2, [(1, 1)])
    second_back(3, [(2, 1), (0, 2)])

    made_out = spread("h", "out", lambda d, h: s.OS.at[h], lambda k: s.OR.at[ha])
    s.OR[ha] = s.OS[ha]
    s.G1A[...] = jnp.zeros((256, 576), F32)

    def loop_back(i, carry):
        d = (s.B1[i] * s.S1[i]).astype(BF)
        s.DL1[i] = d
        s.G1A[...] += dot_nt(d, s.T1[pl.ds(2 * i, 3)].reshape(576, 256))
        return carry

    lax.fori_loop(0, 4, loop_back, 0)
    def sum_parts(total, received, size):
        for k in range(1, size):
            total = total + received[k].astype(F32)
        return total

    gh = dot_nt(s.DL1[:, 0:32, :].reshape(128, 256), s.TH[...])
    sum_a = jnp.zeros((32, 576), F32)
    sum_b = jnp.zeros((32, 576), F32)
    for j in range(8):
        mask_a, mask_b = tap_masks(j)
        g = s.G1A[32 * j : 32 * j + 32, :]
        sum_a = sum_a + jnp.where(mask_a, g, 0.0)
        sum_b = sum_b + jnp.where(mask_b, g, 0.0)
    g1 = dot_nt(split_rows(sum_a), s.i_expand[:, 0:576])
    g1 = g1 + dot_nt(split_rows(sum_b), s.i_expand[:, 576:1152])
    for i in range(4):
        g1 = g1 + dot_nt(split_rows(gh[32 * i : 32 * i + 32]), s.i_halo[:, i * 256 : i * 256 + 192])
    g1 = g1[0:32] + g1[32:64]
    s.G1S[...] = g1.astype(BF)
    made_g1h = spread("a", "g1h", lambda d, h: s.G1S, lambda k: s.R1H.at[k])

    gather(made_g3h)
    total = sum_parts(s.G3T[ha], s.R3H, nh)
    s.P3F[...] = total
    s.P3S[...] = total.astype(BF)
    made_g3d = spread("z", "g3d", lambda d, h: s.P3S, lambda k: s.R3D.at[k])
    gather(made_g2h)
    g2 = sum_parts(s.G2F[core, ha], s.R2H, nh * nc)
    s.G2D[...] = g2.astype(BF)
    made_g2d = spread("z", "g2d", lambda d, h: s.G2D, lambda k: s.R2D.at[k])
    gather(made_out)
    x = s.OR[...].reshape(128, 128)
    x = jnp.concatenate([x[:, 0:64], x[:, 64:128]], 0)
    o3[...] = dot_tn(s.i_rows[...], x).astype(BF).reshape(pb, 2 * nh, 64)
    gather(made_g1h)
    g1 = sum_parts(g1, s.R1H, nh * nc)
    s.G1D[...] = g1.astype(BF)
    made_g1d = spread("z", "g1d", lambda d, h: s.G1D, lambda k: s.R1D.at[k])
    gather(made_g2d)
    g2 = sum_parts(g2, s.R2D, nz)
    s.F2[...] = g2.astype(BF)
    s.F2H[core, ha] = g2.astype(BF)
    settled = len(pending)
    made_g2z = spread("a", "g2z", lambda d, h: s.F2, lambda k: s.F2H.at[core, ha])
    gather(made_g3d)
    s.F3[core] = sum_parts(s.P3F[...], s.R3D, nz)
    if nc == 2:
        to_partner("g3p", s.F3.at[core], s.F3.at[core])
        g3p = copy(s.F3.at[1 - core], s.F3.at[1 - core], plan.sem["g3p"], (dev + 1 - 2 * core, ha))
    gather(made_g1d)
    x = (sum_parts(g1, s.R1D, nz) * scales[0]).T
    for t in range(27):
        g1o[t] = x[4 * t : 4 * t + 4]
    if nc == 2:
        g3p.wait_recv()
    for t in range(27):
        c, r = divmod(64 * t, half)
        g3o[t] = s.F3[c, :, r : r + 64] * scales[2]
    finish_sends(pending[:settled])
    gather(made_g2z)
    x = s.F2H[...].reshape(512, 128).astype(F32) * scales[1]
    g2o[0:512, :] = x[:, 0:64]
    g2o[512:864, :] = x[0:352, 64:128]
    finish_sends(pending[settled:])


def finish(*refs):
    copies = [pltpu.make_async_copy(refs[k], refs[4 + k], refs[8].at[k]) for k in range(4)]
    for c in copies:
        c.start()
    for c in copies:
        c.wait()


def local(nd, nh, volume, w_first, w_second, w_third, cotangent):
    plan = Plan(nd, nh)
    pb = plan.pb
    cells = volume.shape[1] * nd * volume.shape[2] * nh * volume.shape[3]
    scales = tuple(1.0 / math.sqrt(cells // 8**n) for n in (1, 2, 3))
    inputs = dict(
        vol=volume,
        w1=w_first.reshape(27, 4, 32),
        w2=w_second.reshape(864, 64),
        w3=jnp.transpose(w_third.reshape(27, 64, pb), (0, 2, 1)),
        cot=cotangent.reshape(pb, 2 * nh, 64),
    )
    inputs.update(zip(INPUTS[5:], constants(nh)))
    scratch = plan.scratch()
    for name in INPUTS:
        scratch["i_" + name] = pltpu.VMEM(inputs[name].shape, BF)
    names = list(scratch)
    vmem, hbm = pl.BlockSpec(memory_space=pltpu.VMEM), pl.BlockSpec(memory_space=pltpu.HBM)
    shapes = [((pb, 2 * nh, 64), BF), ((27, 4, 32), F32), ((864, 64), F32), ((27, pb, 64), F32)]
    made = pl.pallas_call(
        functools.partial(kernel, plan, names, scales),
        out_shape=[pltpu.VMEM(*x) for x in shapes],
        in_specs=[hbm] * len(INPUTS),
        out_specs=[vmem] * 4,
        scratch_shapes=[scratch[n] for n in names],
        compiler_params=pltpu.CompilerParams(
            collective_id=0 if nd * nh > 1 else None, has_side_effects=True, vmem_limit_bytes=48 * 2**20
        ),
        name="step",
    )(*[pltpu.with_memory_space_constraint(inputs[n], pltpu.HBM) for n in INPUTS])
    out3, g1, g2, g3 = pl.pallas_call(
        finish,
        out_shape=[jax.ShapeDtypeStruct(*x) for x in shapes],
        in_specs=[vmem] * 4,
        out_specs=[hbm] * 4,
        scratch_shapes=[pltpu.SemaphoreType.DMA((4,))],
        compiler_params=pltpu.CompilerParams(vmem_limit_bytes=48 * 2**20),
        name="finish",
    )(*made)
    return (
        out3.reshape(pb, 1, 2 * nh, 64),
        g1.reshape(3, 3, 3, 4, 32),
        g2.reshape(3, 3, 3, 32, 64),
        jnp.transpose(g3, (0, 2, 1)).reshape(3, 3, 3, 64, pb),
    )


def solution(mesh):
    placed = (
        P(None, "dev", "ha", None),
        P(),
        P(),
        P(None, None, None, None, "ha"),
        P("ha", "dev", None, None),
    )
    return jax.shard_map(
        functools.partial(local, mesh.shape["dev"], mesh.shape["ha"]),
        mesh=mesh,
        in_specs=placed,
        out_specs=(P("ha", "dev", None, None), P(), P(), P(None, None, None, None, "ha")),
        check_vma=False,
    )
```
